128 devices in a mesh: ctx: 8 (over z, y_hi), tp: 16 (over y_lo, x, core).
Axes of the slice: x: 4, y: 4 (y_hi: 2, y_lo: 2; y = y_hi * 2 + y_lo), z: 4, core: 2. Of those that a mesh axis runs over, the one named last changes fastest.
Arguments:
- byte_embeds: bfloat16 [24576, 1024], P(('ctx', 'tp')), may hold values from -6 to 6
- local_embeds: bfloat16 [24576, 1024], P(('ctx', 'tp')), may hold values from -6 to 6
- global_qkv: bfloat16 [3, 8192, 4096], P(None, None, 'tp'), may hold values from -0.0625 to 0.0625
- global_out: bfloat16 [4096, 8192], P('tp'), may hold values from -1.5 to 1.5
- local_qkv: bfloat16 [1, 1024, 3072], replicated, may hold values from -0.1875 to 0.1875
- local_out: bfloat16 [1, 1024, 1024], replicated, may hold values from -0.1875 to 0.1875
- cotangent: bfloat16 [24576, 1024], P(('ctx', 'tp')), may hold values from -6 to 6
Outputs:
- hidden: bfloat16 [24576, 1024], P(('ctx', 'tp'))
- grad_qkv: float32 [1, 1024, 3072], P(None, ('ctx', 'tp'))
- grad_out: float32 [1, 1024, 1024], P(None, ('ctx', 'tp'))
The draws below stay inside these ranges and needn't reach their ends.
All inputs are finite; a program needn't handle non-finite values.
Results may differ from the reference program's by a relative error of at most 0.028.
Values may be sent and summed in bfloat16 or wider, within the bound.
A program may use at most 128 MiB of HBM per device.

```python
import math
import jax
import jax.numpy as jnp
from jax import lax

PATCH = 8
LOCAL_WIDTH = 1024
HEADS = 32
HEAD_DIM = 128
LOCAL_HEADS = 8
LOCAL_HEAD_DIM = 128
LAYERS = 1
GLOBAL_WIDTH = 8192
ATTN_WIDTH = 4096
BYTES = 24576


def block_levels(stream_key, shape, cuts, low, top_value):
    def one(axis_at, shards_of):
        steps = jax.random.uniform(jax.random.fold_in(jax.random.fold_in(stream_key, 6), axis_at), (shards_of,), jnp.float32, low / len(cuts), top_value / len(cuts))
        return jnp.repeat(jnp.exp(steps), shape[axis_at] // shards_of).reshape((-1,) + (1,) * (len(shape) - axis_at - 1))

    gain = one(*cuts[0])
    for cut in cuts[1:]:
        gain = gain * one(*cut)
    return gain


def gaussian(stream_key, extent, scale, reach, shards=(), dtype=jnp.bfloat16):
    drawn = jax.random.normal(stream_key, extent, jnp.float32) * scale
    if len(shards) > 0:
        drawn = block_levels(stream_key, extent, shards, -0.22, 0.18) * drawn
    return jnp.clip(drawn, min=-reach, max=reach).astype(dtype)


def setup_inputs(seed: int = 0) -> dict:
    splits = jax.random.split(jax.random.key(seed), 8)
    return {
        "byte_embeds": gaussian(splits[0], (BYTES, LOCAL_WIDTH), 1.0, 6.0, ((0, 128),)),
        "local_embeds": gaussian(splits[1], (BYTES, LOCAL_WIDTH), 1.0, 6.0, ((0, 128),)),
        "global_qkv": gaussian(splits[2], (3, GLOBAL_WIDTH, ATTN_WIDTH), GLOBAL_WIDTH ** -0.5, 0.0625, ((2, 16),)),
        "global_out": gaussian(splits[3], (ATTN_WIDTH, GLOBAL_WIDTH), 0.25, 1.5, ((0, 16),)),
        "local_qkv": gaussian(splits[4], (LAYERS, LOCAL_WIDTH, 3 * LOCAL_WIDTH), LOCAL_WIDTH ** -0.5, 0.1875),
        "local_out": gaussian(splits[5], (LAYERS, LOCAL_WIDTH, LOCAL_WIDTH), LOCAL_WIDTH ** -0.5, 0.1875),
        "cotangent": gaussian(splits[6], (BYTES, LOCAL_WIDTH), 1.0, 6.0, ((0, 128),)),
    }


def rms_norm(values):
    return values * lax.rsqrt(lax.optimization_barrier(jnp.mean(values * values, axis=-1, keepdims=True)) + 1e-06)

def local_core(qkv_rows):
    total = qkv_rows.shape[0]
    groups = total // PATCH
    width = qkv_rows.shape[1] // 3
    parts = qkv_rows.reshape(groups, PATCH, 3, LOCAL_HEADS, LOCAL_HEAD_DIM)
    queries = rms_norm(parts[:, :, 0])
    keys_all = rms_norm(parts[:, :, 1])
    values = parts[:, :, 2]
    scores = jnp.einsum('npha,nqha->nhpq', queries, keys_all) / math.sqrt(LOCAL_HEAD_DIM)
    causal = jnp.arange(PATCH)[:, None] >= jnp.arange(PATCH)[None, :]
    weights = jnp.where(causal[None, None], jnp.exp(scores), 0.0)
    numerator = jnp.einsum('nhpq,nqha->npha', weights, values)
    denominator = lax.optimization_barrier(jnp.sum(weights, axis=-1)).transpose(0, 2, 1)[..., None]
    return (numerator / denominator).reshape(total, width)

def local_pass(state, local_qkv, local_out, cotangent):
    saved = []
    for layer in range(LAYERS):
        normed = rms_norm(state).astype(jnp.bfloat16)
        qkv_rows = jnp.dot(normed, local_qkv[layer], preferred_element_type=jnp.float32)
        core, core_back = jax.vjp(local_core, qkv_rows)
        attended = core.astype(jnp.bfloat16)
        saved.append((state, normed, core_back, attended))
        state = state + jnp.dot(attended, local_out[layer], preferred_element_type=jnp.float32)
    hidden = state.astype(jnp.bfloat16)
    grad_state = cotangent.astype(jnp.float32)
    grads_qkv = []
    grads_out = []
    for layer in range(LAYERS - 1, -1, -1):
        before, normed, core_back, attended = saved[layer]
        grad_round = grad_state.astype(jnp.bfloat16)
        grads_out.append(jnp.dot(attended.T, grad_round, preferred_element_type=jnp.float32))
        grad_core = jnp.dot(grad_round, local_out[layer].T, preferred_element_type=jnp.float32)
        grad_rows = core_back(grad_core)[0].astype(jnp.bfloat16)
        grads_qkv.append(jnp.dot(normed.T, grad_rows, preferred_element_type=jnp.float32))
        if layer > 0:
            grad_normed = jnp.dot(grad_rows, local_qkv[layer].T, preferred_element_type=jnp.float32)
            norm_back = jax.vjp(rms_norm, before)[1]
            grad_state = grad_state + norm_back(grad_normed)[0]
    return (hidden, jnp.stack(grads_qkv[::-1]), jnp.stack(grads_out[::-1]))

def reference(byte_embeds, local_embeds, global_qkv, global_out, local_qkv, local_out, cotangent):
    patch_count = byte_embeds.shape[0] // PATCH
    patch_in = byte_embeds.reshape(patch_count, PATCH * LOCAL_WIDTH).astype(jnp.float32)
    normed = rms_norm(patch_in).astype(jnp.bfloat16)
    query_proj = jnp.dot(normed, global_qkv[0], preferred_element_type=jnp.float32)
    key_proj = jnp.dot(normed, global_qkv[1], preferred_element_type=jnp.float32)
    value_proj = jnp.dot(normed, global_qkv[2], preferred_element_type=jnp.float32)
    queries = rms_norm(query_proj.reshape(patch_count, HEADS, HEAD_DIM)).astype(jnp.bfloat16)
    keys_all = rms_norm(key_proj.reshape(patch_count, HEADS, HEAD_DIM)).astype(jnp.bfloat16)
    values = value_proj.reshape(patch_count, HEADS, HEAD_DIM).astype(jnp.bfloat16)
    causal = jnp.arange(patch_count)[:, None] >= jnp.arange(patch_count)[None, :]

    def one_head(operands):
        head_q, head_k, head_v = operands
        scores = jnp.dot(head_q, head_k.T, preferred_element_type=jnp.float32) / math.sqrt(HEAD_DIM)
        expo = jnp.where(causal, jnp.exp(scores), 0.0)
        numerator = jnp.dot(expo.astype(jnp.bfloat16), head_v, preferred_element_type=jnp.float32)
        denominator = lax.optimization_barrier(jnp.sum(expo, axis=1))
        return numerator / denominator[:, None]
    per_head = lax.map(one_head, (queries.transpose(1, 0, 2), keys_all.transpose(1, 0, 2), values.transpose(1, 0, 2)))
    attended = per_head.transpose(1, 0, 2).reshape(patch_count, HEADS * HEAD_DIM).astype(jnp.bfloat16)
    patch_out = jnp.dot(attended, global_out, preferred_element_type=jnp.float32).astype(jnp.bfloat16)
    shifted = jnp.concatenate([jnp.zeros((1, patch_out.shape[1]), jnp.bfloat16), patch_out[:-1]], axis=0)
    context = shifted.reshape(byte_embeds.shape[0], LOCAL_WIDTH)
    state = local_embeds.astype(jnp.float32) + context.astype(jnp.float32)
    return local_pass(state, local_qkv, local_out, cotangent)
```

```python
import math

import jax
import jax.numpy as jnp
from jax import lax
from jax.sharding import PartitionSpec as P

PATCH = 8
HEAD_DIM = 128
LOCAL_HEADS = 8
LOCAL_HEAD_DIM = 128


def from_behind(value, axis, steps):
    count = lax.axis_size(axis)
    initial, last = (max(0, -steps), min(count, count - steps))
    return lax.ppermute(value, axis, [(source, source + steps) for source in range(initial, last)])


def rms_norm(values):
    return values * lax.rsqrt(jnp.mean(values * values, axis=-1, keepdims=True) + 1e-06)


def local_core(qkv_rows):
    total = qkv_rows.shape[0]
    groups = total // PATCH
    width = qkv_rows.shape[1] // 3
    parts = qkv_rows.reshape(groups, PATCH, 3, LOCAL_HEADS, LOCAL_HEAD_DIM)
    queries = rms_norm(parts[:, :, 0])
    keys_all = rms_norm(parts[:, :, 1])
    values = parts[:, :, 2]
    scores = jnp.einsum("npha,nqha->nhpq", queries, keys_all) / math.sqrt(LOCAL_HEAD_DIM)
    causal = jnp.arange(PATCH)[:, None] >= jnp.arange(PATCH)[None, :]
    weights = jnp.where(causal[None, None], jnp.exp(scores), 0.0)
    numerator = jnp.einsum("nhpq,nqha->npha", weights, values)
    denominator = jnp.sum(weights, axis=-1).transpose(0, 2, 1)[..., None]
    return (numerator / denominator).reshape(total, width)


def local_pass(state, local_qkv, local_out, cotangent):
    layer = 0
    normed = rms_norm(state).astype(jnp.bfloat16)
    qkv_rows = jnp.dot(normed, local_qkv[layer], preferred_element_type=jnp.float32)
    core, core_back = jax.vjp(local_core, qkv_rows)
    attended = core.astype(jnp.bfloat16)
    saved = [(state, normed, core_back, attended)]
    state = state + jnp.dot(attended, local_out[layer], preferred_element_type=jnp.float32)
    hidden = state.astype(jnp.bfloat16)
    grad_state = cotangent.astype(jnp.float32)
    layer = 0
    before, normed, core_back, attended = saved[layer]
    grad_round = grad_state.astype(jnp.bfloat16)
    grads_out = [jnp.dot(attended.T, grad_round, preferred_element_type=jnp.float32)]
    grad_core = jnp.dot(grad_round, local_out[layer].T, preferred_element_type=jnp.float32)
    grad_rows = core_back(grad_core)[0].astype(jnp.bfloat16)
    grads_qkv = [jnp.dot(normed.T, grad_rows, preferred_element_type=jnp.float32)]
    return (hidden, jnp.stack(grads_qkv[::-1]), jnp.stack(grads_out[::-1]))


def per_device(byte_embeds, local_embeds, global_qkv, global_out, local_qkv, local_out, cotangent):
    byte_count = byte_embeds.shape[0]
    patch_count = byte_count // PATCH
    full_width = PATCH * byte_embeds.shape[1]
    patch_in = byte_embeds.reshape(patch_count, full_width).astype(jnp.float32)
    normed = rms_norm(patch_in).astype(jnp.bfloat16)
    projected = jnp.einsum(
        "nd,cdh->nch",
        lax.all_gather(normed, "tp", axis=0, tiled=True),
        global_qkv,
        preferred_element_type=jnp.float32,
    )
    shard_rows = projected.shape[0]
    head_width = global_qkv.shape[2]
    head_count = head_width // HEAD_DIM
    queries = rms_norm(projected[:, 0].reshape(shard_rows, head_count, HEAD_DIM)).astype(
        jnp.bfloat16
    )
    keys_mine = rms_norm(projected[:, 1].reshape(shard_rows, head_count, HEAD_DIM)).astype(
        jnp.bfloat16
    )
    values_mine = projected[:, 2].reshape(shard_rows, head_count, HEAD_DIM).astype(jnp.bfloat16)
    query_pos = lax.axis_index("ctx") * shard_rows + jnp.arange(shard_rows, dtype=jnp.int32)
    pieces = lax.all_gather(
        jnp.concatenate([keys_mine, values_mine], axis=1), "ctx", axis=0, tiled=True
    )
    key_piece, value_piece = pieces[:, :head_count], pieces[:, head_count:]
    key_count = key_piece.shape[0]
    scores = jnp.einsum(
        "rha,kha->rhk", queries, key_piece, preferred_element_type=jnp.float32
    ) / math.sqrt(HEAD_DIM)
    key_pos = jnp.arange(key_count, dtype=jnp.int32)
    allowed = key_pos[None, None, :] <= query_pos[:, None, None]
    expo = jnp.where(allowed, jnp.exp(scores), 0.0)
    numerator = jnp.einsum(
        "rhk,kha->rha", expo.astype(jnp.bfloat16), value_piece, preferred_element_type=jnp.float32
    )
    denominator = jnp.sum(expo, axis=-1)
    numerator, denominator = (numerator, denominator)
    attended = (
        (numerator / denominator[..., None]).reshape(shard_rows, head_width).astype(jnp.bfloat16)
    )
    patch_out = lax.psum_scatter(
        jnp.dot(attended, global_out, preferred_element_type=jnp.float32).astype(jnp.bfloat16),
        "tp",
        scatter_dimension=0,
        tiled=True,
    )
    earlier_row = from_behind(patch_out[-1:], ("ctx", "tp"), 1)
    patch_out = jnp.concatenate([earlier_row, patch_out[:-1]], axis=0)
    context = patch_out.reshape(byte_count, byte_embeds.shape[1])
    state = local_embeds.astype(jnp.float32) + context.astype(jnp.float32)
    hidden, grad_qkv, grad_out = local_pass(state, local_qkv, local_out, cotangent)
    width = grad_qkv.shape[2]
    grads = jnp.concatenate([grad_qkv[0], grad_out[0]], axis=1)
    ctx_count, tp_count = lax.axis_size("ctx"), lax.axis_size("tp")
    grads = grads.reshape(ctx_count, tp_count, -1, grads.shape[1]).transpose(1, 0, 2, 3)
    grads = grads.reshape(-1, grads.shape[3]).astype(jnp.bfloat16)
    grads = lax.psum_scatter(grads, "tp", scatter_dimension=0, tiled=True)
    grads = lax.psum_scatter(
        grads.astype(jnp.float32), "ctx", scatter_dimension=0, tiled=True
    )
    grads = grads.reshape(1, -1, grads.shape[1])
    grad_qkv, grad_out = grads[:, :, :width], grads[:, :, width:]
    return (hidden, grad_qkv, grad_out)


def solution(mesh):
    in_specs = (
        P(("ctx", "tp"), None),
        P(("ctx", "tp"), None),
        P(None, None, "tp"),
        P("tp", None),
        P(),
        P(),
        P(("ctx", "tp"), None),
    )
    out_specs = (P(("ctx", "tp"), None), P(None, ("ctx", "tp"), None), P(None, ("ctx", "tp"), None))
    return jax.shard_map(
        per_device, mesh=mesh, in_specs=in_specs, out_specs=out_specs, check_vma=False
    )
```

```python
import math

import jax
import jax.numpy as jnp
from jax import lax
from jax.experimental import pallas as pl
from jax.experimental.pallas import tpu as pltpu
from jax.sharding import PartitionSpec as P

PATCH = 8
HEAD_DIM = 128
LOCAL_HEADS = 8
LOCAL_HEAD_DIM = 128


def from_behind(value, axis, steps):
    count = lax.axis_size(axis)
    initial, last = (max(0, -steps), min(count, count - steps))
    return lax.ppermute(value, axis, [(source, source + steps) for source in range(initial, last)])


MESH = pl.DeviceIdType.MESH


def coords():
    ctx, tp = lax.axis_index("ctx"), lax.axis_index("tp")
    x, core = lax.rem(lax.div(tp, 2), 4), lax.rem(tp, 2)
    y = lax.rem(ctx, 2) * 2 + lax.div(tp, 8)
    return x, y, lax.div(ctx, 2), core


def device_at(x, y, z, core):
    return {"ctx": z * 2 + lax.div(y, 2), "tp": lax.rem(y, 2) * 8 + x * 2 + core}


def greet(peers):
    barrier = pltpu.get_barrier_semaphore()
    for peer in peers:
        pl.semaphore_signal(barrier, inc=1, device_id=peer, device_id_type=MESH)
    pl.semaphore_wait(barrier, len(peers))


def remote(source, target, send_sem, recv_sem, peer):
    return pltpu.make_async_remote_copy(
        src_ref=source,
        dst_ref=target,
        send_sem=send_sem,
        recv_sem=recv_sem,
        device_id=peer,
        device_id_type=MESH,
    )


PART_COLS = (640, 640, 768)
PART_ORDERS = ((0, 1, 2), (1, 2, 0), (2, 0, 1))


def grads_kernel(
    xn_ref, gq_ref, ab_ref, gb_ref, out_q, out_o,
    xn2, gq2, ab2, gb2,
    part0, part1, part2, relay0, relay1, relay2, near0, near1, near2,
    sum0, sum1, sum2, got0, got1, got2, low0, low1, low2, last0, last1, last2,
    fin, other, pair_send, pair_recv, send1, recv1, send2, recv2, send3, recv3,
    fin_send, fin_recv,
):
    place = coords()
    core = place[3]

    def peer_along(axis, step):
        at = list(place)
        at[axis] = lax.rem(at[axis] + step, 4)
        return device_at(*at)

    partner = device_at(place[0], place[1], place[2], 1 - core)
    greet([partner] + [peer_along(axis, step) for axis in range(3) for step in (1, 2, 3)])

    rows = xn_ref.shape[0]
    qh, oh = gq2.shape[1], gb2.shape[1]
    mine_q, mine_o = pl.multiple_of(core * qh, qh), pl.multiple_of(core * oh, oh)
    its_q, its_o = pl.multiple_of((1 - core) * qh, qh), pl.multiple_of((1 - core) * oh, oh)
    bottom = pl.ds(rows, rows)
    swaps = [
        remote(xn_ref, xn2.at[bottom], pair_send.at[0], pair_recv.at[0], partner),
        remote(gq_ref.at[:, pl.ds(its_q, qh)], gq2.at[bottom], pair_send.at[1], pair_recv.at[1], partner),
        remote(ab_ref, ab2.at[bottom], pair_send.at[2], pair_recv.at[2], partner),
        remote(gb_ref.at[:, pl.ds(its_o, oh)], gb2.at[bottom], pair_send.at[3], pair_recv.at[3], partner),
    ]
    for swap in swaps:
        swap.start()
    top = pl.ds(0, rows)
    xn2[top] = xn_ref[...]
    gq2[top] = gq_ref[:, pl.ds(mine_q, qh)]
    ab2[top] = ab_ref[...]
    gb2[top] = gb_ref[:, pl.ds(mine_o, oh)]

    parts = (part0, part1, part2)
    relays, nears = (relay0, relay1, relay2), (near0, near1, near2)
    sums, gots = (sum0, sum1, sum2), (got0, got1, got2)
    lows, lasts = (low0, low1, low2), (last0, last1, last2)

    def fill(part, order, left, right, columns, into):
        width = columns[1] - columns[0]
        for z in range(4):
            block = lax.dot_general(
                left[:, z * 256 : (z + 1) * 256],
                right[:, columns[0] : columns[1]],
                (((0,), (0,)), ((), ())),
                preferred_element_type=jnp.float32,
            ).astype(jnp.bfloat16)
            for y in range(4):
                for x in range(4):
                    at = (x, y, z)
                    row = (y * 4 + x) * 16
                    part[at[order[0]], at[order[1]], at[order[2]], :, into : into + width] = block[
                        row : row + 16
                    ]

    first = []

    def stage1(k):
        order = PART_ORDERS[k]
        axis = order[0]
        me = place[axis]
        right, left, far = lax.rem(me + 1, 4), lax.rem(me + 3, 4), lax.rem(me + 2, 4)
        to_right, to_left = peer_along(axis, 1), peer_along(axis, 3)
        part, relay, near = parts[k], relays[k], nears[k]
        lo, hi = pl.ds(0, 2), pl.ds(2, 2)

        def copy(n, source, target, peer):
            return remote(source, target, send1.at[k, n], recv1.at[k, n], peer)

        copies = [
            copy(0, part.at[far, lo], relay.at[0], to_right),
            copy(1, part.at[far, hi], relay.at[1], to_left),
            copy(2, part.at[right, hi], near.at[0, hi], to_right),
            copy(3, part.at[left, lo], near.at[1, lo], to_left),
            copy(4, part.at[right, lo], near.at[0, lo], to_right),
            copy(5, part.at[left, hi], near.at[1, hi], to_left),
        ]
        for n in range(4):
            copies[n].start()
        return copies, (right, left)

    def add_relay(k, copies, sides):
        part, relay = parts[k], relays[k]
        for n in range(2):
            copies[n].wait_recv()
            for j in range(2):
                at = 2 * n + j
                part[sides[n], at] = (
                    part[sides[n], at].astype(jnp.float32) + relay[n, j].astype(jnp.float32)
                ).astype(jnp.bfloat16)
            copies[4 + n].start()

    def stage2(k, copies):
        order = PART_ORDERS[k]
        for n in range(2, 6):
            copies[n].wait_recv()
        me = place[order[0]]
        for j in range(4):
            sums[k][j] = (
                parts[k][me, j].astype(jnp.float32)
                + nears[k][0, j].astype(jnp.float32)
                + nears[k][1, j].astype(jnp.float32)
            ).astype(jnp.bfloat16)
        axis = order[1]
        at = place[axis]
        sends = []
        for d in range(1, 4):
            send = remote(
                sums[k].at[lax.rem(at + d, 4)], gots[k].at[d - 1],
                send2.at[k, d - 1], recv2.at[k, d - 1], peer_along(axis, d),
            )
            send.start()
            sends.append(send)
        return sends

    def stage3(k, copies):
        order = PART_ORDERS[k]
        for copy in copies:
            copy.wait_recv()
        me = place[order[1]]
        total = sums[k][me].astype(jnp.float32)
        for d in range(3):
            total = total + gots[k][d].astype(jnp.float32)
        lows[k][...] = total.astype(jnp.bfloat16)
        axis = order[2]
        at = place[axis]
        sends = []
        for d in range(1, 4):
            send = remote(
                lows[k].at[lax.rem(at + d, 4)], lasts[k].at[d - 1],
                send3.at[k, d - 1], recv3.at[k, d - 1], peer_along(axis, d),
            )
            send.start()
            sends.append(send)
        return sends

    def finish(k, copies):
        for copy in copies:
            copy.wait_recv()
        me = place[PART_ORDERS[k][2]]
        total = lows[k][me].astype(jnp.float32)
        for d in range(3):
            total = total + lasts[k][d].astype(jnp.float32)
        start = sum(PART_COLS[:k])
        fin[:, start : start + PART_COLS[k]] = total

    swaps[0].wait_recv()
    swaps[1].wait_recv()
    split = PART_COLS[0] + PART_COLS[1]
    fill(part0, PART_ORDERS[0], xn2, gq2, (0, PART_COLS[0]), 0)
    first.append(stage1(0))
    fill(part1, PART_ORDERS[1], xn2, gq2, (PART_COLS[0], split), 0)
    first.append(stage1(1))
    swaps[2].wait_recv()
    swaps[3].wait_recv()
    fill(part2, PART_ORDERS[2], xn2, gq2, (split, qh), 0)
    fill(part2, PART_ORDERS[2], ab2, gb2, (0, oh), qh - split)
    first.append(stage1(2))
    for k in range(3):
        add_relay(k, *first[k])
    second = [stage2(k, first[k][0]) for k in range(3)]
    third = [stage3(k, second[k]) for k in range(3)]
    for k in range(3):
        finish(k, third[k])

    keep, give = pl.multiple_of(core * 8, 8), pl.multiple_of((1 - core) * 8, 8)
    end = remote(fin.at[pl.ds(give, 8)], other, fin_send, fin_recv, partner)
    end.start()
    out_q[:, pl.ds(mine_q, qh)] = fin[pl.ds(keep, 8), 0:qh]
    out_o[:, pl.ds(mine_o, oh)] = fin[pl.ds(keep, 8), qh : qh + oh]
    end.wait_recv()
    out_q[:, pl.ds(its_q, qh)] = other[:, 0:qh]
    out_o[:, pl.ds(its_o, oh)] = other[:, qh : qh + oh]
    for copy in swaps + [c for f in first for c in f[0]] + [c for s in second + third for c in s] + [end]:
        copy.wait_send()


def reduce_grads(xn, gq, ab, gb):
    rows, width = xn.shape
    qw, ow = gq.shape[1], gb.shape[1]
    bf, f32 = jnp.bfloat16, jnp.float32
    vmem = pl.BlockSpec(memory_space=pltpu.VMEM)

    def each(*lead):
        return [pltpu.VMEM((*lead, 16, c), bf) for c in PART_COLS]

    return pl.pallas_call(
        grads_kernel,
        name="reduce_grads",
        out_shape=(jax.ShapeDtypeStruct((8, qw), f32), jax.ShapeDtypeStruct((8, ow), f32)),
        in_specs=[vmem] * 4,
        out_specs=(vmem, vmem),
        scratch_shapes=[
            pltpu.VMEM((2 * rows, width), bf),
            pltpu.VMEM((2 * rows, qw // 2), bf),
            pltpu.VMEM((2 * rows, width), bf),
            pltpu.VMEM((2 * rows, ow // 2), bf),
            *each(4, 4, 4), *each(2, 2, 4), *each(2, 4, 4),
            *each(4, 4), *each(3, 4), *each(4), *each(3),
            pltpu.VMEM((16, (qw + ow) // 2), f32),
            pltpu.VMEM((8, (qw + ow) // 2), f32),
            pltpu.SemaphoreType.DMA((4,)), pltpu.SemaphoreType.DMA((4,)),
            pltpu.SemaphoreType.DMA((3, 6)), pltpu.SemaphoreType.DMA((3, 6)),
            pltpu.SemaphoreType.DMA((3, 3)), pltpu.SemaphoreType.DMA((3, 3)),
            pltpu.SemaphoreType.DMA((3, 3)), pltpu.SemaphoreType.DMA((3, 3)),
            pltpu.SemaphoreType.DMA, pltpu.SemaphoreType.DMA,
        ],
        compiler_params=pltpu.CompilerParams(collective_id=5, has_side_effects=True, vmem_limit_bytes=48 << 20),
    )(xn, gq, ab, gb)


def rms_norm(values):
    return values * lax.rsqrt(jnp.mean(values * values, axis=-1, keepdims=True) + 1e-06)


def local_core(qkv_rows):
    total = qkv_rows.shape[0]
    groups = total // PATCH
    width = qkv_rows.shape[1] // 3
    parts = qkv_rows.reshape(groups, PATCH, 3, LOCAL_HEADS, LOCAL_HEAD_DIM)
    queries = rms_norm(parts[:, :, 0])
    keys_all = rms_norm(parts[:, :, 1])
    values = parts[:, :, 2]
    scores = jnp.einsum("npha,nqha->nhpq", queries, keys_all) / math.sqrt(LOCAL_HEAD_DIM)
    causal = jnp.arange(PATCH)[:, None] >= jnp.arange(PATCH)[None, :]
    weights = jnp.where(causal[None, None], jnp.exp(scores), 0.0)
    numerator = jnp.einsum("nhpq,nqha->npha", weights, values)
    denominator = jnp.sum(weights, axis=-1).transpose(0, 2, 1)[..., None]
    return (numerator / denominator).reshape(total, width)


def local_pass(state, local_qkv, local_out, cotangent):
    layer = 0
    normed = rms_norm(state).astype(jnp.bfloat16)
    qkv_rows = jnp.dot(normed, local_qkv[layer], preferred_element_type=jnp.float32)
    core, core_back = jax.vjp(local_core, qkv_rows)
    attended = core.astype(jnp.bfloat16)
    saved = [(state, normed, core_back, attended)]
    state = state + jnp.dot(attended, local_out[layer], preferred_element_type=jnp.float32)
    hidden = state.astype(jnp.bfloat16)
    grad_state = cotangent.astype(jnp.float32)
    layer = 0
    before, normed, core_back, attended = saved[layer]
    grad_round = grad_state.astype(jnp.bfloat16)
    grad_core = jnp.dot(grad_round, local_out[layer].T, preferred_element_type=jnp.float32)
    grad_rows = core_back(grad_core)[0].astype(jnp.bfloat16)
    return hidden, normed, grad_rows, attended, grad_round


def per_device(byte_embeds, local_embeds, global_qkv, global_out, local_qkv, local_out, cotangent):
    byte_count = byte_embeds.shape[0]
    patch_count = byte_count // PATCH
    full_width = PATCH * byte_embeds.shape[1]
    patch_in = byte_embeds.reshape(patch_count, full_width).astype(jnp.float32)
    normed = rms_norm(patch_in).astype(jnp.bfloat16)
    projected = jnp.einsum(
        "nd,cdh->nch",
        lax.all_gather(normed, "tp", axis=0, tiled=True),
        global_qkv,
        preferred_element_type=jnp.float32,
    )
    shard_rows = projected.shape[0]
    head_width = global_qkv.shape[2]
    head_count = head_width // HEAD_DIM
    queries = rms_norm(projected[:, 0].reshape(shard_rows, head_count, HEAD_DIM)).astype(
        jnp.bfloat16
    )
    keys_mine = rms_norm(projected[:, 1].reshape(shard_rows, head_count, HEAD_DIM)).astype(
        jnp.bfloat16
    )
    values_mine = projected[:, 2].reshape(shard_rows, head_count, HEAD_DIM).astype(jnp.bfloat16)
    query_pos = lax.axis_index("ctx") * shard_rows + jnp.arange(shard_rows, dtype=jnp.int32)
    pieces = lax.all_gather(
        jnp.concatenate([keys_mine, values_mine], axis=1), "ctx", axis=0, tiled=True
    )
    key_piece, value_piece = pieces[:, :head_count], pieces[:, head_count:]
    key_count = key_piece.shape[0]
    scores = jnp.einsum(
        "rha,kha->rhk", queries, key_piece, preferred_element_type=jnp.float32
    ) / math.sqrt(HEAD_DIM)
    key_pos = jnp.arange(key_count, dtype=jnp.int32)
    allowed = key_pos[None, None, :] <= query_pos[:, None, None]
    expo = jnp.where(allowed, jnp.exp(scores), 0.0)
    numerator = jnp.einsum(
        "rhk,kha->rha", expo.astype(jnp.bfloat16), value_piece, preferred_element_type=jnp.float32
    )
    denominator = jnp.sum(expo, axis=-1)
    numerator, denominator = (numerator, denominator)
    attended = (
        (numerator / denominator[..., None]).reshape(shard_rows, head_width).astype(jnp.bfloat16)
    )
    patch_out = lax.psum_scatter(
        jnp.dot(attended, global_out, preferred_element_type=jnp.float32).astype(jnp.bfloat16),
        "tp",
        scatter_dimension=0,
        tiled=True,
    )
    earlier_row = from_behind(patch_out[-1:], ("ctx", "tp"), 1)
    patch_out = jnp.concatenate([earlier_row, patch_out[:-1]], axis=0)
    context = patch_out.reshape(byte_count, byte_embeds.shape[1])
    state = local_embeds.astype(jnp.float32) + context.astype(jnp.float32)
    hidden, *factors = local_pass(state, local_qkv, local_out, cotangent)
    grad_qkv, grad_out = reduce_grads(*factors)
    return (hidden, grad_qkv[None], grad_out[None])


def solution(mesh):
    in_specs = (
        P(("ctx", "tp"), None),
        P(("ctx", "tp"), None),
        P(None, None, "tp"),
        P("tp", None),
        P(),
        P(),
        P(("ctx", "tp"), None),
    )
    out_specs = (P(("ctx", "tp"), None), P(None, ("ctx", "tp"), None), P(None, ("ctx", "tp"), None))
    return jax.shard_map(
        per_device, mesh=mesh, in_specs=in_specs, out_specs=out_specs, check_vma=False
    )
```

```python
import math

import jax
import jax.numpy as jnp
from jax import lax
from jax.experimental import pallas as pl
from jax.experimental.pallas import tpu as pltpu
from jax.sharding import PartitionSpec as P

PATCH = 8
HEAD_DIM = 128
LOCAL_HEADS = 8
LOCAL_HEAD_DIM = 128


def from_behind(value, axis, steps):
    count = lax.axis_size(axis)
    initial, last = (max(0, -steps), min(count, count - steps))
    return lax.ppermute(value, axis, [(source, source + steps) for source in range(initial, last)])


MESH = pl.DeviceIdType.MESH


def coords():
    ctx, tp = lax.axis_index("ctx"), lax.axis_index("tp")
    x, core = lax.rem(lax.div(tp, 2), 4), lax.rem(tp, 2)
    y = lax.rem(ctx, 2) * 2 + lax.div(tp, 8)
    return x, y, lax.div(ctx, 2), core


def device_at(x, y, z, core):
    return {"ctx": z * 2 + lax.div(y, 2), "tp": lax.rem(y, 2) * 8 + x * 2 + core}


def greet(peers):
    barrier = pltpu.get_barrier_semaphore()
    for peer in peers:
        pl.semaphore_signal(barrier, inc=1, device_id=peer, device_id_type=MESH)
    pl.semaphore_wait(barrier, len(peers))


def remote(source, target, send_sem, recv_sem, peer):
    return pltpu.make_async_remote_copy(
        src_ref=source,
        dst_ref=target,
        send_sem=send_sem,
        recv_sem=recv_sem,
        device_id=peer,
        device_id_type=MESH,
    )


PART_COLS = (640, 640, 768)
PART_ORDERS = ((0, 1, 2), (1, 2, 0), (2, 0, 1))


def grads_kernel(
    xn_ref, gq_ref, ab_ref, gb_ref, out_q, out_o,
    xn2, gq2, ab2, gb2,
    part0, part1, part2, relay0, relay1, relay2, near0, near1, near2,
    sum0, sum1, sum2, got0, got1, got2, low0, low1, low2, last0, last1, last2,
    fin, other, pair_send, pair_recv, send1, recv1, send2, recv2, send3, recv3,
    fin_send, fin_recv,
):
    place = coords()
    core = place[3]

    def peer_along(axis, step):
        at = list(place)
        at[axis] = lax.rem(at[axis] + step, 4)
        return device_at(*at)

    partner = device_at(place[0], place[1], place[2], 1 - core)
    greet([partner] + [peer_along(axis, step) for axis in range(3) for step in (1, 2, 3)])

    rows = xn_ref.shape[0]
    qh, oh = gq2.shape[1], gb2.shape[1]
    mine_q, mine_o = pl.multiple_of(core * qh, qh), pl.multiple_of(core * oh, oh)
    its_q, its_o = pl.multiple_of((1 - core) * qh, qh), pl.multiple_of((1 - core) * oh, oh)
    bottom = pl.ds(rows, rows)
    swaps = [
        remote(xn_ref, xn2.at[bottom], pair_send.at[0], pair_recv.at[0], partner),
        remote(gq_ref.at[:, pl.ds(its_q, qh)], gq2.at[bottom], pair_send.at[1], pair_recv.at[1], partner),
        remote(ab_ref, ab2.at[bottom], pair_send.at[2], pair_recv.at[2], partner),
        remote(gb_ref.at[:, pl.ds(its_o, oh)], gb2.at[bottom], pair_send.at[3], pair_recv.at[3], partner),
    ]
    for swap in swaps:
        swap.start()
    top = pl.ds(0, rows)
    xn2[top] = xn_ref[...]
    gq2[top] = gq_ref[:, pl.ds(mine_q, qh)]
    ab2[top] = ab_ref[...]
    gb2[top] = gb_ref[:, pl.ds(mine_o, oh)]

    parts = (part0, part1, part2)
    relays, nears = (relay0, relay1, relay2), (near0, near1, near2)
    sums, gots = (sum0, sum1, sum2), (got0, got1, got2)
    lows, lasts = (low0, low1, low2), (last0, last1, last2)

    def fill(part, order, left, right, columns, into):
        width = columns[1] - columns[0]
        for z in range(4):
            block = lax.dot_general(
                left[:, z * 256 : (z + 1) * 256],
                right[:, columns[0] : columns[1]],
                (((0,), (0,)), ((), ())),
                preferred_element_type=jnp.float32,
            ).astype(jnp.bfloat16)
            for y in range(4):
                for x in range(4):
                    at = (x, y, z)
                    row = (y * 4 + x) * 16
                    part[at[order[0]], at[order[1]], at[order[2]], :, into : into + width] = block[
                        row : row + 16
                    ]

    first = []

    def stage1(k):
        order = PART_ORDERS[k]
        axis = order[0]
        me = place[axis]
        right, left, far = lax.rem(me + 1, 4), lax.rem(me + 3, 4), lax.rem(me + 2, 4)
        to_right, to_left = peer_along(axis, 1), peer_along(axis, 3)
        part, relay, near = parts[k], relays[k], nears[k]
        lo, hi = pl.ds(0, 2), pl.ds(2, 2)

        def copy(n, source, target, peer):
            return remote(source, target, send1.at[k, n], recv1.at[k, n], peer)

        copies = [
            copy(0, part.at[far, lo], relay.at[0], to_right),
            copy(1, part.at[far, hi], relay.at[1], to_left),
            copy(2, part.at[right, hi], near.at[0, hi], to_right),
            copy(3, part.at[left, lo], near.at[1, lo], to_left),
            copy(4, part.at[right, lo], near.at[0, lo], to_right),
            copy(5, part.at[left, hi], near.at[1, hi], to_left),
        ]
        for n in range(4):
            copies[n].start()
        return copies, (right, left)

    def add_relay(k, copies, sides):
        part, relay = parts[k], relays[k]
        for n in range(2):
            copies[n].wait_recv()
            for j in range(2):
                at = 2 * n + j
                part[sides[n], at] = (
                    part[sides[n], at].astype(jnp.float32) + relay[n, j].astype(jnp.float32)
                ).astype(jnp.bfloat16)
            copies[4 + n].start()

    def stage2(k, copies):
        order = PART_ORDERS[k]
        for n in range(2, 6):
            copies[n].wait_recv()
        me = place[order[0]]
        for j in range(4):
            sums[k][j] = (
                parts[k][me, j].astype(jnp.float32)
                + nears[k][0, j].astype(jnp.float32)
                + nears[k][1, j].astype(jnp.float32)
            ).astype(jnp.bfloat16)
        axis = order[1]
        at = place[axis]
        sends = []
        for d in range(1, 4):
            send = remote(
                sums[k].at[lax.rem(at + d, 4)], gots[k].at[d - 1],
                send2.at[k, d - 1], recv2.at[k, d - 1], peer_along(axis, d),
            )
            send.start()
            sends.append(send)
        return sends

    def stage3(k, copies):
        order = PART_ORDERS[k]
        for copy in copies:
            copy.wait_recv()
        me = place[order[1]]
        total = sums[k][me].astype(jnp.float32)
        for d in range(3):
            total = total + gots[k][d].astype(jnp.float32)
        lows[k][...] = total.astype(jnp.bfloat16)
        axis = order[2]
        at = place[axis]
        sends = []
        for d in range(1, 4):
            send = remote(
                lows[k].at[lax.rem(at + d, 4)], lasts[k].at[d - 1],
                send3.at[k, d - 1], recv3.at[k, d - 1], peer_along(axis, d),
            )
            send.start()
            sends.append(send)
        return sends

    def finish(k, copies):
        for copy in copies:
            copy.wait_recv()
        me = place[PART_ORDERS[k][2]]
        total = lows[k][me].astype(jnp.float32)
        for d in range(3):
            total = total + lasts[k][d].astype(jnp.float32)
        start = sum(PART_COLS[:k])
        fin[:, start : start + PART_COLS[k]] = total

    swaps[0].wait_recv()
    swaps[1].wait_recv()
    split = PART_COLS[0] + PART_COLS[1]
    fill(part0, PART_ORDERS[0], xn2, gq2, (0, PART_COLS[0]), 0)
    first.append(stage1(0))
    fill(part1, PART_ORDERS[1], xn2, gq2, (PART_COLS[0], split), 0)
    first.append(stage1(1))
    swaps[2].wait_recv()
    swaps[3].wait_recv()
    fill(part2, PART_ORDERS[2], xn2, gq2, (split, qh), 0)
    fill(part2, PART_ORDERS[2], ab2, gb2, (0, oh), qh - split)
    first.append(stage1(2))
    for k in range(3):
        add_relay(k, *first[k])
    second = [stage2(k, first[k][0]) for k in range(3)]
    third = [stage3(k, second[k]) for k in range(3)]
    for k in range(3):
        finish(k, third[k])

    keep, give = pl.multiple_of(core * 8, 8), pl.multiple_of((1 - core) * 8, 8)
    end = remote(fin.at[pl.ds(give, 8)], other, fin_send, fin_recv, partner)
    end.start()
    out_q[:, pl.ds(mine_q, qh)] = fin[pl.ds(keep, 8), 0:qh]
    out_o[:, pl.ds(mine_o, oh)] = fin[pl.ds(keep, 8), qh : qh + oh]
    end.wait_recv()
    out_q[:, pl.ds(its_q, qh)] = other[:, 0:qh]
    out_o[:, pl.ds(its_o, oh)] = other[:, qh : qh + oh]
    for copy in swaps + [c for f in first for c in f[0]] + [c for s in second + third for c in s] + [end]:
        copy.wait_send()


def reduce_grads(xn, gq, ab, gb):
    rows, width = xn.shape
    qw, ow = gq.shape[1], gb.shape[1]
    bf, f32 = jnp.bfloat16, jnp.float32
    vmem = pl.BlockSpec(memory_space=pltpu.VMEM)

    def each(*lead):
        return [pltpu.VMEM((*lead, 16, c), bf) for c in PART_COLS]

    return pl.pallas_call(
        grads_kernel,
        name="reduce_grads",
        out_shape=(jax.ShapeDtypeStruct((8, qw), f32), jax.ShapeDtypeStruct((8, ow), f32)),
        in_specs=[vmem] * 4,
        out_specs=(vmem, vmem),
        scratch_shapes=[
            pltpu.VMEM((2 * rows, width), bf),
            pltpu.VMEM((2 * rows, qw // 2), bf),
            pltpu.VMEM((2 * rows, width), bf),
            pltpu.VMEM((2 * rows, ow // 2), bf),
            *each(4, 4, 4), *each(2, 2, 4), *each(2, 4, 4),
            *each(4, 4), *each(3, 4), *each(4), *each(3),
            pltpu.VMEM((16, (qw + ow) // 2), f32),
            pltpu.VMEM((8, (qw + ow) // 2), f32),
            pltpu.SemaphoreType.DMA((4,)), pltpu.SemaphoreType.DMA((4,)),
            pltpu.SemaphoreType.DMA((3, 6)), pltpu.SemaphoreType.DMA((3, 6)),
            pltpu.SemaphoreType.DMA((3, 3)), pltpu.SemaphoreType.DMA((3, 3)),
            pltpu.SemaphoreType.DMA((3, 3)), pltpu.SemaphoreType.DMA((3, 3)),
            pltpu.SemaphoreType.DMA, pltpu.SemaphoreType.DMA,
        ],
        compiler_params=pltpu.CompilerParams(collective_id=5, has_side_effects=True, vmem_limit_bytes=48 << 20),
    )(xn, gq, ab, gb)


CHUNK = 512
LANES = 4096


def out_kernel(
    att_ref, w_ref, out_ref, att2, w2, pbuf, relay, near, psum, pgot, qbuf, qgot, qsum, qlast, fin, other,
    w_sem, pair_send, pair_recv, p_send, p_recv, q_send, q_recv, att_send, att_recv, fin_send, fin_recv,
):
    x, y, z, core = coords()
    pair = lax.rem(y, 2)
    partner = device_at(x, y, z, 1 - core)
    across = device_at(x, y + 1 - 2 * pair, z, core)

    def beside(step):
        return device_at(lax.rem(x + step, 4), y, z, core)

    greet([partner, across, beside(1), beside(2), beside(3)])
    depth = att_ref.shape[1]
    copies = []

    def begin(copy):
        copy.start()
        copies.append(copy)
        return copy

    swap = begin(remote(att_ref, att2.at[:, depth : 2 * depth], att_send, att_recv, partner))
    order = [c for n in range(4) for c in (4 + n, n)]
    theirs, mine = {}, {}
    for c in order:
        into = pl.ds(c * CHUNK, CHUNK)
        give = pl.ds(pl.multiple_of((1 - core) * LANES + c * CHUNK, CHUNK), CHUNK)
        keep = pl.ds(pl.multiple_of(core * LANES + c * CHUNK, CHUNK), CHUNK)
        theirs[c] = begin(
            remote(w_ref.at[:, give], w2.at[pl.ds(depth, depth), into], pair_send.at[c], pair_recv.at[c], partner)
        )
        mine[c] = pltpu.make_async_copy(w_ref.at[:, keep], w2.at[pl.ds(0, depth), into], w_sem.at[c])
        mine[c].start()
    att2[:, 0:depth] = att_ref[...]
    swap.wait_recv()

    right, left, far = lax.rem(x + 1, 4), lax.rem(x + 3, 4), lax.rem(x + 2, 4)
    pcopies, qcopies = {}, {}
    for c in order:
        mine[c].wait()
        theirs[c].wait_recv()
        block = jnp.dot(
            att2[...], w2[:, c * CHUNK : (c + 1) * CHUNK], preferred_element_type=jnp.float32
        ).astype(jnp.bfloat16)
        for row in range(8):
            piece = block[row * 48 : row * 48 + 48]
            if c < 4:
                pbuf[c, row % 4, row // 4] = piece
            else:
                qbuf[c - 4, row // 4, row % 4] = piece
        if c < 4:

            def copy(k, source, target, peer):
                return remote(source, target, p_send.at[c, k], p_recv.at[c, k], peer)

            pcopies[c] = [
                copy(0, pbuf.at[c, far, 0], relay.at[c, 0], beside(1)),
                copy(1, pbuf.at[c, far, 1], relay.at[c, 1], beside(3)),
                copy(2, pbuf.at[c, right, 1], near.at[c, 0, 1], beside(1)),
                copy(3, pbuf.at[c, left, 0], near.at[c, 1, 0], beside(3)),
                copy(4, pbuf.at[c, right, 0], near.at[c, 0, 0], beside(1)),
                copy(5, pbuf.at[c, left, 1], near.at[c, 1, 1], beside(3)),
                copy(6, psum.at[c, 1 - pair], pgot.at[c], across),
            ]
            for k in range(4):
                begin(pcopies[c][k])
        else:
            n = c - 4
            qcopies[n] = [remote(qbuf.at[n, 1 - pair], qgot.at[n], q_send.at[n, 0], q_recv.at[n, 0], across)] + [
                remote(qsum.at[n, lax.rem(x + d, 4)], qlast.at[n, d - 1], q_send.at[n, d], q_recv.at[n, d], beside(d))
                for d in (1, 2, 3)
            ]
            begin(qcopies[n][0])

    def wide(value):
        return value.astype(jnp.float32)

    def p_relay(n):
        for k, side in ((0, right), (1, left)):
            pcopies[n][k].wait_recv()
            pbuf[n, side, k] = (wide(pbuf[n, side, k]) + wide(relay[n, k])).astype(jnp.bfloat16)
            begin(pcopies[n][4 + k])

    def p_across(n):
        for k in range(2, 6):
            pcopies[n][k].wait_recv()
        for k in range(2):
            psum[n, k] = (wide(pbuf[n, x, k]) + wide(near[n, 0, k]) + wide(near[n, 1, k])).astype(jnp.bfloat16)
        begin(pcopies[n][6])

    def p_end(n):
        pcopies[n][6].wait_recv()
        fin[:, n * CHUNK : (n + 1) * CHUNK] = wide(psum[n, pair]) + wide(pgot[n])

    def q_beside(n):
        qcopies[n][0].wait_recv()
        for k in range(4):
            qsum[n, k] = (wide(qbuf[n, pair, k]) + wide(qgot[n, k])).astype(jnp.bfloat16)
        for k in (2, 1, 3):
            begin(qcopies[n][k])

    def q_end(n):
        for k in (1, 2, 3):
            qcopies[n][k].wait_recv()
        total = wide(qsum[n, x])
        for k in range(3):
            total = total + wide(qlast[n, k])
        fin[:, (4 + n) * CHUNK : (5 + n) * CHUNK] = total

    p_relay(0)
    p_relay(1)
    q_beside(0)
    p_relay(2)
    p_relay(3)
    q_beside(1)
    p_across(0)
    p_across(1)
    q_beside(2)
    p_across(2)
    p_across(3)
    q_end(0)
    q_end(1)
    q_beside(3)
    for n in range(4):
        p_end(n)
    q_end(2)
    q_end(3)

    keep, give = pl.multiple_of(core * 24, 8), pl.multiple_of((1 - core) * 24, 8)
    end = begin(remote(fin.at[pl.ds(give, 24)], other, fin_send, fin_recv, partner))
    for b in range(4):
        out_ref[:, core * 4 + b, :] = fin[pl.ds(keep, 24), b * 1024 : b * 1024 + 1024]
    end.wait_recv()
    for b in range(4):
        out_ref[:, (1 - core) * 4 + b, :] = other[:, b * 1024 : b * 1024 + 1024]
    for copy in copies:
        copy.wait_send()


def project_out(att, w):
    rows, depth = att.shape
    bf, f32 = jnp.bfloat16, jnp.float32
    vmem = pl.BlockSpec(memory_space=pltpu.VMEM)

    def units(*lead):
        return pltpu.VMEM((*lead, 48, CHUNK), bf)

    def sems(*shape):
        return pltpu.SemaphoreType.DMA(shape)

    return pl.pallas_call(
        out_kernel,
        name="project_out",
        out_shape=jax.ShapeDtypeStruct((24, 8, 1024), f32),
        in_specs=[vmem, pl.BlockSpec(memory_space=pl.ANY)],
        out_specs=vmem,
        scratch_shapes=[
            pltpu.VMEM((rows, 2 * depth), bf),
            pltpu.VMEM((2 * depth, LANES), bf),
            units(4, 4, 2), units(4, 2), units(4, 2, 2), units(4, 2), units(4),
            units(4, 2, 4), units(4, 4), units(4, 4), units(4, 3),
            pltpu.VMEM((48, LANES), f32),
            pltpu.VMEM((24, LANES), f32),
            sems(8), sems(8), sems(8), sems(4, 7), sems(4, 7), sems(4, 4), sems(4, 4),
            pltpu.SemaphoreType.DMA, pltpu.SemaphoreType.DMA,
            pltpu.SemaphoreType.DMA, pltpu.SemaphoreType.DMA,
        ],
        compiler_params=pltpu.CompilerParams(collective_id=3, has_side_effects=True, vmem_limit_bytes=40 << 20),
    )(att, w)


def rms_norm(values):
    return values * lax.rsqrt(jnp.mean(values * values, axis=-1, keepdims=True) + 1e-06)


def local_core(qkv_rows):
    total = qkv_rows.shape[0]
    groups = total // PATCH
    width = qkv_rows.shape[1] // 3
    parts = qkv_rows.reshape(groups, PATCH, 3, LOCAL_HEADS, LOCAL_HEAD_DIM)
    queries = rms_norm(parts[:, :, 0])
    keys_all = rms_norm(parts[:, :, 1])
    values = parts[:, :, 2]
    scores = jnp.einsum("npha,nqha->nhpq", queries, keys_all) / math.sqrt(LOCAL_HEAD_DIM)
    causal = jnp.arange(PATCH)[:, None] >= jnp.arange(PATCH)[None, :]
    weights = jnp.where(causal[None, None], jnp.exp(scores), 0.0)
    numerator = jnp.einsum("nhpq,nqha->npha", weights, values)
    denominator = jnp.sum(weights, axis=-1).transpose(0, 2, 1)[..., None]
    return (numerator / denominator).reshape(total, width)


def local_pass(state, local_qkv, local_out, cotangent):
    layer = 0
    normed = rms_norm(state).astype(jnp.bfloat16)
    qkv_rows = jnp.dot(normed, local_qkv[layer], preferred_element_type=jnp.float32)
    core, core_back = jax.vjp(local_core, qkv_rows)
    attended = core.astype(jnp.bfloat16)
    saved = [(state, normed, core_back, attended)]
    state = state + jnp.dot(attended, local_out[layer], preferred_element_type=jnp.float32)
    hidden = state.astype(jnp.bfloat16)
    grad_state = cotangent.astype(jnp.float32)
    layer = 0
    before, normed, core_back, attended = saved[layer]
    grad_round = grad_state.astype(jnp.bfloat16)
    grad_core = jnp.dot(grad_round, local_out[layer].T, preferred_element_type=jnp.float32)
    grad_rows = core_back(grad_core)[0].astype(jnp.bfloat16)
    return hidden, normed, grad_rows, attended, grad_round


def per_device(byte_embeds, local_embeds, global_qkv, global_out, local_qkv, local_out, cotangent):
    byte_count = byte_embeds.shape[0]
    patch_count = byte_count // PATCH
    full_width = PATCH * byte_embeds.shape[1]
    patch_in = byte_embeds.reshape(patch_count, full_width).astype(jnp.float32)
    normed = rms_norm(patch_in).astype(jnp.bfloat16)
    projected = jnp.einsum(
        "nd,cdh->nch",
        lax.all_gather(normed, "tp", axis=0, tiled=True),
        global_qkv,
        preferred_element_type=jnp.float32,
    )
    shard_rows = projected.shape[0]
    head_width = global_qkv.shape[2]
    head_count = head_width // HEAD_DIM
    queries = rms_norm(projected[:, 0].reshape(shard_rows, head_count, HEAD_DIM)).astype(
        jnp.bfloat16
    )
    keys_mine = rms_norm(projected[:, 1].reshape(shard_rows, head_count, HEAD_DIM)).astype(
        jnp.bfloat16
    )
    values_mine = projected[:, 2].reshape(shard_rows, head_count, HEAD_DIM).astype(jnp.bfloat16)
    query_pos = lax.axis_index("ctx") * shard_rows + jnp.arange(shard_rows, dtype=jnp.int32)
    pieces = lax.all_gather(
        jnp.concatenate([keys_mine, values_mine], axis=1), "ctx", axis=0, tiled=True
    )
    key_piece, value_piece = pieces[:, :head_count], pieces[:, head_count:]
    key_count = key_piece.shape[0]
    scores = jnp.einsum(
        "rha,kha->rhk", queries, key_piece, preferred_element_type=jnp.float32
    ) / math.sqrt(HEAD_DIM)
    key_pos = jnp.arange(key_count, dtype=jnp.int32)
    allowed = key_pos[None, None, :] <= query_pos[:, None, None]
    expo = jnp.where(allowed, jnp.exp(scores), 0.0)
    numerator = jnp.einsum(
        "rhk,kha->rha", expo.astype(jnp.bfloat16), value_piece, preferred_element_type=jnp.float32
    )
    denominator = jnp.sum(expo, axis=-1)
    numerator, denominator = (numerator, denominator)
    attended = (
        (numerator / denominator[..., None]).reshape(shard_rows, head_width).astype(jnp.bfloat16)
    )
    before = from_behind(attended[-1:], "ctx", 1)
    attended = jnp.concatenate([before, attended[:-1]], axis=0)
    context = project_out(attended, global_out).reshape(byte_count, byte_embeds.shape[1])
    context = context.astype(jnp.bfloat16)
    state = local_embeds.astype(jnp.float32) + context.astype(jnp.float32)
    hidden, *factors = local_pass(state, local_qkv, local_out, cotangent)
    grad_qkv, grad_out = reduce_grads(*factors)
    return (hidden, grad_qkv[None], grad_out[None])


def solution(mesh):
    in_specs = (
        P(("ctx", "tp"), None),
        P(("ctx", "tp"), None),
        P(None, None, "tp"),
        P("tp", None),
        P(),
        P(),
        P(("ctx", "tp"), None),
    )
    out_specs = (P(("ctx", "tp"), None), P(None, ("ctx", "tp"), None), P(None, ("ctx", "tp"), None))
    return jax.shard_map(
        per_device, mesh=mesh, in_specs=in_specs, out_specs=out_specs, check_vma=False
    )
```

```python
import math

import jax
import jax.numpy as jnp
from jax import lax
from jax.experimental import pallas as pl
from jax.experimental.pallas import tpu as pltpu
from jax.sharding import PartitionSpec as P

PATCH = 8
HEAD_DIM = 128
LOCAL_HEADS = 8
LOCAL_HEAD_DIM = 128


MESH = pl.DeviceIdType.MESH


def coords():
    ctx, tp = lax.axis_index("ctx"), lax.axis_index("tp")
    x, core = lax.rem(lax.div(tp, 2), 4), lax.rem(tp, 2)
    y = lax.rem(ctx, 2) * 2 + lax.div(tp, 8)
    return x, y, lax.div(ctx, 2), core


def device_at(x, y, z, core):
    return {"ctx": z * 2 + lax.div(y, 2), "tp": lax.rem(y, 2) * 8 + x * 2 + core}


def greet(peers):
    barrier = pltpu.get_barrier_semaphore()
    for peer in peers:
        pl.semaphore_signal(barrier, inc=1, device_id=peer, device_id_type=MESH)
    pl.semaphore_wait(barrier, len(peers))


def remote(source, target, send_sem, recv_sem, peer):
    return pltpu.make_async_remote_copy(
        src_ref=source,
        dst_ref=target,
        send_sem=send_sem,
        recv_sem=recv_sem,
        device_id=peer,
        device_id_type=MESH,
    )


PART_COLS = (640, 640, 768)
PART_ORDERS = ((0, 1, 2), (1, 2, 0), (2, 0, 1))


def grads_kernel(
    xn_ref, gq_ref, ab_ref, gb_ref, out_q, out_o,
    xn2, gq2, ab2, gb2,
    part0, part1, part2, relay0, relay1, relay2, near0, near1, near2,
    sum0, sum1, sum2, got0, got1, got2, low0, low1, low2, last0, last1, last2,
    fin, other, pair_send, pair_recv, send1, recv1, send2, recv2, send3, recv3,
    fin_send, fin_recv,
):
    place = coords()
    core = place[3]

    def peer_along(axis, step):
        at = list(place)
        at[axis] = lax.rem(at[axis] + step, 4)
        return device_at(*at)

    partner = device_at(place[0], place[1], place[2], 1 - core)
    greet([partner] + [peer_along(axis, step) for axis in range(3) for step in (1, 2, 3)])

    rows = xn_ref.shape[0]
    qh, oh = gq2.shape[1], gb2.shape[1]
    mine_q, mine_o = pl.multiple_of(core * qh, qh), pl.multiple_of(core * oh, oh)
    its_q, its_o = pl.multiple_of((1 - core) * qh, qh), pl.multiple_of((1 - core) * oh, oh)
    bottom = pl.ds(rows, rows)
    swaps = [
        remote(xn_ref, xn2.at[bottom], pair_send.at[0], pair_recv.at[0], partner),
        remote(gq_ref.at[:, pl.ds(its_q, qh)], gq2.at[bottom], pair_send.at[1], pair_recv.at[1], partner),
        remote(ab_ref, ab2.at[bottom], pair_send.at[2], pair_recv.at[2], partner),
        remote(gb_ref.at[:, pl.ds(its_o, oh)], gb2.at[bottom], pair_send.at[3], pair_recv.at[3], partner),
    ]
    for swap in swaps:
        swap.start()
    top = pl.ds(0, rows)
    xn2[top] = xn_ref[...]
    gq2[top] = gq_ref[:, pl.ds(mine_q, qh)]
    ab2[top] = ab_ref[...]
    gb2[top] = gb_ref[:, pl.ds(mine_o, oh)]

    parts = (part0, part1, part2)
    relays, nears = (relay0, relay1, relay2), (near0, near1, near2)
    sums, gots = (sum0, sum1, sum2), (got0, got1, got2)
    lows, lasts = (low0, low1, low2), (last0, last1, last2)

    def fill(part, order, left, right, columns, into):
        width = columns[1] - columns[0]
        for z in range(4):
            block = lax.dot_general(
                left[:, z * 256 : (z + 1) * 256],
                right[:, columns[0] : columns[1]],
                (((0,), (0,)), ((), ())),
                preferred_element_type=jnp.float32,
            ).astype(jnp.bfloat16)
            for y in range(4):
                for x in range(4):
                    at = (x, y, z)
                    row = (y * 4 + x) * 16
                    part[at[order[0]], at[order[1]], at[order[2]], :, into : into + width] = block[
                        row : row + 16
                    ]

    first = []

    def stage1(k):
        order = PART_ORDERS[k]
        axis = order[0]
        me = place[axis]
        right, left, far = lax.rem(me + 1, 4), lax.rem(me + 3, 4), lax.rem(me + 2, 4)
        to_right, to_left = peer_along(axis, 1), peer_along(axis, 3)
        part, relay, near = parts[k], relays[k], nears[k]
        lo, hi = pl.ds(0, 2), pl.ds(2, 2)

        def copy(n, source, target, peer):
            return remote(source, target, send1.at[k, n], recv1.at[k, n], peer)

        copies = [
            copy(0, part.at[far, lo], relay.at[0], to_right),
            copy(1, part.at[far, hi], relay.at[1], to_left),
            copy(2, part.at[right, hi], near.at[0, hi], to_right),
            copy(3, part.at[left, lo], near.at[1, lo], to_left),
            copy(4, part.at[right, lo], near.at[0, lo], to_right),
            copy(5, part.at[left, hi], near.at[1, hi], to_left),
        ]
        for n in range(4):
            copies[n].start()
        return copies, (right, left)

    def add_relay(k, copies, sides):
        part, relay = parts[k], relays[k]
        for n in range(2):
            copies[n].wait_recv()
            for j in range(2):
                at = 2 * n + j
                part[sides[n], at] = (
                    part[sides[n], at].astype(jnp.float32) + relay[n, j].astype(jnp.float32)
                ).astype(jnp.bfloat16)
            copies[4 + n].start()

    def stage2(k, copies):
        order = PART_ORDERS[k]
        for n in range(2, 6):
            copies[n].wait_recv()
        me = place[order[0]]
        for j in range(4):
            sums[k][j] = (
                parts[k][me, j].astype(jnp.float32)
                + nears[k][0, j].astype(jnp.float32)
                + nears[k][1, j].astype(jnp.float32)
            ).astype(jnp.bfloat16)
        axis = order[1]
        at = place[axis]
        sends = []
        for d in range(1, 4):
            send = remote(
                sums[k].at[lax.rem(at + d, 4)], gots[k].at[d - 1],
                send2.at[k, d - 1], recv2.at[k, d - 1], peer_along(axis, d),
            )
            send.start()
            sends.append(send)
        return sends

    def stage3(k, copies):
        order = PART_ORDERS[k]
        for copy in copies:
            copy.wait_recv()
        me = place[order[1]]
        total = sums[k][me].astype(jnp.float32)
        for d in range(3):
            total = total + gots[k][d].astype(jnp.float32)
        lows[k][...] = total.astype(jnp.bfloat16)
        axis = order[2]
        at = place[axis]
        sends = []
        for d in range(1, 4):
            send = remote(
                lows[k].at[lax.rem(at + d, 4)], lasts[k].at[d - 1],
                send3.at[k, d - 1], recv3.at[k, d - 1], peer_along(axis, d),
            )
            send.start()
            sends.append(send)
        return sends

    def finish(k, copies):
        for copy in copies:
            copy.wait_recv()
        me = place[PART_ORDERS[k][2]]
        total = lows[k][me].astype(jnp.float32)
        for d in range(3):
            total = total + lasts[k][d].astype(jnp.float32)
        start = sum(PART_COLS[:k])
        fin[:, start : start + PART_COLS[k]] = total

    swaps[0].wait_recv()
    swaps[1].wait_recv()
    split = PART_COLS[0] + PART_COLS[1]
    fill(part0, PART_ORDERS[0], xn2, gq2, (0, PART_COLS[0]), 0)
    first.append(stage1(0))
    fill(part1, PART_ORDERS[1], xn2, gq2, (PART_COLS[0], split), 0)
    first.append(stage1(1))
    swaps[2].wait_recv()
    swaps[3].wait_recv()
    fill(part2, PART_ORDERS[2], xn2, gq2, (split, qh), 0)
    fill(part2, PART_ORDERS[2], ab2, gb2, (0, oh), qh - split)
    first.append(stage1(2))
    for k in range(3):
        add_relay(k, *first[k])
    second = [stage2(k, first[k][0]) for k in range(3)]
    third = [stage3(k, second[k]) for k in range(3)]
    for k in range(3):
        finish(k, third[k])

    keep, give = pl.multiple_of(core * 8, 8), pl.multiple_of((1 - core) * 8, 8)
    end = remote(fin.at[pl.ds(give, 8)], other, fin_send, fin_recv, partner)
    end.start()
    out_q[:, pl.ds(mine_q, qh)] = fin[pl.ds(keep, 8), 0:qh]
    out_o[:, pl.ds(mine_o, oh)] = fin[pl.ds(keep, 8), qh : qh + oh]
    end.wait_recv()
    out_q[:, pl.ds(its_q, qh)] = other[:, 0:qh]
    out_o[:, pl.ds(its_o, oh)] = other[:, qh : qh + oh]
    for copy in swaps + [c for f in first for c in f[0]] + [c for s in second + third for c in s] + [end]:
        copy.wait_send()


def reduce_grads(xn, gq, ab, gb):
    rows, width = xn.shape
    qw, ow = gq.shape[1], gb.shape[1]
    bf, f32 = jnp.bfloat16, jnp.float32
    vmem = pl.BlockSpec(memory_space=pltpu.VMEM)

    def each(*lead):
        return [pltpu.VMEM((*lead, 16, c), bf) for c in PART_COLS]

    return pl.pallas_call(
        grads_kernel,
        name="reduce_grads",
        out_shape=(jax.ShapeDtypeStruct((8, qw), f32), jax.ShapeDtypeStruct((8, ow), f32)),
        in_specs=[vmem] * 4,
        out_specs=(vmem, vmem),
        scratch_shapes=[
            pltpu.VMEM((2 * rows, width), bf),
            pltpu.VMEM((2 * rows, qw // 2), bf),
            pltpu.VMEM((2 * rows, width), bf),
            pltpu.VMEM((2 * rows, ow // 2), bf),
            *each(4, 4, 4), *each(2, 2, 4), *each(2, 4, 4),
            *each(4, 4), *each(3, 4), *each(4), *each(3),
            pltpu.VMEM((16, (qw + ow) // 2), f32),
            pltpu.VMEM((8, (qw + ow) // 2), f32),
            pltpu.SemaphoreType.DMA((4,)), pltpu.SemaphoreType.DMA((4,)),
            pltpu.SemaphoreType.DMA((3, 6)), pltpu.SemaphoreType.DMA((3, 6)),
            pltpu.SemaphoreType.DMA((3, 3)), pltpu.SemaphoreType.DMA((3, 3)),
            pltpu.SemaphoreType.DMA((3, 3)), pltpu.SemaphoreType.DMA((3, 3)),
            pltpu.SemaphoreType.DMA, pltpu.SemaphoreType.DMA,
        ],
        compiler_params=pltpu.CompilerParams(collective_id=5, has_side_effects=True, vmem_limit_bytes=48 << 20),
    )(xn, gq, ab, gb)


CHUNK = 512
LANES = 4096


def attend(
    x, y, z, core, begin, q_ref, k_ref, v_ref, att2, q2, ka, va, acc, tall, back,
    y_send, y_recv, z_send, z_recv, row_send, row_recv, back_send, back_recv, swap_send, swap_recv,
):
    half = lax.div(y, 2)
    partner = device_at(x, y, z, 1 - core)
    opposite = device_at(x, lax.rem(y + 2, 4), z, core)
    rows = q_ref.shape[0]
    mine = pl.ds(pl.multiple_of(half * HEAD_DIM, HEAD_DIM), HEAD_DIM)
    its = pl.ds(pl.multiple_of((1 - half) * HEAD_DIM, HEAD_DIM), HEAD_DIM)

    across = [
        begin(remote(source.at[:, its], target, y_send.at[n], y_recv.at[n], opposite))
        for n, (source, target) in enumerate(
            ((k_ref, ka.at[z, half]), (v_ref, va.at[z, half]), (q_ref, q2.at[half]))
        )
    ]

    def up(d, kind, which):
        block = half if which == 0 else 1 - half
        target = (ka, va)[kind].at[z, block]
        source = (k_ref, v_ref)[kind].at[:, mine] if which == 0 else target
        return remote(
            source, target, z_send.at[d - 1, kind, which], z_recv.at[d - 1, kind, which],
            device_at(x, y, lax.rem(z + d, 4), core),
        )

    lifts = {(d, kind, which): up(d, kind, which) for which in (0, 1) for kind in (0, 1) for d in (1, 3, 2)}
    for (d, kind, which), copy in lifts.items():
        if which == 0:
            pl.when(z + d <= 3)(copy.start)
    ka[z, half] = k_ref[:, mine]
    va[z, half] = v_ref[:, mine]
    q2[half] = q_ref[:, mine]
    for kind in (0, 1):
        across[kind].wait_recv()
        for d in (1, 3, 2):
            pl.when(z + d <= 3)(lifts[d, kind, 1].start)
    across[2].wait_recv()

    tile = 128
    tiles = rows // tile
    scale = 1.0 / math.sqrt(HEAD_DIM)

    def attend_tile(block, n, keys, values, masked, first):
        s = lax.dot_general(
            q2[block, n * tile : (n + 1) * tile], keys, (((1,), (1,)), ((), ())), preferred_element_type=jnp.float32
        )
        e = jnp.exp(s * scale)
        if masked:
            row = n * tile + lax.broadcasted_iota(jnp.int32, e.shape, 0)
            e = jnp.where(lax.broadcasted_iota(jnp.int32, e.shape, 1) <= row, e, 0.0)
        sums = jnp.dot(e.astype(jnp.bfloat16), values, preferred_element_type=jnp.float32)
        at = slice(n * tile, (n + 1) * tile)
        acc[block, at] = sums if first else acc[block, at] + sums

    def with_ones(values):
        return jnp.concatenate([values, jnp.ones_like(values)], axis=1)

    for k in (0, 1):
        keys, values = ka[z, k], with_ones(va[z, k])
        for block in range(k, 2):
            for n in range(tiles):
                attend_tile(block, n, keys, values, block == k, k == 0)

    for d in (1, 3, 2):

        @pl.when(z >= d)
        def _():
            for kind in (0, 1):
                for which in (0, 1):
                    lifts[d, kind, which].wait_recv()
            below = lax.rem(z + 4 - d, 4)

            def body(k, carry):
                keys, values = ka[below, k], with_ones(va[below, k])
                for block in (0, 1):
                    for n in range(tiles):
                        attend_tile(block, n, keys, values, False, False)
                return carry

            lax.fori_loop(0, 2, body, 0)

    for block in (0, 1):
        tall[8 + block * rows : 8 + (block + 1) * rows] = acc[block, :, 0:HEAD_DIM] / acc[block, :, HEAD_DIM:]
    row = remote(
        tall.at[pl.ds(2 * rows, 8)], tall.at[pl.ds(0, 8)], row_send, row_recv,
        device_at(x, y, lax.rem(z + 1, 4), core),
    )
    pl.when(z < 3)(row.start)
    pl.when(z > 0)(row.wait_recv)

    @pl.when(z == 0)
    def _():
        tall[0:8] = jnp.zeros((8, HEAD_DIM), jnp.float32)

    for part in (0, 1):

        @pl.when(half == part)
        def _():
            back[...] = tall[7 + (1 - part) * rows : 7 + (2 - part) * rows].astype(jnp.bfloat16)
            att2[:, part * HEAD_DIM : (part + 1) * HEAD_DIM] = tall[
                7 + part * rows : 7 + (part + 1) * rows
            ].astype(jnp.bfloat16)

    width = 2 * HEAD_DIM
    far_mine = pl.ds(pl.multiple_of(width + half * HEAD_DIM, HEAD_DIM), HEAD_DIM)
    far_its = pl.ds(pl.multiple_of(width + (1 - half) * HEAD_DIM, HEAD_DIM), HEAD_DIM)
    returned = begin(remote(back, att2.at[:, mine], back_send, back_recv, opposite))
    near = begin(remote(att2.at[:, mine], att2.at[:, far_mine], swap_send.at[0], swap_recv.at[0], partner))
    returned.wait_recv()
    last = begin(remote(att2.at[:, its], att2.at[:, far_its], swap_send.at[1], swap_recv.at[1], partner))
    near.wait_recv()
    last.wait_recv()
    pl.when(z < 3)(row.wait_send)
    for (d, kind, which), copy in lifts.items():
        pl.when(z + d <= 3)(copy.wait_send)


def out_kernel(
    q_ref, k_ref, v_ref, w_ref, out_ref, q2, ka, va, acc, tall, back, att2, w2, pbuf, relay, near, psum, pgot, qbuf, qgot, qsum, qlast, fin, other,
    w_sem, pair_send, pair_recv, p_send, p_recv, q_send, q_recv, fin_send, fin_recv,
    *att_sems,
):
    x, y, z, core = coords()
    pair = lax.rem(y, 2)
    partner = device_at(x, y, z, 1 - core)
    across = device_at(x, y + 1 - 2 * pair, z, core)

    def beside(step):
        return device_at(lax.rem(x + step, 4), y, z, core)

    greet(
        [partner, across, beside(1), beside(2), beside(3), device_at(x, lax.rem(y + 2, 4), z, core)]
        + [device_at(x, y, lax.rem(z + d, 4), core) for d in (1, 2, 3)]
    )
    depth = q_ref.shape[1]
    copies = []

    def begin(copy):
        copy.start()
        copies.append(copy)
        return copy

    order = [c for n in range(4) for c in (4 + n, n)]
    theirs, mine = {}, {}
    for c in order:
        into = pl.ds(c * CHUNK, CHUNK)
        give = pl.ds(pl.multiple_of((1 - core) * LANES + c * CHUNK, CHUNK), CHUNK)
        keep = pl.ds(pl.multiple_of(core * LANES + c * CHUNK, CHUNK), CHUNK)
        theirs[c] = begin(
            remote(w_ref.at[:, give], w2.at[pl.ds(depth, depth), into], pair_send.at[c], pair_recv.at[c], partner)
        )
        mine[c] = pltpu.make_async_copy(w_ref.at[:, keep], w2.at[pl.ds(0, depth), into], w_sem.at[c])
        mine[c].start()
    attend(
        x, y, z, core, begin, q_ref, k_ref, v_ref, att2, q2, ka, va, acc, tall, back, *att_sems
    )

    right, left, far = lax.rem(x + 1, 4), lax.rem(x + 3, 4), lax.rem(x + 2, 4)
    pcopies, qcopies = {}, {}
    for c in order:
        mine[c].wait()
        theirs[c].wait_recv()
        block = jnp.dot(
            att2[...], w2[:, c * CHUNK : (c + 1) * CHUNK], preferred_element_type=jnp.float32
        ).astype(jnp.bfloat16)
        for row in range(8):
            piece = block[row * 48 : row * 48 + 48]
            if c < 4:
                pbuf[c, row % 4, row // 4] = piece
            else:
                qbuf[c - 4, row // 4, row % 4] = piece
        if c < 4:

            def copy(k, source, target, peer):
                return remote(source, target, p_send.at[c, k], p_recv.at[c, k], peer)

            pcopies[c] = [
                copy(0, pbuf.at[c, far, 0], relay.at[c, 0], beside(1)),
                copy(1, pbuf.at[c, far, 1], relay.at[c, 1], beside(3)),
                copy(2, pbuf.at[c, right, 1], near.at[c, 0, 1], beside(1)),
                copy(3, pbuf.at[c, left, 0], near.at[c, 1, 0], beside(3)),
                copy(4, pbuf.at[c, right, 0], near.at[c, 0, 0], beside(1)),
                copy(5, pbuf.at[c, left, 1], near.at[c, 1, 1], beside(3)),
                copy(6, psum.at[c, 1 - pair], pgot.at[c], across),
            ]
            for k in range(4):
                begin(pcopies[c][k])
        else:
            n = c - 4
            qcopies[n] = [remote(qbuf.at[n, 1 - pair], qgot.at[n], q_send.at[n, 0], q_recv.at[n, 0], across)] + [
                remote(qsum.at[n, lax.rem(x + d, 4)], qlast.at[n, d - 1], q_send.at[n, d], q_recv.at[n, d], beside(d))
                for d in (1, 2, 3)
            ]
            begin(qcopies[n][0])

    def wide(value):
        return value.astype(jnp.float32)

    def p_relay(n):
        for k, side in ((0, right), (1, left)):
            pcopies[n][k].wait_recv()
            pbuf[n, side, k] = (wide(pbuf[n, side, k]) + wide(relay[n, k])).astype(jnp.bfloat16)
            begin(pcopies[n][4 + k])

    def p_across(n):
        for k in range(2, 6):
            pcopies[n][k].wait_recv()
        for k in range(2):
            psum[n, k] = (wide(pbuf[n, x, k]) + wide(near[n, 0, k]) + wide(near[n, 1, k])).astype(jnp.bfloat16)
        begin(pcopies[n][6])

    def p_end(n):
        pcopies[n][6].wait_recv()
        fin[:, n * CHUNK : (n + 1) * CHUNK] = wide(psum[n, pair]) + wide(pgot[n])

    def q_beside(n):
        qcopies[n][0].wait_recv()
        for k in range(4):
            qsum[n, k] = (wide(qbuf[n, pair, k]) + wide(qgot[n, k])).astype(jnp.bfloat16)
        for k in (2, 1, 3):
            begin(qcopies[n][k])

    def q_end(n):
        for k in (1, 2, 3):
            qcopies[n][k].wait_recv()
        total = wide(qsum[n, x])
        for k in range(3):
            total = total + wide(qlast[n, k])
        fin[:, (4 + n) * CHUNK : (5 + n) * CHUNK] = total

    p_relay(0)
    p_relay(1)
    q_beside(0)
    p_relay(2)
    p_relay(3)
    q_beside(1)
    p_across(0)
    p_across(1)
    q_beside(2)
    p_across(2)
    p_across(3)
    q_end(0)
    q_end(1)
    q_beside(3)
    for n in range(4):
        p_end(n)
    q_end(2)
    q_end(3)

    keep, give = pl.multiple_of(core * 24, 8), pl.multiple_of((1 - core) * 24, 8)
    end = begin(remote(fin.at[pl.ds(give, 24)], other, fin_send, fin_recv, partner))
    for b in range(4):
        out_ref[:, core * 4 + b, :] = fin[pl.ds(keep, 24), b * 1024 : b * 1024 + 1024]
    end.wait_recv()
    for b in range(4):
        out_ref[:, (1 - core) * 4 + b, :] = other[:, b * 1024 : b * 1024 + 1024]
    for copy in copies:
        copy.wait_send()


def attend_and_project(q, k, v, w):
    rows, depth = q.shape
    bf, f32 = jnp.bfloat16, jnp.float32
    vmem = pl.BlockSpec(memory_space=pltpu.VMEM)

    def units(*lead):
        return pltpu.VMEM((*lead, 48, CHUNK), bf)

    def sems(*shape):
        return pltpu.SemaphoreType.DMA(shape)

    return pl.pallas_call(
        out_kernel,
        name="attend_out",
        out_shape=jax.ShapeDtypeStruct((24, 8, 1024), f32),
        in_specs=[vmem] * 3 + [pl.BlockSpec(memory_space=pl.ANY)],
        out_specs=vmem,
        scratch_shapes=[
            pltpu.VMEM((2, rows, HEAD_DIM), bf),
            pltpu.VMEM((4, 2, rows, HEAD_DIM), bf),
            pltpu.VMEM((4, 2, rows, HEAD_DIM), bf),
            pltpu.VMEM((2, rows, 2 * HEAD_DIM), f32),
            pltpu.VMEM((8 + 2 * rows, HEAD_DIM), f32),
            pltpu.VMEM((rows, HEAD_DIM), bf),
            pltpu.VMEM((rows, 2 * depth), bf),
            pltpu.VMEM((2 * depth, LANES), bf),
            units(4, 4, 2), units(4, 2), units(4, 2, 2), units(4, 2), units(4),
            units(4, 2, 4), units(4, 4), units(4, 4), units(4, 3),
            pltpu.VMEM((48, LANES), f32),
            pltpu.VMEM((24, LANES), f32),
            sems(8), sems(8), sems(8), sems(4, 7), sems(4, 7), sems(4, 4), sems(4, 4),
            pltpu.SemaphoreType.DMA, pltpu.SemaphoreType.DMA,
            sems(3), sems(3), sems(3, 2, 2), sems(3, 2, 2),
            pltpu.SemaphoreType.DMA, pltpu.SemaphoreType.DMA,
            pltpu.SemaphoreType.DMA, pltpu.SemaphoreType.DMA, sems(2), sems(2),
        ],
        compiler_params=pltpu.CompilerParams(collective_id=3, has_side_effects=True, vmem_limit_bytes=40 << 20),
    )(q, k, v, w)


def rms_norm(values):
    return values * lax.rsqrt(jnp.mean(values * values, axis=-1, keepdims=True) + 1e-06)


def local_core(qkv_rows):
    total = qkv_rows.shape[0]
    groups = total // PATCH
    width = qkv_rows.shape[1] // 3
    parts = qkv_rows.reshape(groups, PATCH, 3, LOCAL_HEADS, LOCAL_HEAD_DIM)
    queries = rms_norm(parts[:, :, 0])
    keys_all = rms_norm(parts[:, :, 1])
    values = parts[:, :, 2]
    scores = jnp.einsum("npha,nqha->nhpq", queries, keys_all) / math.sqrt(LOCAL_HEAD_DIM)
    causal = jnp.arange(PATCH)[:, None] >= jnp.arange(PATCH)[None, :]
    weights = jnp.where(causal[None, None], jnp.exp(scores), 0.0)
    numerator = jnp.einsum("nhpq,nqha->npha", weights, values)
    denominator = jnp.sum(weights, axis=-1).transpose(0, 2, 1)[..., None]
    return (numerator / denominator).reshape(total, width)


def local_pass(state, local_qkv, local_out, cotangent):
    layer = 0
    normed = rms_norm(state).astype(jnp.bfloat16)
    qkv_rows = jnp.dot(normed, local_qkv[layer], preferred_element_type=jnp.float32)
    core, core_back = jax.vjp(local_core, qkv_rows)
    attended = core.astype(jnp.bfloat16)
    saved = [(state, normed, core_back, attended)]
    state = state + jnp.dot(attended, local_out[layer], preferred_element_type=jnp.float32)
    hidden = state.astype(jnp.bfloat16)
    grad_state = cotangent.astype(jnp.float32)
    layer = 0
    before, normed, core_back, attended = saved[layer]
    grad_round = grad_state.astype(jnp.bfloat16)
    grad_core = jnp.dot(grad_round, local_out[layer].T, preferred_element_type=jnp.float32)
    grad_rows = core_back(grad_core)[0].astype(jnp.bfloat16)
    return hidden, normed, grad_rows, attended, grad_round


def per_device(byte_embeds, local_embeds, global_qkv, global_out, local_qkv, local_out, cotangent):
    byte_count = byte_embeds.shape[0]
    patch_count = byte_count // PATCH
    full_width = PATCH * byte_embeds.shape[1]
    patch_in = byte_embeds.reshape(patch_count, full_width).astype(jnp.float32)
    normed = rms_norm(patch_in).astype(jnp.bfloat16)
    projected = jnp.einsum(
        "nd,cdh->nch",
        lax.all_gather(normed, "tp", axis=0, tiled=True),
        global_qkv,
        preferred_element_type=jnp.float32,
    )
    shard_rows = projected.shape[0]
    head_width = global_qkv.shape[2]
    head_count = head_width // HEAD_DIM
    queries = rms_norm(projected[:, 0].reshape(shard_rows, head_count, HEAD_DIM)).astype(
        jnp.bfloat16
    )
    keys_mine = rms_norm(projected[:, 1].reshape(shard_rows, head_count, HEAD_DIM)).astype(
        jnp.bfloat16
    )
    values_mine = projected[:, 2].reshape(shard_rows, head_count, HEAD_DIM).astype(jnp.bfloat16)
    flat = [part.reshape(shard_rows, head_width) for part in (queries, keys_mine, values_mine)]
    context = attend_and_project(*flat, global_out).reshape(byte_count, byte_embeds.shape[1])
    context = context.astype(jnp.bfloat16)
    state = local_embeds.astype(jnp.float32) + context.astype(jnp.float32)
    hidden, *factors = local_pass(state, local_qkv, local_out, cotangent)
    grad_qkv, grad_out = reduce_grads(*factors)
    return (hidden, grad_qkv[None], grad_out[None])


def solution(mesh):
    in_specs = (
        P(("ctx", "tp"), None),
        P(("ctx", "tp"), None),
        P(None, None, "tp"),
        P("tp", None),
        P(),
        P(),
        P(("ctx", "tp"), None),
    )
    out_specs = (P(("ctx", "tp"), None), P(None, ("ctx", "tp"), None), P(None, ("ctx", "tp"), None))
    return jax.shard_map(
        per_device, mesh=mesh, in_specs=in_specs, out_specs=out_specs, check_vma=False
    )
```

```python
import math

import jax
import jax.numpy as jnp
from jax import lax
from jax.experimental import pallas as pl
from jax.experimental.pallas import tpu as pltpu
from jax.sharding import PartitionSpec as P

PATCH = 8
HEAD_DIM = 128
LOCAL_HEADS = 8
LOCAL_HEAD_DIM = 128


MESH = pl.DeviceIdType.MESH


def coords():
    ctx, tp = lax.axis_index("ctx"), lax.axis_index("tp")
    x, core = lax.rem(lax.div(tp, 2), 4), lax.rem(tp, 2)
    y = lax.rem(ctx, 2) * 2 + lax.div(tp, 8)
    return x, y, lax.div(ctx, 2), core


def device_at(x, y, z, core):
    return {"ctx": z * 2 + lax.div(y, 2), "tp": lax.rem(y, 2) * 8 + x * 2 + core}


def greet(peers):
    barrier = pltpu.get_barrier_semaphore()
    for peer in peers:
        pl.semaphore_signal(barrier, inc=1, device_id=peer, device_id_type=MESH)
    pl.semaphore_wait(barrier, len(peers))


def remote(source, target, send_sem, recv_sem, peer):
    return pltpu.make_async_remote_copy(
        src_ref=source,
        dst_ref=target,
        send_sem=send_sem,
        recv_sem=recv_sem,
        device_id=peer,
        device_id_type=MESH,
    )


PART_COLS = (640, 640, 768)
PART_ORDERS = ((0, 1, 2), (1, 2, 0), (2, 0, 1))


def grads_kernel(
    xn_ref, gq_ref, ab_ref, gb_ref, out_q, out_o,
    xn2, gq2, ab2, gb2,
    part0, part1, part2, relay0, relay1, relay2, near0, near1, near2,
    sum0, sum1, sum2, got0, got1, got2, low0, low1, low2, last0, last1, last2,
    fin, other, pair_send, pair_recv, send1, recv1, send2, recv2, send3, recv3,
    fin_send, fin_recv,
):
    place = coords()
    core = place[3]

    def peer_along(axis, step):
        at = list(place)
        at[axis] = lax.rem(at[axis] + step, 4)
        return device_at(*at)

    partner = device_at(place[0], place[1], place[2], 1 - core)
    greet([partner] + [peer_along(axis, step) for axis in range(3) for step in (1, 2, 3)])

    rows = xn_ref.shape[0]
    qh, oh = gq2.shape[1], gb2.shape[1]
    mine_q, mine_o = pl.multiple_of(core * qh, qh), pl.multiple_of(core * oh, oh)
    its_q, its_o = pl.multiple_of((1 - core) * qh, qh), pl.multiple_of((1 - core) * oh, oh)
    bottom = pl.ds(rows, rows)
    swaps = [
        remote(xn_ref, xn2.at[bottom], pair_send.at[0], pair_recv.at[0], partner),
        remote(gq_ref.at[:, pl.ds(its_q, qh)], gq2.at[bottom], pair_send.at[1], pair_recv.at[1], partner),
        remote(ab_ref, ab2.at[bottom], pair_send.at[2], pair_recv.at[2], partner),
        remote(gb_ref.at[:, pl.ds(its_o, oh)], gb2.at[bottom], pair_send.at[3], pair_recv.at[3], partner),
    ]
    for swap in swaps:
        swap.start()
    top = pl.ds(0, rows)
    xn2[top] = xn_ref[...]
    gq2[top] = gq_ref[:, pl.ds(mine_q, qh)]
    ab2[top] = ab_ref[...]
    gb2[top] = gb_ref[:, pl.ds(mine_o, oh)]

    parts = (part0, part1, part2)
    relays, nears = (relay0, relay1, relay2), (near0, near1, near2)
    sums, gots = (sum0, sum1, sum2), (got0, got1, got2)
    lows, lasts = (low0, low1, low2), (last0, last1, last2)

    def fill(part, order, left, right, columns, into):
        width = columns[1] - columns[0]
        for z in range(4):
            block = lax.dot_general(
                left[:, z * 256 : (z + 1) * 256],
                right[:, columns[0] : columns[1]],
                (((0,), (0,)), ((), ())),
                preferred_element_type=jnp.float32,
            ).astype(jnp.bfloat16)
            for y in range(4):
                for x in range(4):
                    at = (x, y, z)
                    row = (y * 4 + x) * 16
                    part[at[order[0]], at[order[1]], at[order[2]], :, into : into + width] = block[
                        row : row + 16
                    ]

    first = []

    def stage1(k):
        order = PART_ORDERS[k]
        axis = order[0]
        me = place[axis]
        right, left, far = lax.rem(me + 1, 4), lax.rem(me + 3, 4), lax.rem(me + 2, 4)
        to_right, to_left = peer_along(axis, 1), peer_along(axis, 3)
        part, relay, near = parts[k], relays[k], nears[k]
        lo, hi = pl.ds(0, 2), pl.ds(2, 2)

        def copy(n, source, target, peer):
            return remote(source, target, send1.at[k, n], recv1.at[k, n], peer)

        copies = [
            copy(0, part.at[far, lo], relay.at[0], to_right),
            copy(1, part.at[far, hi], relay.at[1], to_left),
            copy(2, part.at[right, hi], near.at[0, hi], to_right),
            copy(3, part.at[left, lo], near.at[1, lo], to_left),
            copy(4, part.at[right, lo], near.at[0, lo], to_right),
            copy(5, part.at[left, hi], near.at[1, hi], to_left),
        ]
        for n in range(4):
            copies[n].start()
        return copies, (right, left)

    def add_relay(k, copies, sides):
        part, relay = parts[k], relays[k]
        for n in range(2):
            copies[n].wait_recv()
            for j in range(2):
                at = 2 * n + j
                part[sides[n], at] = (
                    part[sides[n], at].astype(jnp.float32) + relay[n, j].astype(jnp.float32)
                ).astype(jnp.bfloat16)
            copies[4 + n].start()

    def stage2(k, copies):
        order = PART_ORDERS[k]
        for n in range(2, 6):
            copies[n].wait_recv()
        me = place[order[0]]
        for j in range(4):
            sums[k][j] = (
                parts[k][me, j].astype(jnp.float32)
                + nears[k][0, j].astype(jnp.float32)
                + nears[k][1, j].astype(jnp.float32)
            ).astype(jnp.bfloat16)
        axis = order[1]
        at = place[axis]
        sends = []
        for d in range(1, 4):
            send = remote(
                sums[k].at[lax.rem(at + d, 4)], gots[k].at[d - 1],
                send2.at[k, d - 1], recv2.at[k, d - 1], peer_along(axis, d),
            )
            send.start()
            sends.append(send)
        return sends

    def stage3(k, copies):
        order = PART_ORDERS[k]
        for copy in copies:
            copy.wait_recv()
        me = place[order[1]]
        total = sums[k][me].astype(jnp.float32)
        for d in range(3):
            total = total + gots[k][d].astype(jnp.float32)
        lows[k][...] = total.astype(jnp.bfloat16)
        axis = order[2]
        at = place[axis]
        sends = []
        for d in range(1, 4):
            send = remote(
                lows[k].at[lax.rem(at + d, 4)], lasts[k].at[d - 1],
                send3.at[k, d - 1], recv3.at[k, d - 1], peer_along(axis, d),
            )
            send.start()
            sends.append(send)
        return sends

    def finish(k, copies):
        for copy in copies:
            copy.wait_recv()
        me = place[PART_ORDERS[k][2]]
        total = lows[k][me].astype(jnp.float32)
        for d in range(3):
            total = total + lasts[k][d].astype(jnp.float32)
        start = sum(PART_COLS[:k])
        fin[:, start : start + PART_COLS[k]] = total

    swaps[0].wait_recv()
    swaps[1].wait_recv()
    split = PART_COLS[0] + PART_COLS[1]
    fill(part0, PART_ORDERS[0], xn2, gq2, (0, PART_COLS[0]), 0)
    first.append(stage1(0))
    fill(part1, PART_ORDERS[1], xn2, gq2, (PART_COLS[0], split), 0)
    first.append(stage1(1))
    swaps[2].wait_recv()
    swaps[3].wait_recv()
    fill(part2, PART_ORDERS[2], xn2, gq2, (split, qh), 0)
    fill(part2, PART_ORDERS[2], ab2, gb2, (0, oh), qh - split)
    first.append(stage1(2))
    for k in range(3):
        add_relay(k, *first[k])
    second = [stage2(k, first[k][0]) for k in range(3)]
    third = [stage3(k, second[k]) for k in range(3)]
    for k in range(3):
        finish(k, third[k])

    keep, give = pl.multiple_of(core * 8, 8), pl.multiple_of((1 - core) * 8, 8)
    end = remote(fin.at[pl.ds(give, 8)], other, fin_send, fin_recv, partner)
    end.start()
    out_q[:, pl.ds(mine_q, qh)] = fin[pl.ds(keep, 8), 0:qh]
    out_o[:, pl.ds(mine_o, oh)] = fin[pl.ds(keep, 8), qh : qh + oh]
    end.wait_recv()
    out_q[:, pl.ds(its_q, qh)] = other[:, 0:qh]
    out_o[:, pl.ds(its_o, oh)] = other[:, qh : qh + oh]
    for copy in swaps + [c for f in first for c in f[0]] + [c for s in second + third for c in s] + [end]:
        copy.wait_send()


def reduce_grads(xn, gq, ab, gb):
    rows, width = xn.shape
    qw, ow = gq.shape[1], gb.shape[1]
    bf, f32 = jnp.bfloat16, jnp.float32
    vmem = pl.BlockSpec(memory_space=pltpu.VMEM)

    def each(*lead):
        return [pltpu.VMEM((*lead, 16, c), bf) for c in PART_COLS]

    return pl.pallas_call(
        grads_kernel,
        name="reduce_grads",
        out_shape=(jax.ShapeDtypeStruct((8, qw), f32), jax.ShapeDtypeStruct((8, ow), f32)),
        in_specs=[vmem] * 4,
        out_specs=(vmem, vmem),
        scratch_shapes=[
            pltpu.VMEM((2 * rows, width), bf),
            pltpu.VMEM((2 * rows, qw // 2), bf),
            pltpu.VMEM((2 * rows, width), bf),
            pltpu.VMEM((2 * rows, ow // 2), bf),
            *each(4, 4, 4), *each(2, 2, 4), *each(2, 4, 4),
            *each(4, 4), *each(3, 4), *each(4), *each(3),
            pltpu.VMEM((16, (qw + ow) // 2), f32),
            pltpu.VMEM((8, (qw + ow) // 2), f32),
            pltpu.SemaphoreType.DMA((4,)), pltpu.SemaphoreType.DMA((4,)),
            pltpu.SemaphoreType.DMA((3, 6)), pltpu.SemaphoreType.DMA((3, 6)),
            pltpu.SemaphoreType.DMA((3, 3)), pltpu.SemaphoreType.DMA((3, 3)),
            pltpu.SemaphoreType.DMA((3, 3)), pltpu.SemaphoreType.DMA((3, 3)),
            pltpu.SemaphoreType.DMA, pltpu.SemaphoreType.DMA,
        ],
        compiler_params=pltpu.CompilerParams(collective_id=5, has_side_effects=True, vmem_limit_bytes=48 << 20),
    )(xn, gq, ab, gb)


CHUNK = 512
LANES = 4096


def project_kernel(
    bytes_ref, w_ref, q_ref, k_ref, v_ref, theirs, wide_rows, xs, ws, acc,
    swap_send, swap_recv, w_sem, p_send, p_recv, q_send, q_recv, f_send, f_recv,
):
    x, y, z, core = coords()
    pair = lax.rem(y, 2)
    partner = device_at(x, y, z, 1 - core)
    across = device_at(x, y + 1 - 2 * pair, z, core)

    def beside(step):
        return device_at(lax.rem(x + step, 4), y, z, core)

    greet([partner, across, beside(1), beside(2), beside(3)])
    copies = []

    def begin(copy):
        copy.start()
        copies.append(copy)
        return copy

    swap = begin(remote(bytes_ref, theirs, swap_send, swap_recv, partner))
    order = [c for n in range(4) for c in (4 + n, n)]
    mine, its = [core * 8 + c for c in range(8)], [(1 - core) * 8 + c for c in range(8)]
    loads = {}
    for c in order:
        for who, g in enumerate((mine[c], its[c])):
            load = pltpu.make_async_copy(
                w_ref.at[:, pl.ds(pl.multiple_of(g * CHUNK, CHUNK), CHUNK), :], ws.at[g], w_sem.at[who, c]
            )
            load.start()
            loads[who, c] = load
    rows = bytes_ref.shape[0]
    lane_tiles = bytes_ref.shape[1] // 128

    def spread(source, side):
        at = pl.ds(pl.multiple_of(side * rows, rows), rows)
        for n in range(lane_tiles):
            wide_rows[n, at] = source[:, n * 128 : (n + 1) * 128].astype(jnp.float32)

    spread(bytes_ref, core)
    acc[...] = jnp.zeros_like(acc)
    swap.wait_recv()
    spread(theirs, 1 - core)

    def entries(n, b):
        return wide_rows[n, pl.ds(b, 48, stride=PATCH), :]

    squares = jnp.zeros((48, 128), jnp.float32)
    for n in range(lane_tiles):
        for b in range(PATCH):
            squares = squares + entries(n, b) * entries(n, b)
    mean = jnp.sum(squares, axis=-1, keepdims=True) / (PATCH * lane_tiles * 128)
    scale = lax.rsqrt(mean + 1e-06)
    for side in (0, 1):

        @pl.when(core == side)
        def _():
            for c in range(8):
                for n in range(4):
                    normed = entries(c % 2 * 4 + n, side * 4 + c // 2) * scale
                    xs[side * 8 + c, pair, x, :, n * 128 : (n + 1) * 128] = normed.astype(jnp.bfloat16)

    right, left = lax.rem(x + 1, 4), lax.rem(x + 3, 4)
    pc, qc = {}, {}
    for n in range(4):
        g = mine[n]

        def copy(k, part, peer):
            return remote(part, part, p_send.at[n, k], p_recv.at[n, k], peer)

        pc[n] = [
            copy(0, xs.at[g, pair, x], across),
            copy(1, xs.at[g, :, x], beside(1)),
            copy(2, xs.at[g, :, x], beside(3)),
            copy(3, xs.at[g, 0, left], beside(1)),
            copy(4, xs.at[g, 1, right], beside(3)),
        ]
        g = mine[4 + n]

        def copy(k, part, peer):
            return remote(part, part, q_send.at[n, k], q_recv.at[n, k], peer)

        qc[n] = [copy(0, xs.at[g, pair], across)] + [copy(d, xs.at[g, pair, x], beside(d)) for d in (1, 2, 3)]
    for n in range(4):
        begin(pc[n][0])
        for d in (2, 1, 3):
            begin(qc[n][d])

    forwards = {
        c: remote(xs.at[mine[c]], xs.at[mine[c]], f_send.at[c], f_recv.at[c], partner) for c in range(8)
    }

    def multiply(who, c):
        loads[who, c].wait()
        g = (mine, its)[who][c]
        block = xs[g].reshape(acc.shape[1], CHUNK)

        def body(j, carry):
            acc[j] += jnp.dot(block, ws[g, j], preferred_element_type=jnp.float32)
            return carry

        lax.fori_loop(0, 3, body, 0)

    def p_turn(n):
        pc[n][0].wait_recv()
        begin(pc[n][1])
        begin(pc[n][2])

    def q_turn(n):
        for d in (1, 2, 3):
            qc[n][d].wait_recv()
        begin(qc[n][0])

    def p_relay(n):
        pc[n][1].wait_recv()
        begin(pc[n][3])
        pc[n][2].wait_recv()
        begin(pc[n][4])

    def p_done(n):
        pc[n][3].wait_recv()
        pc[n][4].wait_recv()
        begin(forwards[n])
        multiply(0, n)

    def q_done(n):
        qc[n][0].wait_recv()
        begin(forwards[4 + n])
        multiply(0, 4 + n)

    def other(c):
        forwards[c].wait_recv()
        multiply(1, c)

    p_turn(0)
    p_turn(1)
    q_turn(0)
    p_turn(2)
    p_turn(3)
    q_turn(1)
    q_turn(2)
    q_turn(3)
    q_done(0)
    p_relay(0)
    other(4)
    p_relay(1)
    p_done(0)
    q_done(1)
    p_relay(2)
    other(0)
    p_done(1)
    p_relay(3)
    other(5)
    other(1)
    q_done(2)
    p_done(2)
    other(6)
    other(2)
    p_done(3)
    q_done(3)
    other(3)
    other(7)

    for j, out in enumerate((q_ref, k_ref, v_ref)):
        for head in range(out.shape[1] // HEAD_DIM):
            at = slice(head * HEAD_DIM, (head + 1) * HEAD_DIM)
            value = acc[j, :, at]
            if j < 2:
                value = rms_norm(value)
            out[:, at] = value.astype(jnp.bfloat16)
    for copy in copies:
        copy.wait_send()


def project_patches(byte_rows, w):
    bf, f32 = jnp.bfloat16, jnp.float32
    vmem = pl.BlockSpec(memory_space=pltpu.VMEM)
    rows, width = byte_rows.shape
    total, cols = 2 * rows // PATCH * 8, w.shape[2]

    def sems(*shape):
        return pltpu.SemaphoreType.DMA(shape)

    return pl.pallas_call(
        project_kernel,
        name="project_patches",
        out_shape=[jax.ShapeDtypeStruct((total, cols), bf)] * 3,
        in_specs=[vmem, pl.BlockSpec(memory_space=pl.ANY)],
        out_specs=[vmem] * 3,
        scratch_shapes=[
            pltpu.VMEM((rows, width), bf),
            pltpu.VMEM((width // 128, 2 * rows, 128), f32),
            pltpu.VMEM((16, 2, 4, 48, CHUNK), bf),
            pltpu.VMEM((16, 3, CHUNK, cols), bf),
            pltpu.VMEM((3, total, cols), f32),
            pltpu.SemaphoreType.DMA, pltpu.SemaphoreType.DMA,
            sems(2, 8), sems(4, 5), sems(4, 5), sems(4, 4), sems(4, 4), sems(8), sems(8),
        ],
        compiler_params=pltpu.CompilerParams(collective_id=1, has_side_effects=True, vmem_limit_bytes=44 << 20),
    )(byte_rows, w)


def attend(
    x, y, z, core, begin, q_ref, k_ref, v_ref, att2, q2, ka, va, acc, tall, back,
    y_send, y_recv, z_send, z_recv, row_send, row_recv, back_send, back_recv, swap_send, swap_recv,
):
    half = lax.div(y, 2)
    partner = device_at(x, y, z, 1 - core)
    opposite = device_at(x, lax.rem(y + 2, 4), z, core)
    rows = q_ref.shape[0]
    mine = pl.ds(pl.multiple_of(half * HEAD_DIM, HEAD_DIM), HEAD_DIM)
    its = pl.ds(pl.multiple_of((1 - half) * HEAD_DIM, HEAD_DIM), HEAD_DIM)

    across = [
        begin(remote(source.at[:, its], target, y_send.at[n], y_recv.at[n], opposite))
        for n, (source, target) in enumerate(
            ((k_ref, ka.at[z, half]), (v_ref, va.at[z, half]), (q_ref, q2.at[half]))
        )
    ]

    def up(d, kind, which):
        block = half if which == 0 else 1 - half
        target = (ka, va)[kind].at[z, block]
        source = (k_ref, v_ref)[kind].at[:, mine] if which == 0 else target
        return remote(
            source, target, z_send.at[d - 1, kind, which], z_recv.at[d - 1, kind, which],
            device_at(x, y, lax.rem(z + d, 4), core),
        )

    lifts = {(d, kind, which): up(d, kind, which) for which in (0, 1) for kind in (0, 1) for d in (1, 3, 2)}
    for (d, kind, which), copy in lifts.items():
        if which == 0:
            pl.when(z + d <= 3)(copy.start)
    ka[z, half] = k_ref[:, mine]
    va[z, half] = v_ref[:, mine]
    q2[half] = q_ref[:, mine]
    for kind in (0, 1):
        across[kind].wait_recv()
        for d in (1, 3, 2):
            pl.when(z + d <= 3)(lifts[d, kind, 1].start)
    across[2].wait_recv()

    tile = 128
    tiles = rows // tile
    scale = 1.0 / math.sqrt(HEAD_DIM)

    def attend_tile(block, n, keys, values, masked, first):
        s = lax.dot_general(
            q2[block, n * tile : (n + 1) * tile], keys, (((1,), (1,)), ((), ())), preferred_element_type=jnp.float32
        )
        e = jnp.exp(s * scale)
        if masked:
            row = n * tile + lax.broadcasted_iota(jnp.int32, e.shape, 0)
            e = jnp.where(lax.broadcasted_iota(jnp.int32, e.shape, 1) <= row, e, 0.0)
        sums = jnp.dot(e.astype(jnp.bfloat16), values, preferred_element_type=jnp.float32)
        at = slice(n * tile, (n + 1) * tile)
        acc[block, at] = sums if first else acc[block, at] + sums

    def with_ones(values):
        return jnp.concatenate([values, jnp.ones_like(values)], axis=1)

    for k in (0, 1):
        keys, values = ka[z, k], with_ones(va[z, k])
        for block in range(k, 2):
            for n in range(tiles):
                attend_tile(block, n, keys, values, block == k, k == 0)

    for d in (1, 3, 2):

        @pl.when(z >= d)
        def _():
            for kind in (0, 1):
                for which in (0, 1):
                    lifts[d, kind, which].wait_recv()
            below = lax.rem(z + 4 - d, 4)

            def body(k, carry):
                keys, values = ka[below, k], with_ones(va[below, k])
                for block in (0, 1):
                    for n in range(tiles):
                        attend_tile(block, n, keys, values, False, False)
                return carry

            lax.fori_loop(0, 2, body, 0)

    for block in (0, 1):
        tall[8 + block * rows : 8 + (block + 1) * rows] = acc[block, :, 0:HEAD_DIM] / acc[block, :, HEAD_DIM:]
    row = remote(
        tall.at[pl.ds(2 * rows, 8)], tall.at[pl.ds(0, 8)], row_send, row_recv,
        device_at(x, y, lax.rem(z + 1, 4), core),
    )
    pl.when(z < 3)(row.start)
    pl.when(z > 0)(row.wait_recv)

    @pl.when(z == 0)
    def _():
        tall[0:8] = jnp.zeros((8, HEAD_DIM), jnp.float32)

    for part in (0, 1):

        @pl.when(half == part)
        def _():
            back[...] = tall[7 + (1 - part) * rows : 7 + (2 - part) * rows].astype(jnp.bfloat16)
            att2[:, part * HEAD_DIM : (part + 1) * HEAD_DIM] = tall[
                7 + part * rows : 7 + (part + 1) * rows
            ].astype(jnp.bfloat16)

    width = 2 * HEAD_DIM
    far_mine = pl.ds(pl.multiple_of(width + half * HEAD_DIM, HEAD_DIM), HEAD_DIM)
    far_its = pl.ds(pl.multiple_of(width + (1 - half) * HEAD_DIM, HEAD_DIM), HEAD_DIM)
    returned = begin(remote(back, att2.at[:, mine], back_send, back_recv, opposite))
    near = begin(remote(att2.at[:, mine], att2.at[:, far_mine], swap_send.at[0], swap_recv.at[0], partner))
    returned.wait_recv()
    last = begin(remote(att2.at[:, its], att2.at[:, far_its], swap_send.at[1], swap_recv.at[1], partner))
    near.wait_recv()
    last.wait_recv()
    pl.when(z < 3)(row.wait_send)
    for (d, kind, which), copy in lifts.items():
        pl.when(z + d <= 3)(copy.wait_send)


def out_kernel(
    q_ref, k_ref, v_ref, w_ref, out_ref, q2, ka, va, acc, tall, back, att2, w2, pbuf, relay, near, psum, pgot, qbuf, qgot, qsum, qlast, fin, other,
    w_sem, pair_send, pair_recv, p_send, p_recv, q_send, q_recv, fin_send, fin_recv,
    *att_sems,
):
    x, y, z, core = coords()
    pair = lax.rem(y, 2)
    partner = device_at(x, y, z, 1 - core)
    across = device_at(x, y + 1 - 2 * pair, z, core)

    def beside(step):
        return device_at(lax.rem(x + step, 4), y, z, core)

    greet(
        [partner, across, beside(1), beside(2), beside(3), device_at(x, lax.rem(y + 2, 4), z, core)]
        + [device_at(x, y, lax.rem(z + d, 4), core) for d in (1, 2, 3)]
    )
    depth = q_ref.shape[1]
    copies = []

    def begin(copy):
        copy.start()
        copies.append(copy)
        return copy

    order = [c for n in range(4) for c in (4 + n, n)]
    theirs, mine = {}, {}
    for c in order:
        into = pl.ds(c * CHUNK, CHUNK)
        give = pl.ds(pl.multiple_of((1 - core) * LANES + c * CHUNK, CHUNK), CHUNK)
        keep = pl.ds(pl.multiple_of(core * LANES + c * CHUNK, CHUNK), CHUNK)
        theirs[c] = begin(
            remote(w_ref.at[:, give], w2.at[pl.ds(depth, depth), into], pair_send.at[c], pair_recv.at[c], partner)
        )
        mine[c] = pltpu.make_async_copy(w_ref.at[:, keep], w2.at[pl.ds(0, depth), into], w_sem.at[c])
        mine[c].start()
    attend(
        x, y, z, core, begin, q_ref, k_ref, v_ref, att2, q2, ka, va, acc, tall, back, *att_sems
    )

    right, left, far = lax.rem(x + 1, 4), lax.rem(x + 3, 4), lax.rem(x + 2, 4)
    pcopies, qcopies = {}, {}
    for c in order:
        mine[c].wait()
        theirs[c].wait_recv()
        block = jnp.dot(
            att2[...], w2[:, c * CHUNK : (c + 1) * CHUNK], preferred_element_type=jnp.float32
        ).astype(jnp.bfloat16)
        for row in range(8):
            piece = block[row * 48 : row * 48 + 48]
            if c < 4:
                pbuf[c, row % 4, row // 4] = piece
            else:
                qbuf[c - 4, row // 4, row % 4] = piece
        if c < 4:

            def copy(k, source, target, peer):
                return remote(source, target, p_send.at[c, k], p_recv.at[c, k], peer)

            pcopies[c] = [
                copy(0, pbuf.at[c, far, 0], relay.at[c, 0], beside(1)),
                copy(1, pbuf.at[c, far, 1], relay.at[c, 1], beside(3)),
                copy(2, pbuf.at[c, right, 1], near.at[c, 0, 1], beside(1)),
                copy(3, pbuf.at[c, left, 0], near.at[c, 1, 0], beside(3)),
                copy(4, pbuf.at[c, right, 0], near.at[c, 0, 0], beside(1)),
                copy(5, pbuf.at[c, left, 1], near.at[c, 1, 1], beside(3)),
                copy(6, psum.at[c, 1 - pair], pgot.at[c], across),
            ]
            for k in range(4):
                begin(pcopies[c][k])
        else:
            n = c - 4
            qcopies[n] = [remote(qbuf.at[n, 1 - pair], qgot.at[n], q_send.at[n, 0], q_recv.at[n, 0], across)] + [
                remote(qsum.at[n, lax.rem(x + d, 4)], qlast.at[n, d - 1], q_send.at[n, d], q_recv.at[n, d], beside(d))
                for d in (1, 2, 3)
            ]
            begin(qcopies[n][0])

    def wide(value):
        return value.astype(jnp.float32)

    def p_relay(n):
        for k, side in ((0, right), (1, left)):
            pcopies[n][k].wait_recv()
            pbuf[n, side, k] = (wide(pbuf[n, side, k]) + wide(relay[n, k])).astype(jnp.bfloat16)
            begin(pcopies[n][4 + k])

    def p_across(n):
        for k in range(2, 6):
            pcopies[n][k].wait_recv()
        for k in range(2):
            psum[n, k] = (wide(pbuf[n, x, k]) + wide(near[n, 0, k]) + wide(near[n, 1, k])).astype(jnp.bfloat16)
        begin(pcopies[n][6])

    def p_end(n):
        pcopies[n][6].wait_recv()
        fin[:, n * CHUNK : (n + 1) * CHUNK] = wide(psum[n, pair]) + wide(pgot[n])

    def q_beside(n):
        qcopies[n][0].wait_recv()
        for k in range(4):
            qsum[n, k] = (wide(qbuf[n, pair, k]) + wide(qgot[n, k])).astype(jnp.bfloat16)
        for k in (2, 1, 3):
            begin(qcopies[n][k])

    def q_end(n):
        for k in (1, 2, 3):
            qcopies[n][k].wait_recv()
        total = wide(qsum[n, x])
        for k in range(3):
            total = total + wide(qlast[n, k])
        fin[:, (4 + n) * CHUNK : (5 + n) * CHUNK] = total

    p_relay(0)
    p_relay(1)
    q_beside(0)
    p_relay(2)
    p_relay(3)
    q_beside(1)
    p_across(0)
    p_across(1)
    q_beside(2)
    p_across(2)
    p_across(3)
    q_end(0)
    q_end(1)
    q_beside(3)
    for n in range(4):
        p_end(n)
    q_end(2)
    q_end(3)

    keep, give = pl.multiple_of(core * 24, 8), pl.multiple_of((1 - core) * 24, 8)
    end = begin(remote(fin.at[pl.ds(give, 24)], other, fin_send, fin_recv, partner))
    for b in range(4):
        out_ref[:, core * 4 + b, :] = fin[pl.ds(keep, 24), b * 1024 : b * 1024 + 1024]
    end.wait_recv()
    for b in range(4):
        out_ref[:, (1 - core) * 4 + b, :] = other[:, b * 1024 : b * 1024 + 1024]
    for copy in copies:
        copy.wait_send()


def attend_and_project(q, k, v, w):
    rows, depth = q.shape
    bf, f32 = jnp.bfloat16, jnp.float32
    vmem = pl.BlockSpec(memory_space=pltpu.VMEM)

    def units(*lead):
        return pltpu.VMEM((*lead, 48, CHUNK), bf)

    def sems(*shape):
        return pltpu.SemaphoreType.DMA(shape)

    return pl.pallas_call(
        out_kernel,
        name="attend_out",
        out_shape=jax.ShapeDtypeStruct((24, 8, 1024), f32),
        in_specs=[vmem] * 3 + [pl.BlockSpec(memory_space=pl.ANY)],
        out_specs=vmem,
        scratch_shapes=[
            pltpu.VMEM((2, rows, HEAD_DIM), bf),
            pltpu.VMEM((4, 2, rows, HEAD_DIM), bf),
            pltpu.VMEM((4, 2, rows, HEAD_DIM), bf),
            pltpu.VMEM((2, rows, 2 * HEAD_DIM), f32),
            pltpu.VMEM((8 + 2 * rows, HEAD_DIM), f32),
            pltpu.VMEM((rows, HEAD_DIM), bf),
            pltpu.VMEM((rows, 2 * depth), bf),
            pltpu.VMEM((2 * depth, LANES), bf),
            units(4, 4, 2), units(4, 2), units(4, 2, 2), units(4, 2), units(4),
            units(4, 2, 4), units(4, 4), units(4, 4), units(4, 3),
            pltpu.VMEM((48, LANES), f32),
            pltpu.VMEM((24, LANES), f32),
            sems(8), sems(8), sems(8), sems(4, 7), sems(4, 7), sems(4, 4), sems(4, 4),
            pltpu.SemaphoreType.DMA, pltpu.SemaphoreType.DMA,
            sems(3), sems(3), sems(3, 2, 2), sems(3, 2, 2),
            pltpu.SemaphoreType.DMA, pltpu.SemaphoreType.DMA,
            pltpu.SemaphoreType.DMA, pltpu.SemaphoreType.DMA, sems(2), sems(2),
        ],
        compiler_params=pltpu.CompilerParams(collective_id=3, has_side_effects=True, vmem_limit_bytes=40 << 20),
    )(q, k, v, w)


def rms_norm(values):
    return values * lax.rsqrt(jnp.mean(values * values, axis=-1, keepdims=True) + 1e-06)


def local_core(qkv_rows):
    total = qkv_rows.shape[0]
    groups = total // PATCH
    width = qkv_rows.shape[1] // 3
    parts = qkv_rows.reshape(groups, PATCH, 3, LOCAL_HEADS, LOCAL_HEAD_DIM)
    queries = rms_norm(parts[:, :, 0])
    keys_all = rms_norm(parts[:, :, 1])
    values = parts[:, :, 2]
    scores = jnp.einsum("npha,nqha->nhpq", queries, keys_all) / math.sqrt(LOCAL_HEAD_DIM)
    causal = jnp.arange(PATCH)[:, None] >= jnp.arange(PATCH)[None, :]
    weights = jnp.where(causal[None, None], jnp.exp(scores), 0.0)
    numerator = jnp.einsum("nhpq,nqha->npha", weights, values)
    denominator = jnp.sum(weights, axis=-1).transpose(0, 2, 1)[..., None]
    return (numerator / denominator).reshape(total, width)


def local_pass(state, local_qkv, local_out, cotangent):
    layer = 0
    normed = rms_norm(state).astype(jnp.bfloat16)
    qkv_rows = jnp.dot(normed, local_qkv[layer], preferred_element_type=jnp.float32)
    core, core_back = jax.vjp(local_core, qkv_rows)
    attended = core.astype(jnp.bfloat16)
    saved = [(state, normed, core_back, attended)]
    state = state + jnp.dot(attended, local_out[layer], preferred_element_type=jnp.float32)
    hidden = state.astype(jnp.bfloat16)
    grad_state = cotangent.astype(jnp.float32)
    layer = 0
    before, normed, core_back, attended = saved[layer]
    grad_round = grad_state.astype(jnp.bfloat16)
    grad_core = jnp.dot(grad_round, local_out[layer].T, preferred_element_type=jnp.float32)
    grad_rows = core_back(grad_core)[0].astype(jnp.bfloat16)
    return hidden, normed, grad_rows, attended, grad_round


def per_device(byte_embeds, local_embeds, global_qkv, global_out, local_qkv, local_out, cotangent):
    byte_count = byte_embeds.shape[0]
    flat = project_patches(byte_embeds, global_qkv)
    context = attend_and_project(*flat, global_out).reshape(byte_count, byte_embeds.shape[1])
    context = context.astype(jnp.bfloat16)
    state = local_embeds.astype(jnp.float32) + context.astype(jnp.float32)
    hidden, *factors = local_pass(state, local_qkv, local_out, cotangent)
    grad_qkv, grad_out = reduce_grads(*factors)
    return (hidden, grad_qkv[None], grad_out[None])


def solution(mesh):
    in_specs = (
        P(("ctx", "tp"), None),
        P(("ctx", "tp"), None),
        P(None, None, "tp"),
        P("tp", None),
        P(),
        P(),
        P(("ctx", "tp"), None),
    )
    out_specs = (P(("ctx", "tp"), None), P(None, ("ctx", "tp"), None), P(None, ("ctx", "tp"), None))
    return jax.shard_map(
        per_device, mesh=mesh, in_specs=in_specs, out_specs=out_specs, check_vma=False
    )
```

```python
import math

import jax
import jax.numpy as jnp
from jax import lax
from jax.experimental import pallas as pl
from jax.experimental.pallas import tpu as pltpu
from jax.sharding import PartitionSpec as P

PATCH = 8
HEAD_DIM = 128
LOCAL_HEADS = 8
LOCAL_HEAD_DIM = 128


MESH = pl.DeviceIdType.MESH


def coords():
    ctx, tp = lax.axis_index("ctx"), lax.axis_index("tp")
    x, core = lax.rem(lax.div(tp, 2), 4), lax.rem(tp, 2)
    y = lax.rem(ctx, 2) * 2 + lax.div(tp, 8)
    return x, y, lax.div(ctx, 2), core


def device_at(x, y, z, core):
    return {"ctx": z * 2 + lax.div(y, 2), "tp": lax.rem(y, 2) * 8 + x * 2 + core}


def greet(peers):
    barrier = pltpu.get_barrier_semaphore()
    for peer in peers:
        pl.semaphore_signal(barrier, inc=1, device_id=peer, device_id_type=MESH)
    pl.semaphore_wait(barrier, len(peers))


def remote(source, target, send_sem, recv_sem, peer):
    return pltpu.make_async_remote_copy(
        src_ref=source,
        dst_ref=target,
        send_sem=send_sem,
        recv_sem=recv_sem,
        device_id=peer,
        device_id_type=MESH,
    )


def rms_norm(values):
    return values * lax.rsqrt(jnp.mean(values * values, axis=-1, keepdims=True) + 1e-06)


CHUNK = 512
LANES = 4096


def project_kernel(
    bytes_ref, w_ref, q_ref, k_ref, v_ref, theirs, wide_rows, xs, ws, acc,
    swap_send, swap_recv, w_sem, p_send, p_recv, q_send, q_recv, f_send, f_recv,
):
    x, y, z, core = coords()
    pair = lax.rem(y, 2)
    partner = device_at(x, y, z, 1 - core)
    across = device_at(x, y + 1 - 2 * pair, z, core)

    def beside(step):
        return device_at(lax.rem(x + step, 4), y, z, core)

    greet([partner, across, beside(1), beside(2), beside(3)])
    copies = []

    def begin(copy):
        copy.start()
        copies.append(copy)
        return copy

    swap = begin(remote(bytes_ref, theirs, swap_send, swap_recv, partner))
    order = [c for n in range(4) for c in (4 + n, n)]
    mine, its = [core * 8 + c for c in range(8)], [(1 - core) * 8 + c for c in range(8)]
    loads = {}
    for c in order:
        for who, g in enumerate((mine[c], its[c])):
            load = pltpu.make_async_copy(
                w_ref.at[:, pl.ds(pl.multiple_of(g * CHUNK, CHUNK), CHUNK), :], ws.at[g], w_sem.at[who, c]
            )
            load.start()
            loads[who, c] = load
    rows = bytes_ref.shape[0]
    lane_tiles = bytes_ref.shape[1] // 128

    def spread(source, side):
        at = pl.ds(pl.multiple_of(side * rows, rows), rows)
        for n in range(lane_tiles):
            wide_rows[n, at] = source[:, n * 128 : (n + 1) * 128].astype(jnp.float32)

    spread(bytes_ref, core)
    acc[...] = jnp.zeros_like(acc)
    swap.wait_recv()
    spread(theirs, 1 - core)

    def entries(n, b):
        return wide_rows[n, pl.ds(b, 48, stride=PATCH), :]

    squares = jnp.zeros((48, 128), jnp.float32)
    for n in range(lane_tiles):
        for b in range(PATCH):
            squares = squares + entries(n, b) * entries(n, b)
    mean = jnp.sum(squares, axis=-1, keepdims=True) / (PATCH * lane_tiles * 128)
    scale = lax.rsqrt(mean + 1e-06)
    for side in (0, 1):

        @pl.when(core == side)
        def _():
            for c in range(8):
                for n in range(4):
                    normed = entries(c % 2 * 4 + n, side * 4 + c // 2) * scale
                    xs[side * 8 + c, pair, x, :, n * 128 : (n + 1) * 128] = normed.astype(jnp.bfloat16)

    right, left = lax.rem(x + 1, 4), lax.rem(x + 3, 4)
    pc, qc = {}, {}
    for n in range(4):
        g = mine[n]

        def copy(k, part, peer):
            return remote(part, part, p_send.at[n, k], p_recv.at[n, k], peer)

        pc[n] = [
            copy(0, xs.at[g, pair, x], across),
            copy(1, xs.at[g, :, x], beside(1)),
            copy(2, xs.at[g, :, x], beside(3)),
            copy(3, xs.at[g, 0, left], beside(1)),
            copy(4, xs.at[g, 1, right], beside(3)),
        ]
        g = mine[4 + n]

        def copy(k, part, peer):
            return remote(part, part, q_send.at[n, k], q_recv.at[n, k], peer)

        qc[n] = [copy(0, xs.at[g, pair], across)] + [copy(d, xs.at[g, pair, x], beside(d)) for d in (1, 2, 3)]
    for n in range(4):
        begin(pc[n][0])
        for d in (2, 1, 3):
            begin(qc[n][d])

    forwards = {
        c: remote(xs.at[mine[c]], xs.at[mine[c]], f_send.at[c], f_recv.at[c], partner) for c in range(8)
    }

    def multiply(who, c):
        loads[who, c].wait()
        g = (mine, its)[who][c]
        block = xs[g].reshape(acc.shape[1], CHUNK)

        def body(j, carry):
            acc[j] += jnp.dot(block, ws[g, j], preferred_element_type=jnp.float32)
            return carry

        lax.fori_loop(0, 3, body, 0)

    def p_turn(n):
        pc[n][0].wait_recv()
        begin(pc[n][1])
        begin(pc[n][2])

    def q_turn(n):
        for d in (1, 2, 3):
            qc[n][d].wait_recv()
        begin(qc[n][0])

    def p_relay(n):
        pc[n][1].wait_recv()
        begin(pc[n][3])
        pc[n][2].wait_recv()
        begin(pc[n][4])

    def p_done(n):
        pc[n][3].wait_recv()
        pc[n][4].wait_recv()
        begin(forwards[n])
        multiply(0, n)

    def q_done(n):
        qc[n][0].wait_recv()
        begin(forwards[4 + n])
        multiply(0, 4 + n)

    def other(c):
        forwards[c].wait_recv()
        multiply(1, c)

    p_turn(0)
    p_turn(1)
    q_turn(0)
    p_turn(2)
    p_turn(3)
    q_turn(1)
    q_turn(2)
    q_turn(3)
    q_done(0)
    p_relay(0)
    other(4)
    p_relay(1)
    p_done(0)
    q_done(1)
    p_relay(2)
    other(0)
    p_done(1)
    p_relay(3)
    other(5)
    other(1)
    q_done(2)
    p_done(2)
    other(6)
    other(2)
    p_done(3)
    q_done(3)
    other(3)
    other(7)

    for j, out in enumerate((q_ref, k_ref, v_ref)):
        for head in range(out.shape[1] // HEAD_DIM):
            at = slice(head * HEAD_DIM, (head + 1) * HEAD_DIM)
            value = acc[j, :, at]
            if j < 2:
                value = rms_norm(value)
            out[:, at] = value.astype(jnp.bfloat16)
    for copy in copies:
        copy.wait_send()


def project_patches(byte_rows, w):
    bf, f32 = jnp.bfloat16, jnp.float32
    vmem = pl.BlockSpec(memory_space=pltpu.VMEM)
    rows, width = byte_rows.shape
    total, cols = 2 * rows // PATCH * 8, w.shape[2]

    def sems(*shape):
        return pltpu.SemaphoreType.DMA(shape)

    return pl.pallas_call(
        project_kernel,
        name="project_patches",
        out_shape=[jax.ShapeDtypeStruct((total, cols), bf)] * 3,
        in_specs=[vmem, pl.BlockSpec(memory_space=pl.ANY)],
        out_specs=[vmem] * 3,
        scratch_shapes=[
            pltpu.VMEM((rows, width), bf),
            pltpu.VMEM((width // 128, 2 * rows, 128), f32),
            pltpu.VMEM((16, 2, 4, 48, CHUNK), bf),
            pltpu.VMEM((16, 3, CHUNK, cols), bf),
            pltpu.VMEM((3, total, cols), f32),
            pltpu.SemaphoreType.DMA, pltpu.SemaphoreType.DMA,
            sems(2, 8), sems(4, 5), sems(4, 5), sems(4, 4), sems(4, 4), sems(8), sems(8),
        ],
        compiler_params=pltpu.CompilerParams(collective_id=1, has_side_effects=True, vmem_limit_bytes=44 << 20),
    )(byte_rows, w)


def attend(
    x, y, z, core, begin, q_ref, k_ref, v_ref, att2, q2, ka, va, acc, tall, back,
    y_send, y_recv, z_send, z_recv, row_send, row_recv, back_send, back_recv, swap_send, swap_recv,
):
    half = lax.div(y, 2)
    partner = device_at(x, y, z, 1 - core)
    opposite = device_at(x, lax.rem(y + 2, 4), z, core)
    rows = q_ref.shape[0]
    mine = pl.ds(pl.multiple_of(half * HEAD_DIM, HEAD_DIM), HEAD_DIM)
    its = pl.ds(pl.multiple_of((1 - half) * HEAD_DIM, HEAD_DIM), HEAD_DIM)

    across = [
        begin(remote(source.at[:, its], target, y_send.at[n], y_recv.at[n], opposite))
        for n, (source, target) in enumerate(
            ((k_ref, ka.at[z, half]), (v_ref, va.at[z, half]), (q_ref, q2.at[half]))
        )
    ]

    def up(d, kind, which):
        block = half if which == 0 else 1 - half
        target = (ka, va)[kind].at[z, block]
        source = (k_ref, v_ref)[kind].at[:, mine] if which == 0 else target
        return remote(
            source, target, z_send.at[d - 1, kind, which], z_recv.at[d - 1, kind, which],
            device_at(x, y, lax.rem(z + d, 4), core),
        )

    lifts = {(d, kind, which): up(d, kind, which) for which in (0, 1) for kind in (0, 1) for d in (1, 3, 2)}
    for (d, kind, which), copy in lifts.items():
        if which == 0:
            pl.when(z + d <= 3)(copy.start)
    ka[z, half] = k_ref[:, mine]
    va[z, half] = v_ref[:, mine]
    q2[half] = q_ref[:, mine]
    for kind in (0, 1):
        across[kind].wait_recv()
        for d in (1, 3, 2):
            pl.when(z + d <= 3)(lifts[d, kind, 1].start)
    across[2].wait_recv()

    tile = 128
    tiles = rows // tile
    scale = 1.0 / math.sqrt(HEAD_DIM)

    def attend_tile(block, n, keys, values, masked, first):
        s = lax.dot_general(
            q2[block, n * tile : (n + 1) * tile], keys, (((1,), (1,)), ((), ())), preferred_element_type=jnp.float32
        )
        e = jnp.exp(s * scale)
        if masked:
            row = n * tile + lax.broadcasted_iota(jnp.int32, e.shape, 0)
            e = jnp.where(lax.broadcasted_iota(jnp.int32, e.shape, 1) <= row, e, 0.0)
        sums = jnp.dot(e.astype(jnp.bfloat16), values, preferred_element_type=jnp.float32)
        at = slice(n * tile, (n + 1) * tile)
        acc[block, at] = sums if first else acc[block, at] + sums

    def with_ones(values):
        return jnp.concatenate([values, jnp.ones_like(values)], axis=1)

    for k in (0, 1):
        keys, values = ka[z, k], with_ones(va[z, k])
        for block in range(k, 2):
            for n in range(tiles):
                attend_tile(block, n, keys, values, block == k, k == 0)

    for d in (1, 3, 2):

        @pl.when(z >= d)
        def _():
            for kind in (0, 1):
                for which in (0, 1):
                    lifts[d, kind, which].wait_recv()
            below = lax.rem(z + 4 - d, 4)

            def body(k, carry):
                keys, values = ka[below, k], with_ones(va[below, k])
                for block in (0, 1):
                    for n in range(tiles):
                        attend_tile(block, n, keys, values, False, False)
                return carry

            lax.fori_loop(0, 2, body, 0)

    for block in (0, 1):
        tall[8 + block * rows : 8 + (block + 1) * rows] = acc[block, :, 0:HEAD_DIM] / acc[block, :, HEAD_DIM:]
    row = remote(
        tall.at[pl.ds(2 * rows, 8)], tall.at[pl.ds(0, 8)], row_send, row_recv,
        device_at(x, y, lax.rem(z + 1, 4), core),
    )
    pl.when(z < 3)(row.start)
    pl.when(z > 0)(row.wait_recv)

    @pl.when(z == 0)
    def _():
        tall[0:8] = jnp.zeros((8, HEAD_DIM), jnp.float32)

    for part in (0, 1):

        @pl.when(half == part)
        def _():
            back[...] = tall[7 + (1 - part) * rows : 7 + (2 - part) * rows].astype(jnp.bfloat16)
            att2[:, part * HEAD_DIM : (part + 1) * HEAD_DIM] = tall[
                7 + part * rows : 7 + (part + 1) * rows
            ].astype(jnp.bfloat16)

    width = 2 * HEAD_DIM
    far_mine = pl.ds(pl.multiple_of(width + half * HEAD_DIM, HEAD_DIM), HEAD_DIM)
    far_its = pl.ds(pl.multiple_of(width + (1 - half) * HEAD_DIM, HEAD_DIM), HEAD_DIM)
    returned = begin(remote(back, att2.at[:, mine], back_send, back_recv, opposite))
    near = begin(remote(att2.at[:, mine], att2.at[:, far_mine], swap_send.at[0], swap_recv.at[0], partner))
    returned.wait_recv()
    last = begin(remote(att2.at[:, its], att2.at[:, far_its], swap_send.at[1], swap_recv.at[1], partner))
    near.wait_recv()
    last.wait_recv()
    pl.when(z < 3)(row.wait_send)
    for (d, kind, which), copy in lifts.items():
        pl.when(z + d <= 3)(copy.wait_send)


def out_kernel(
    q_ref, k_ref, v_ref, w_ref, out_ref, q2, ka, va, acc, tall, back, att2, w2, pbuf, relay, near, psum, pgot, qbuf, qgot, qsum, qlast, fin, other,
    w_sem, pair_send, pair_recv, p_send, p_recv, q_send, q_recv, fin_send, fin_recv,
    *att_sems,
):
    x, y, z, core = coords()
    pair = lax.rem(y, 2)
    partner = device_at(x, y, z, 1 - core)
    across = device_at(x, y + 1 - 2 * pair, z, core)

    def beside(step):
        return device_at(lax.rem(x + step, 4), y, z, core)

    greet(
        [partner, across, beside(1), beside(2), beside(3), device_at(x, lax.rem(y + 2, 4), z, core)]
        + [device_at(x, y, lax.rem(z + d, 4), core) for d in (1, 2, 3)]
    )
    depth = q_ref.shape[1]
    copies = []

    def begin(copy):
        copy.start()
        copies.append(copy)
        return copy

    order = [c for n in range(4) for c in (4 + n, n)]
    theirs, mine = {}, {}
    for c in order:
        into = pl.ds(c * CHUNK, CHUNK)
        give = pl.ds(pl.multiple_of((1 - core) * LANES + c * CHUNK, CHUNK), CHUNK)
        keep = pl.ds(pl.multiple_of(core * LANES + c * CHUNK, CHUNK), CHUNK)
        theirs[c] = begin(
            remote(w_ref.at[:, give], w2.at[pl.ds(depth, depth), into], pair_send.at[c], pair_recv.at[c], partner)
        )
        mine[c] = pltpu.make_async_copy(w_ref.at[:, keep], w2.at[pl.ds(0, depth), into], w_sem.at[c])
        mine[c].start()
    attend(
        x, y, z, core, begin, q_ref, k_ref, v_ref, att2, q2, ka, va, acc, tall, back, *att_sems
    )

    right, left, far = lax.rem(x + 1, 4), lax.rem(x + 3, 4), lax.rem(x + 2, 4)
    pcopies, qcopies = {}, {}
    for c in order:
        mine[c].wait()
        theirs[c].wait_recv()
        block = jnp.dot(
            att2[...], w2[:, c * CHUNK : (c + 1) * CHUNK], preferred_element_type=jnp.float32
        ).astype(jnp.bfloat16)
        for row in range(8):
            piece = block[row * 48 : row * 48 + 48]
            if c < 4:
                pbuf[c, row % 4, row // 4] = piece
            else:
                qbuf[c - 4, row // 4, row % 4] = piece
        if c < 4:

            def copy(k, source, target, peer):
                return remote(source, target, p_send.at[c, k], p_recv.at[c, k], peer)

            pcopies[c] = [
                copy(0, pbuf.at[c, far, 0], relay.at[c, 0], beside(1)),
                copy(1, pbuf.at[c, far, 1], relay.at[c, 1], beside(3)),
                copy(2, pbuf.at[c, right, 1], near.at[c, 0, 1], beside(1)),
                copy(3, pbuf.at[c, left, 0], near.at[c, 1, 0], beside(3)),
                copy(4, pbuf.at[c, right, 0], near.at[c, 0, 0], beside(1)),
                copy(5, pbuf.at[c, left, 1], near.at[c, 1, 1], beside(3)),
                copy(6, psum.at[c, 1 - pair], pgot.at[c], across),
            ]
            for k in range(4):
                begin(pcopies[c][k])
        else:
            n = c - 4
            qcopies[n] = [remote(qbuf.at[n, 1 - pair], qgot.at[n], q_send.at[n, 0], q_recv.at[n, 0], across)] + [
                remote(qsum.at[n, lax.rem(x + d, 4)], qlast.at[n, d - 1], q_send.at[n, d], q_recv.at[n, d], beside(d))
                for d in (1, 2, 3)
            ]
            begin(qcopies[n][0])

    def wide(value):
        return value.astype(jnp.float32)

    def p_relay(n):
        for k, side in ((0, right), (1, left)):
            pcopies[n][k].wait_recv()
            pbuf[n, side, k] = (wide(pbuf[n, side, k]) + wide(relay[n, k])).astype(jnp.bfloat16)
            begin(pcopies[n][4 + k])

    def p_across(n):
        for k in range(2, 6):
            pcopies[n][k].wait_recv()
        for k in range(2):
            psum[n, k] = (wide(pbuf[n, x, k]) + wide(near[n, 0, k]) + wide(near[n, 1, k])).astype(jnp.bfloat16)
        begin(pcopies[n][6])

    def p_end(n):
        pcopies[n][6].wait_recv()
        fin[:, n * CHUNK : (n + 1) * CHUNK] = wide(psum[n, pair]) + wide(pgot[n])

    def q_beside(n):
        qcopies[n][0].wait_recv()
        for k in range(4):
            qsum[n, k] = (wide(qbuf[n, pair, k]) + wide(qgot[n, k])).astype(jnp.bfloat16)
        for k in (2, 1, 3):
            begin(qcopies[n][k])

    def q_end(n):
        for k in (1, 2, 3):
            qcopies[n][k].wait_recv()
        total = wide(qsum[n, x])
        for k in range(3):
            total = total + wide(qlast[n, k])
        fin[:, (4 + n) * CHUNK : (5 + n) * CHUNK] = total

    p_relay(0)
    p_relay(1)
    q_beside(0)
    p_relay(2)
    p_relay(3)
    q_beside(1)
    p_across(0)
    p_across(1)
    q_beside(2)
    p_across(2)
    p_across(3)
    q_end(0)
    q_end(1)
    q_beside(3)
    for n in range(4):
        p_end(n)
    q_end(2)
    q_end(3)

    keep, give = pl.multiple_of(core * 24, 8), pl.multiple_of((1 - core) * 24, 8)
    end = begin(remote(fin.at[pl.ds(give, 24)], other, fin_send, fin_recv, partner))
    for b in range(4):
        out_ref[:, core * 4 + b, :] = fin[pl.ds(keep, 24), b * 1024 : b * 1024 + 1024]
    end.wait_recv()
    for b in range(4):
        out_ref[:, (1 - core) * 4 + b, :] = other[:, b * 1024 : b * 1024 + 1024]
    for copy in copies:
        copy.wait_send()


def attend_and_project(q, k, v, w):
    rows, depth = q.shape
    bf, f32 = jnp.bfloat16, jnp.float32
    vmem = pl.BlockSpec(memory_space=pltpu.VMEM)

    def units(*lead):
        return pltpu.VMEM((*lead, 48, CHUNK), bf)

    def sems(*shape):
        return pltpu.SemaphoreType.DMA(shape)

    return pl.pallas_call(
        out_kernel,
        name="attend_out",
        out_shape=jax.ShapeDtypeStruct((24, 8, 1024), f32),
        in_specs=[vmem] * 3 + [pl.BlockSpec(memory_space=pl.ANY)],
        out_specs=vmem,
        scratch_shapes=[
            pltpu.VMEM((2, rows, HEAD_DIM), bf),
            pltpu.VMEM((4, 2, rows, HEAD_DIM), bf),
            pltpu.VMEM((4, 2, rows, HEAD_DIM), bf),
            pltpu.VMEM((2, rows, 2 * HEAD_DIM), f32),
            pltpu.VMEM((8 + 2 * rows, HEAD_DIM), f32),
            pltpu.VMEM((rows, HEAD_DIM), bf),
            pltpu.VMEM((rows, 2 * depth), bf),
            pltpu.VMEM((2 * depth, LANES), bf),
            units(4, 4, 2), units(4, 2), units(4, 2, 2), units(4, 2), units(4),
            units(4, 2, 4), units(4, 4), units(4, 4), units(4, 3),
            pltpu.VMEM((48, LANES), f32),
            pltpu.VMEM((24, LANES), f32),
            sems(8), sems(8), sems(8), sems(4, 7), sems(4, 7), sems(4, 4), sems(4, 4),
            pltpu.SemaphoreType.DMA, pltpu.SemaphoreType.DMA,
            sems(3), sems(3), sems(3, 2, 2), sems(3, 2, 2),
            pltpu.SemaphoreType.DMA, pltpu.SemaphoreType.DMA,
            pltpu.SemaphoreType.DMA, pltpu.SemaphoreType.DMA, sems(2), sems(2),
        ],
        compiler_params=pltpu.CompilerParams(collective_id=3, has_side_effects=True, vmem_limit_bytes=40 << 20),
    )(q, k, v, w)


PART_COLS = (640, 640, 768)
PART_ORDERS = ((0, 1, 2), (1, 2, 0), (2, 0, 1))


def rms_scale(values):
    return lax.rsqrt(jnp.mean(values * values, axis=-1, keepdims=True) + 1e-06)


def cross(left, right, left_axis, right_axis):
    return lax.dot_general(
        left, right, (((left_axis,), (right_axis,)), ((), ())), preferred_element_type=jnp.float32
    )


SPAN = 96


def local_head(h, first, inside, qkv, gcore, gq, ab):
    rows = slice(first, first + SPAN)
    bf = jnp.bfloat16
    width = gcore.shape[1]
    at = [pl.ds(pl.multiple_of(n * width + h * LOCAL_HEAD_DIM, LOCAL_HEAD_DIM), LOCAL_HEAD_DIM) for n in range(3)]
    q, k, v = (qkv[rows, part] for part in at)
    q_scale, k_scale = rms_scale(q), rms_scale(k)
    qn, kn = q * q_scale, k * k_scale
    qb, kb, vb = qn.astype(bf), kn.astype(bf), v.astype(bf)
    scale = 1.0 / math.sqrt(LOCAL_HEAD_DIM)
    e = jnp.where(inside, jnp.exp(cross(qb, kb, 1, 1) * scale), 0.0)
    p = e / jnp.sum(e, axis=-1, keepdims=True)
    pb = p.astype(bf)
    ab[rows, at[0]] = cross(pb, vb, 1, 0).astype(bf)
    back = gcore[rows, at[0]].astype(bf)
    dp = cross(back, vb, 1, 1)
    ds = (p * (dp - jnp.sum(p * dp, axis=-1, keepdims=True)) * scale).astype(bf)

    def through_rms(grad, normed, factor):
        return (factor * (grad - normed * jnp.mean(grad * normed, axis=-1, keepdims=True))).astype(bf)

    gq[rows, at[0]] = through_rms(cross(ds, kb, 1, 0), qn, q_scale)
    gq[rows, at[1]] = through_rms(cross(ds, qb, 0, 0), kn, k_scale)
    gq[rows, at[2]] = cross(pb, back, 0, 0).astype(bf)


def grads_kernel(
    emb_ref, ctx_ref, wqkv_ref, wout_ref, gb_ref, hid_ref, out_q, out_o,
    state, qkv, gcore, gq, xt, abt, xn2, gq2, ab2, gb2,
    part0, part1, part2, relay0, relay1, relay2, near0, near1, near2,
    sum0, sum1, sum2, got0, got1, got2, low0, low1, low2, last0, last1, last2,
    fin, other, pair_send, pair_recv, send1, recv1, send2, recv2, send3, recv3,
    fin_send, fin_recv,
):
    place = coords()
    core = place[3]

    def peer_along(axis, step):
        at = list(place)
        at[axis] = lax.rem(at[axis] + step, 4)
        return device_at(*at)

    partner = device_at(place[0], place[1], place[2], 1 - core)
    greet([partner] + [peer_along(axis, step) for axis in range(3) for step in (1, 2, 3)])

    rows, width = emb_ref.shape
    qh, oh = gq2.shape[1], gb2.shape[1]
    mine_q, mine_o = pl.multiple_of(core * qh, qh), pl.multiple_of(core * oh, oh)
    its_q, its_o = pl.multiple_of((1 - core) * qh, qh), pl.multiple_of((1 - core) * oh, oh)
    top, bottom = pl.ds(0, rows), pl.ds(rows, rows)
    swaps = [
        remote(xn2.at[top], xn2.at[bottom], pair_send.at[0], pair_recv.at[0], partner),
        remote(gq.at[:, pl.ds(its_q, qh)], gq2.at[bottom], pair_send.at[1], pair_recv.at[1], partner),
        remote(ab2.at[top], ab2.at[bottom], pair_send.at[2], pair_recv.at[2], partner),
        remote(gb_ref.at[:, pl.ds(its_o, oh)], gb2.at[bottom], pair_send.at[3], pair_recv.at[3], partner),
    ]
    swaps[3].start()
    state[...] = emb_ref[...].astype(jnp.float32) + ctx_ref[...].astype(jnp.bfloat16).astype(jnp.float32)
    normed = (state[...] * rms_scale(state[...])).astype(jnp.bfloat16)
    xn2[top] = normed
    swaps[0].start()
    gb2[top] = gb_ref[:, pl.ds(mine_o, oh)]

    def project(n, carry):
        at = pl.ds(pl.multiple_of(n * 512, 512), 512)
        qkv[:, at] = jnp.dot(xn2[top], wqkv_ref[:, at], preferred_element_type=jnp.float32)
        return carry

    lax.fori_loop(0, 3 * width // 512, project, 0)
    for n in range(2):
        at = slice(n * width // 2, (n + 1) * width // 2)
        gcore[:, at] = cross(gb_ref[...], wout_ref[at], 1, 1)
    row = lax.broadcasted_iota(jnp.int32, (SPAN, SPAN), 0)
    column = lax.broadcasted_iota(jnp.int32, (SPAN, SPAN), 1)
    inside = (column <= row) & (column >= row - lax.rem(row, PATCH))

    def heads(n, carry):
        for h in (2 * n, 2 * n + 1):
            for first in range(0, rows, SPAN):
                local_head(h, first, inside, qkv, gcore, gq, ab2)
        return carry

    lax.fori_loop(0, LOCAL_HEADS // 2, heads, 0)
    swaps[1].start()
    swaps[2].start()
    gq2[top] = gq[:, pl.ds(mine_q, qh)]
    xt[0] = xn2[top].T
    swaps[0].wait_recv()
    xt[1] = xn2[bottom].T

    parts = (part0, part1, part2)
    relays, nears = (relay0, relay1, relay2), (near0, near1, near2)
    sums, gots = (sum0, sum1, sum2), (got0, got1, got2)
    lows, lasts = (low0, low1, low2), (last0, last1, last2)

    def fill(part, order, left, right, columns, into):
        span = slice(*columns)
        for z in range(4):
            at = slice(z * 256, (z + 1) * 256)
            block = (
                jnp.dot(left[0, at], right[top, span], preferred_element_type=jnp.float32)
                + jnp.dot(left[1, at], right[bottom, span], preferred_element_type=jnp.float32)
            ).astype(jnp.bfloat16)
            for y in range(4):
                for x in range(4):
                    at = (x, y, z)
                    row = (y * 4 + x) * 16
                    part[
                        at[order[0]], at[order[1]], at[order[2]], :, into : into + columns[1] - columns[0]
                    ] = block[row : row + 16]

    first = []

    def stage1(k):
        order = PART_ORDERS[k]
        axis = order[0]
        me = place[axis]
        right, left, far = lax.rem(me + 1, 4), lax.rem(me + 3, 4), lax.rem(me + 2, 4)
        to_right, to_left = peer_along(axis, 1), peer_along(axis, 3)
        part, relay, near = parts[k], relays[k], nears[k]
        lo, hi = pl.ds(0, 2), pl.ds(2, 2)

        def copy(n, source, target, peer):
            return remote(source, target, send1.at[k, n], recv1.at[k, n], peer)

        copies = [
            copy(0, part.at[far, lo], relay.at[0], to_right),
            copy(1, part.at[far, hi], relay.at[1], to_left),
            copy(2, part.at[right, hi], near.at[0, hi], to_right),
            copy(3, part.at[left, lo], near.at[1, lo], to_left),
            copy(4, part.at[right, lo], near.at[0, lo], to_right),
            copy(5, part.at[left, hi], near.at[1, hi], to_left),
        ]
        for n in range(4):
            copies[n].start()
        return copies, (right, left)

    def add_relay(k, copies, sides):
        part, relay = parts[k], relays[k]
        for n in range(2):
            copies[n].wait_recv()
            for j in range(2):
                at = 2 * n + j
                part[sides[n], at] = (
                    part[sides[n], at].astype(jnp.float32) + relay[n, j].astype(jnp.float32)
                ).astype(jnp.bfloat16)
            copies[4 + n].start()

    def stage2(k, copies):
        order = PART_ORDERS[k]
        for n in range(2, 6):
            copies[n].wait_recv()
        me = place[order[0]]
        for j in range(4):
            sums[k][j] = (
                parts[k][me, j].astype(jnp.float32)
                + nears[k][0, j].astype(jnp.float32)
                + nears[k][1, j].astype(jnp.float32)
            ).astype(jnp.bfloat16)
        axis = order[1]
        at = place[axis]
        sends = []
        for d in range(1, 4):
            send = remote(
                sums[k].at[lax.rem(at + d, 4)], gots[k].at[d - 1],
                send2.at[k, d - 1], recv2.at[k, d - 1], peer_along(axis, d),
            )
            send.start()
            sends.append(send)
        return sends

    def stage3(k, copies):
        order = PART_ORDERS[k]
        for copy in copies:
            copy.wait_recv()
        me = place[order[1]]
        total = sums[k][me].astype(jnp.float32)
        for d in range(3):
            total = total + gots[k][d].astype(jnp.float32)
        lows[k][...] = total.astype(jnp.bfloat16)
        axis = order[2]
        at = place[axis]
        sends = []
        for d in range(1, 4):
            send = remote(
                lows[k].at[lax.rem(at + d, 4)], lasts[k].at[d - 1],
                send3.at[k, d - 1], recv3.at[k, d - 1], peer_along(axis, d),
            )
            send.start()
            sends.append(send)
        return sends

    def finish(k, copies):
        for copy in copies:
            copy.wait_recv()
        me = place[PART_ORDERS[k][2]]
        total = lows[k][me].astype(jnp.float32)
        for d in range(3):
            total = total + lasts[k][d].astype(jnp.float32)
        start = sum(PART_COLS[:k])
        fin[:, start : start + PART_COLS[k]] = total

    swaps[1].wait_recv()
    split = PART_COLS[0] + PART_COLS[1]
    fill(part0, PART_ORDERS[0], xt, gq2, (0, PART_COLS[0]), 0)
    first.append(stage1(0))
    fill(part1, PART_ORDERS[1], xt, gq2, (PART_COLS[0], split), 0)
    first.append(stage1(1))
    fill(part2, PART_ORDERS[2], xt, gq2, (split, qh), 0)
    abt[0] = ab2[top].T
    swaps[2].wait_recv()
    abt[1] = ab2[bottom].T
    swaps[3].wait_recv()
    fill(part2, PART_ORDERS[2], abt, gb2, (0, oh), qh - split)
    first.append(stage1(2))
    add_relay(0, *first[0])
    add_relay(1, *first[1])
    hid_ref[...] = (
        state[...] + jnp.dot(ab2[top], wout_ref[...], preferred_element_type=jnp.float32)
    ).astype(jnp.bfloat16)
    add_relay(2, *first[2])
    second = [stage2(k, first[k][0]) for k in range(3)]
    third = [stage3(k, second[k]) for k in range(3)]
    for k in range(3):
        finish(k, third[k])

    keep, give = pl.multiple_of(core * 8, 8), pl.multiple_of((1 - core) * 8, 8)
    end = remote(fin.at[pl.ds(give, 8)], other, fin_send, fin_recv, partner)
    end.start()
    out_q[:, pl.ds(mine_q, qh)] = fin[pl.ds(keep, 8), 0:qh]
    out_o[:, pl.ds(mine_o, oh)] = fin[pl.ds(keep, 8), qh : qh + oh]
    end.wait_recv()
    out_q[:, pl.ds(its_q, qh)] = other[:, 0:qh]
    out_o[:, pl.ds(its_o, oh)] = other[:, qh : qh + oh]
    for copy in swaps + [c for f in first for c in f[0]] + [c for s in second + third for c in s] + [end]:
        copy.wait_send()


def local_window(emb, context, w_qkv, w_out, cotangent):
    rows, width = emb.shape
    qw, ow = w_qkv.shape[1], w_out.shape[1]
    bf, f32 = jnp.bfloat16, jnp.float32
    vmem = pl.BlockSpec(memory_space=pltpu.VMEM)

    def each(*lead):
        return [pltpu.VMEM((*lead, 16, c), bf) for c in PART_COLS]

    def sems(*shape):
        return pltpu.SemaphoreType.DMA(shape)

    return pl.pallas_call(
        grads_kernel,
        name="local_window",
        out_shape=(
            jax.ShapeDtypeStruct((rows, width), bf),
            jax.ShapeDtypeStruct((8, qw), f32),
            jax.ShapeDtypeStruct((8, ow), f32),
        ),
        in_specs=[vmem] * 5,
        out_specs=(vmem,) * 3,
        scratch_shapes=[
            pltpu.VMEM((rows, width), f32),
            pltpu.VMEM((rows, qw), f32),
            pltpu.VMEM((rows, width), f32),
            pltpu.VMEM((rows, qw), bf),
            pltpu.VMEM((2, width, rows), bf),
            pltpu.VMEM((2, width, rows), bf),
            pltpu.VMEM((2 * rows, width), bf),
            pltpu.VMEM((2 * rows, qw // 2), bf),
            pltpu.VMEM((2 * rows, width), bf),
            pltpu.VMEM((2 * rows, ow // 2), bf),
            *each(4, 4, 4), *each(2, 2, 4), *each(2, 4, 4),
            *each(4, 4), *each(3, 4), *each(4), *each(3),
            pltpu.VMEM((16, (qw + ow) // 2), f32),
            pltpu.VMEM((8, (qw + ow) // 2), f32),
            sems(4), sems(4), sems(3, 6), sems(3, 6), sems(3, 3), sems(3, 3), sems(3, 3), sems(3, 3),
            pltpu.SemaphoreType.DMA, pltpu.SemaphoreType.DMA,
        ],
        compiler_params=pltpu.CompilerParams(collective_id=5, has_side_effects=True, vmem_limit_bytes=44 << 20),
    )(emb, context, w_qkv, w_out, cotangent)


def per_device(byte_embeds, local_embeds, global_qkv, global_out, local_qkv, local_out, cotangent):
    flat = project_patches(byte_embeds, global_qkv)
    context = attend_and_project(*flat, global_out).reshape(local_embeds.shape)
    hidden, grad_qkv, grad_out = local_window(local_embeds, context, local_qkv[0], local_out[0], cotangent)
    return (hidden, grad_qkv[None], grad_out[None])


def solution(mesh):
    in_specs = (
        P(("ctx", "tp"), None),
        P(("ctx", "tp"), None),
        P(None, None, "tp"),
        P("tp", None),
        P(),
        P(),
        P(("ctx", "tp"), None),
    )
    out_specs = (P(("ctx", "tp"), None), P(None, ("ctx", "tp"), None), P(None, ("ctx", "tp"), None))
    return jax.shard_map(
        per_device, mesh=mesh, in_specs=in_specs, out_specs=out_specs, check_vma=False
    )
```

```python
import math

import jax
import jax.numpy as jnp
from jax import lax
from jax.experimental import pallas as pl
from jax.experimental.pallas import tpu as pltpu
from jax.sharding import PartitionSpec as P

PATCH = 8
HEAD_DIM = 128
LOCAL_HEADS = 8
LOCAL_HEAD_DIM = 128


MESH = pl.DeviceIdType.MESH


def coords():
    ctx, tp = lax.axis_index("ctx"), lax.axis_index("tp")
    x, core = lax.rem(lax.div(tp, 2), 4), lax.rem(tp, 2)
    y = lax.rem(ctx, 2) * 2 + lax.div(tp, 8)
    return x, y, lax.div(ctx, 2), core


def device_at(x, y, z, core):
    return {"ctx": z * 2 + lax.div(y, 2), "tp": lax.rem(y, 2) * 8 + x * 2 + core}


def greet(peers):
    barrier = pltpu.get_barrier_semaphore()
    for peer in peers:
        pl.semaphore_signal(barrier, inc=1, device_id=peer, device_id_type=MESH)
    pl.semaphore_wait(barrier, len(peers))


def remote(source, target, send_sem, recv_sem, peer):
    return pltpu.make_async_remote_copy(
        src_ref=source,
        dst_ref=target,
        send_sem=send_sem,
        recv_sem=recv_sem,
        device_id=peer,
        device_id_type=MESH,
    )


def rms_norm(values):
    return values * lax.rsqrt(jnp.mean(values * values, axis=-1, keepdims=True) + 1e-06)


CHUNK = 512
LANES = 4096


def project_kernel(
    bytes_ref, w_ref, q_ref, k_ref, v_ref, theirs, wide_rows, xs, ws, acc,
    swap_send, swap_recv, w_sem, p_send, p_recv, q_send, q_recv, f_send, f_recv,
):
    x, y, z, core = coords()
    pair = lax.rem(y, 2)
    partner = device_at(x, y, z, 1 - core)
    across = device_at(x, y + 1 - 2 * pair, z, core)

    def beside(step):
        return device_at(lax.rem(x + step, 4), y, z, core)

    greet([partner, across, beside(1), beside(2), beside(3)])
    copies = []

    def begin(copy):
        copy.start()
        copies.append(copy)
        return copy

    swap = begin(remote(bytes_ref, theirs, swap_send, swap_recv, partner))
    order = [c for n in range(4) for c in (4 + n, n)]
    mine, its = [core * 8 + c for c in range(8)], [(1 - core) * 8 + c for c in range(8)]
    loads = {}
    for c in order:
        for who, g in enumerate((mine[c], its[c])):
            load = pltpu.make_async_copy(
                w_ref.at[:, pl.ds(pl.multiple_of(g * CHUNK, CHUNK), CHUNK), :], ws.at[g], w_sem.at[who, c]
            )
            load.start()
            loads[who, c] = load
    rows = bytes_ref.shape[0]
    lane_tiles = bytes_ref.shape[1] // 128

    def spread(source, side):
        at = pl.ds(pl.multiple_of(side * rows, rows), rows)
        for n in range(lane_tiles):
            wide_rows[n, at] = source[:, n * 128 : (n + 1) * 128].astype(jnp.float32)

    spread(bytes_ref, core)
    acc[...] = jnp.zeros_like(acc)
    swap.wait_recv()
    spread(theirs, 1 - core)

    def entries(n, b):
        return wide_rows[n, pl.ds(b, 48, stride=PATCH), :]

    squares = jnp.zeros((48, 128), jnp.float32)
    for n in range(lane_tiles):
        for b in range(PATCH):
            squares = squares + entries(n, b) * entries(n, b)
    mean = jnp.sum(squares, axis=-1, keepdims=True) / (PATCH * lane_tiles * 128)
    scale = lax.rsqrt(mean + 1e-06)
    for side in (0, 1):

        @pl.when(core == side)
        def _():
            for c in range(8):
                for n in range(4):
                    normed = entries(c % 2 * 4 + n, side * 4 + c // 2) * scale
                    xs[side * 8 + c, pair, x, :, n * 128 : (n + 1) * 128] = normed.astype(jnp.bfloat16)

    right, left = lax.rem(x + 1, 4), lax.rem(x + 3, 4)
    pc, qc = {}, {}
    for n in range(4):
        g = mine[n]

        def copy(k, part, peer):
            return remote(part, part, p_send.at[n, k], p_recv.at[n, k], peer)

        pc[n] = [
            copy(0, xs.at[g, pair, x], across),
            copy(1, xs.at[g, :, x], beside(1)),
            copy(2, xs.at[g, :, x], beside(3)),
            copy(3, xs.at[g, 0, left], beside(1)),
            copy(4, xs.at[g, 1, right], beside(3)),
        ]
        g = mine[4 + n]

        def copy(k, part, peer):
            return remote(part, part, q_send.at[n, k], q_recv.at[n, k], peer)

        qc[n] = [copy(0, xs.at[g, pair], across)] + [copy(d, xs.at[g, pair, x], beside(d)) for d in (1, 2, 3)]
    for n in range(4):
        begin(pc[n][0])
        for d in (2, 1, 3):
            begin(qc[n][d])

    forwards = {
        c: remote(xs.at[mine[c]], xs.at[mine[c]], f_send.at[c], f_recv.at[c], partner) for c in range(8)
    }

    def multiply(who, c):
        loads[who, c].wait()
        g = (mine, its)[who][c]
        block = xs[g].reshape(acc.shape[1], CHUNK)

        def body(j, carry):
            acc[j] += jnp.dot(block, ws[g, j], preferred_element_type=jnp.float32)
            return carry

        lax.fori_loop(0, 3, body, 0)

    def p_turn(n):
        pc[n][0].wait_recv()
        begin(pc[n][1])
        begin(pc[n][2])

    def q_turn(n):
        for d in (1, 2, 3):
            qc[n][d].wait_recv()
        begin(qc[n][0])

    def p_relay(n):
        pc[n][1].wait_recv()
        begin(pc[n][3])
        pc[n][2].wait_recv()
        begin(pc[n][4])

    def p_done(n):
        pc[n][3].wait_recv()
        pc[n][4].wait_recv()
        begin(forwards[n])
        multiply(0, n)

    def q_done(n):
        qc[n][0].wait_recv()
        begin(forwards[4 + n])
        multiply(0, 4 + n)

    def other(c):
        forwards[c].wait_recv()
        multiply(1, c)

    p_turn(0)
    p_turn(1)
    q_turn(0)
    p_turn(2)
    p_turn(3)
    q_turn(1)
    q_turn(2)
    q_turn(3)
    q_done(0)
    p_relay(0)
    other(4)
    p_relay(1)
    p_done(0)
    q_done(1)
    p_relay(2)
    other(0)
    p_done(1)
    p_relay(3)
    other(5)
    other(1)
    q_done(2)
    p_done(2)
    other(6)
    other(2)
    p_done(3)
    q_done(3)
    other(3)
    other(7)

    for j, out in enumerate((q_ref, k_ref, v_ref)):
        for head in range(out.shape[1] // HEAD_DIM):
            at = slice(head * HEAD_DIM, (head + 1) * HEAD_DIM)
            value = acc[j, :, at]
            if j < 2:
                value = rms_norm(value)
            out[:, at] = value.astype(jnp.bfloat16)
    for copy in copies:
        copy.wait_send()


def project_patches(byte_rows, w):
    bf, f32 = jnp.bfloat16, jnp.float32
    vmem = pl.BlockSpec(memory_space=pltpu.VMEM)
    rows, width = byte_rows.shape
    total, cols = 2 * rows // PATCH * 8, w.shape[2]

    def sems(*shape):
        return pltpu.SemaphoreType.DMA(shape)

    return pl.pallas_call(
        project_kernel,
        name="project_patches",
        out_shape=[jax.ShapeDtypeStruct((total, cols), bf)] * 3,
        in_specs=[vmem, pl.BlockSpec(memory_space=pl.ANY)],
        out_specs=[vmem] * 3,
        scratch_shapes=[
            pltpu.VMEM((rows, width), bf),
            pltpu.VMEM((width // 128, 2 * rows, 128), f32),
            pltpu.VMEM((16, 2, 4, 48, CHUNK), bf),
            pltpu.VMEM((16, 3, CHUNK, cols), bf),
            pltpu.VMEM((3, total, cols), f32),
            pltpu.SemaphoreType.DMA, pltpu.SemaphoreType.DMA,
            sems(2, 8), sems(4, 5), sems(4, 5), sems(4, 4), sems(4, 4), sems(8), sems(8),
        ],
        compiler_params=pltpu.CompilerParams(collective_id=1, has_side_effects=True, vmem_limit_bytes=44 << 20),
    )(byte_rows, w)


def attend(
    x, y, z, core, begin, q_ref, k_ref, v_ref, att2, q2, ka, va, acc, tall, back,
    y_send, y_recv, z_send, z_recv, row_send, row_recv, back_send, back_recv, swap_send, swap_recv,
):
    half = lax.div(y, 2)
    partner = device_at(x, y, z, 1 - core)
    opposite = device_at(x, lax.rem(y + 2, 4), z, core)
    rows = q_ref.shape[0]
    mine = pl.ds(pl.multiple_of(half * HEAD_DIM, HEAD_DIM), HEAD_DIM)
    its = pl.ds(pl.multiple_of((1 - half) * HEAD_DIM, HEAD_DIM), HEAD_DIM)

    across = [
        begin(remote(source.at[:, its], target, y_send.at[n], y_recv.at[n], opposite))
        for n, (source, target) in enumerate(
            ((k_ref, ka.at[z, half]), (v_ref, va.at[z, half]), (q_ref, q2.at[half]))
        )
    ]

    above, below = device_at(x, y, lax.rem(z + 1, 4), core), device_at(x, y, lax.rem(z + 3, 4), core)
    stores = (ka, va)
    jobs = []

    def piece(owner, kind, which):
        return stores[kind].at[owner, half if which == 0 else 1 - half]

    def job(slot, kind, which, owner, peer, sends, fresh):
        target = piece(owner, kind, which)
        source = (k_ref, v_ref)[kind].at[:, mine] if fresh and which == 0 else target
        made = remote(source, target, z_send.at[slot, kind, which], z_recv.at[slot, kind, which], peer)
        jobs.append((sends, made))
        return made

    direct, wrap, transit, relay_k, relay_v = {}, {}, {}, {}, {}
    for which in (0, 1):
        for kind in (0, 1):
            direct[kind, which] = job(0, kind, which, z, above, z < 3, True)
            wrap[kind, which] = job(1, kind, which, z, below, z == 0, True)
        transit[which] = job(3, 1, which, z, below, z == 1, True)
        relay_k[which] = job(2, 0, which, lax.rem(z + 3, 4), above, (z == 1) | (z == 2), False)
        relay_v[which] = job(2, 1, which, 1 - lax.div(z, 3), below, (z == 0) | (z == 3), False)

    def send_fresh(kind, which):
        pl.when(z < 3)(direct[kind, which].start)
        pl.when(z == 0)(wrap[kind, which].start)
        if kind == 1:
            pl.when(z == 1)(transit[which].start)

    def send_on(which):
        @pl.when((z == 1) | (z == 2))
        def _():
            direct[0, which].wait_recv()
            relay_k[which].start()

        @pl.when(z == 3)
        def _():
            wrap[1, which].wait_recv()
            relay_v[which].start()

        @pl.when(z == 0)
        def _():
            transit[which].wait_recv()
            relay_v[which].start()

    send_fresh(0, 0)
    send_fresh(1, 0)
    ka[z, half] = k_ref[:, mine]
    va[z, half] = v_ref[:, mine]
    q2[half] = q_ref[:, mine]
    for kind in (0, 1):
        across[kind].wait_recv()
        send_fresh(kind, 1)
    across[2].wait_recv()
    send_on(0)

    tile = 128
    tiles = rows // tile
    scale = 1.0 / math.sqrt(HEAD_DIM)

    def attend_tile(block, n, keys, values, masked, first):
        s = lax.dot_general(
            q2[block, n * tile : (n + 1) * tile], keys, (((1,), (1,)), ((), ())), preferred_element_type=jnp.float32
        )
        e = jnp.exp(s * scale)
        if masked:
            row = n * tile + lax.broadcasted_iota(jnp.int32, e.shape, 0)
            e = jnp.where(lax.broadcasted_iota(jnp.int32, e.shape, 1) <= row, e, 0.0)
        sums = jnp.dot(e.astype(jnp.bfloat16), values, preferred_element_type=jnp.float32)
        at = slice(n * tile, (n + 1) * tile)
        acc[block, at] = sums if first else acc[block, at] + sums

    def with_ones(values):
        return jnp.concatenate([values, jnp.ones_like(values)], axis=1)

    for k in (0, 1):
        keys, values = ka[z, k], with_ones(va[z, k])
        for block in range(k, 2):
            for n in range(tiles):
                attend_tile(block, n, keys, values, block == k, k == 0)

    send_on(1)

    def attend_all(owner):
        def body(k, carry):
            keys, values = ka[owner, k], with_ones(va[owner, k])
            for block in (0, 1):
                for n in range(tiles):
                    attend_tile(block, n, keys, values, False, False)
            return carry

        lax.fori_loop(0, 2, body, 0)

    @pl.when(z == 3)
    def _():
        for which in (0, 1):
            wrap[0, which].wait_recv()
        attend_all(0)

    @pl.when(z >= 1)
    def _():
        for which in (0, 1):
            pl.when(z == 3)(direct[0, which].wait_recv)
            direct[1, which].wait_recv()
        attend_all(z - 1)

    @pl.when(z >= 2)
    def _():
        for which in (0, 1):
            relay_k[which].wait_recv()
            relay_v[which].wait_recv()
        attend_all(z - 2)

    for block in (0, 1):
        tall[8 + block * rows : 8 + (block + 1) * rows] = acc[block, :, 0:HEAD_DIM] / acc[block, :, HEAD_DIM:]
    row = remote(
        tall.at[pl.ds(2 * rows, 8)], tall.at[pl.ds(0, 8)], row_send, row_recv,
        device_at(x, y, lax.rem(z + 1, 4), core),
    )
    pl.when(z < 3)(row.start)
    pl.when(z > 0)(row.wait_recv)

    @pl.when(z == 0)
    def _():
        tall[0:8] = jnp.zeros((8, HEAD_DIM), jnp.float32)

    for part in (0, 1):

        @pl.when(half == part)
        def _():
            back[...] = tall[7 + (1 - part) * rows : 7 + (2 - part) * rows].astype(jnp.bfloat16)
            att2[:, part * HEAD_DIM : (part + 1) * HEAD_DIM] = tall[
                7 + part * rows : 7 + (part + 1) * rows
            ].astype(jnp.bfloat16)

    width = 2 * HEAD_DIM
    far_mine = pl.ds(pl.multiple_of(width + half * HEAD_DIM, HEAD_DIM), HEAD_DIM)
    far_its = pl.ds(pl.multiple_of(width + (1 - half) * HEAD_DIM, HEAD_DIM), HEAD_DIM)
    returned = begin(remote(back, att2.at[:, mine], back_send, back_recv, opposite))
    near = begin(remote(att2.at[:, mine], att2.at[:, far_mine], swap_send.at[0], swap_recv.at[0], partner))
    returned.wait_recv()
    last = begin(remote(att2.at[:, its], att2.at[:, far_its], swap_send.at[1], swap_recv.at[1], partner))
    near.wait_recv()
    last.wait_recv()
    pl.when(z < 3)(row.wait_send)
    for sends, copy in jobs:
        pl.when(sends)(copy.wait_send)


def out_kernel(
    q_ref, k_ref, v_ref, w_ref, out_ref, q2, ka, va, acc, tall, back, att2, w2, pbuf, relay, near, psum, pgot, qbuf, qgot, qsum, qlast, fin, other,
    w_sem, pair_send, pair_recv, p_send, p_recv, q_send, q_recv, fin_send, fin_recv,
    *att_sems,
):
    x, y, z, core = coords()
    pair = lax.rem(y, 2)
    partner = device_at(x, y, z, 1 - core)
    across = device_at(x, y + 1 - 2 * pair, z, core)

    def beside(step):
        return device_at(lax.rem(x + step, 4), y, z, core)

    greet(
        [partner, across, beside(1), beside(2), beside(3), device_at(x, lax.rem(y + 2, 4), z, core)]
        + [device_at(x, y, lax.rem(z + d, 4), core) for d in (1, 2, 3)]
    )
    depth = q_ref.shape[1]
    copies = []

    def begin(copy):
        copy.start()
        copies.append(copy)
        return copy

    order = [c for n in range(4) for c in (4 + n, n)]
    theirs, mine = {}, {}
    for c in order:
        into = pl.ds(c * CHUNK, CHUNK)
        give = pl.ds(pl.multiple_of((1 - core) * LANES + c * CHUNK, CHUNK), CHUNK)
        keep = pl.ds(pl.multiple_of(core * LANES + c * CHUNK, CHUNK), CHUNK)
        theirs[c] = begin(
            remote(w_ref.at[:, give], w2.at[pl.ds(depth, depth), into], pair_send.at[c], pair_recv.at[c], partner)
        )
        mine[c] = pltpu.make_async_copy(w_ref.at[:, keep], w2.at[pl.ds(0, depth), into], w_sem.at[c])
        mine[c].start()
    attend(
        x, y, z, core, begin, q_ref, k_ref, v_ref, att2, q2, ka, va, acc, tall, back, *att_sems
    )

    right, left, far = lax.rem(x + 1, 4), lax.rem(x + 3, 4), lax.rem(x + 2, 4)
    pcopies, qcopies = {}, {}
    for c in order:
        mine[c].wait()
        theirs[c].wait_recv()
        block = jnp.dot(
            att2[...], w2[:, c * CHUNK : (c + 1) * CHUNK], preferred_element_type=jnp.float32
        ).astype(jnp.bfloat16)
        for row in range(8):
            piece = block[row * 48 : row * 48 + 48]
            if c < 4:
                pbuf[c, row % 4, row // 4] = piece
            else:
                qbuf[c - 4, row // 4, row % 4] = piece
        if c < 4:

            def copy(k, source, target, peer):
                return remote(source, target, p_send.at[c, k], p_recv.at[c, k], peer)

            pcopies[c] = [
                copy(0, pbuf.at[c, far, 0], relay.at[c, 0], beside(1)),
                copy(1, pbuf.at[c, far, 1], relay.at[c, 1], beside(3)),
                copy(2, pbuf.at[c, right, 1], near.at[c, 0, 1], beside(1)),
                copy(3, pbuf.at[c, left, 0], near.at[c, 1, 0], beside(3)),
                copy(4, pbuf.at[c, right, 0], near.at[c, 0, 0], beside(1)),
                copy(5, pbuf.at[c, left, 1], near.at[c, 1, 1], beside(3)),
                copy(6, psum.at[c, 1 - pair], pgot.at[c], across),
            ]
            for k in range(4):
                begin(pcopies[c][k])
        else:
            n = c - 4
            qcopies[n] = [remote(qbuf.at[n, 1 - pair], qgot.at[n], q_send.at[n, 0], q_recv.at[n, 0], across)] + [
                remote(qsum.at[n, lax.rem(x + d, 4)], qlast.at[n, d - 1], q_send.at[n, d], q_recv.at[n, d], beside(d))
                for d in (1, 2, 3)
            ]
            begin(qcopies[n][0])

    def wide(value):
        return value.astype(jnp.float32)

    def p_relay(n):
        for k, side in ((0, right), (1, left)):
            pcopies[n][k].wait_recv()
            pbuf[n, side, k] = (wide(pbuf[n, side, k]) + wide(relay[n, k])).astype(jnp.bfloat16)
            begin(pcopies[n][4 + k])

    def p_across(n):
        for k in range(2, 6):
            pcopies[n][k].wait_recv()
        for k in range(2):
            psum[n, k] = (wide(pbuf[n, x, k]) + wide(near[n, 0, k]) + wide(near[n, 1, k])).astype(jnp.bfloat16)
        begin(pcopies[n][6])

    def p_end(n):
        pcopies[n][6].wait_recv()
        fin[:, n * CHUNK : (n + 1) * CHUNK] = wide(psum[n, pair]) + wide(pgot[n])

    def q_beside(n):
        qcopies[n][0].wait_recv()
        for k in range(4):
            qsum[n, k] = (wide(qbuf[n, pair, k]) + wide(qgot[n, k])).astype(jnp.bfloat16)
        for k in (2, 1, 3):
            begin(qcopies[n][k])

    def q_end(n):
        for k in (1, 2, 3):
            qcopies[n][k].wait_recv()
        total = wide(qsum[n, x])
        for k in range(3):
            total = total + wide(qlast[n, k])
        fin[:, (4 + n) * CHUNK : (5 + n) * CHUNK] = total

    p_relay(0)
    p_relay(1)
    q_beside(0)
    p_relay(2)
    p_relay(3)
    q_beside(1)
    p_across(0)
    p_across(1)
    q_beside(2)
    p_across(2)
    p_across(3)
    q_end(0)
    q_end(1)
    q_beside(3)
    for n in range(4):
        p_end(n)
    q_end(2)
    q_end(3)

    keep, give = pl.multiple_of(core * 24, 8), pl.multiple_of((1 - core) * 24, 8)
    end = begin(remote(fin.at[pl.ds(give, 24)], other, fin_send, fin_recv, partner))
    for b in range(4):
        out_ref[:, core * 4 + b, :] = fin[pl.ds(keep, 24), b * 1024 : b * 1024 + 1024]
    end.wait_recv()
    for b in range(4):
        out_ref[:, (1 - core) * 4 + b, :] = other[:, b * 1024 : b * 1024 + 1024]
    for copy in copies:
        copy.wait_send()


def attend_and_project(q, k, v, w):
    rows, depth = q.shape
    bf, f32 = jnp.bfloat16, jnp.float32
    vmem = pl.BlockSpec(memory_space=pltpu.VMEM)

    def units(*lead):
        return pltpu.VMEM((*lead, 48, CHUNK), bf)

    def sems(*shape):
        return pltpu.SemaphoreType.DMA(shape)

    return pl.pallas_call(
        out_kernel,
        name="attend_out",
        out_shape=jax.ShapeDtypeStruct((24, 8, 1024), f32),
        in_specs=[vmem] * 3 + [pl.BlockSpec(memory_space=pl.ANY)],
        out_specs=vmem,
        scratch_shapes=[
            pltpu.VMEM((2, rows, HEAD_DIM), bf),
            pltpu.VMEM((4, 2, rows, HEAD_DIM), bf),
            pltpu.VMEM((4, 2, rows, HEAD_DIM), bf),
            pltpu.VMEM((2, rows, 2 * HEAD_DIM), f32),
            pltpu.VMEM((8 + 2 * rows, HEAD_DIM), f32),
            pltpu.VMEM((rows, HEAD_DIM), bf),
            pltpu.VMEM((rows, 2 * depth), bf),
            pltpu.VMEM((2 * depth, LANES), bf),
            units(4, 4, 2), units(4, 2), units(4, 2, 2), units(4, 2), units(4),
            units(4, 2, 4), units(4, 4), units(4, 4), units(4, 3),
            pltpu.VMEM((48, LANES), f32),
            pltpu.VMEM((24, LANES), f32),
            sems(8), sems(8), sems(8), sems(4, 7), sems(4, 7), sems(4, 4), sems(4, 4),
            pltpu.SemaphoreType.DMA, pltpu.SemaphoreType.DMA,
            sems(3), sems(3), sems(4, 2, 2), sems(4, 2, 2),
            pltpu.SemaphoreType.DMA, pltpu.SemaphoreType.DMA,
            pltpu.SemaphoreType.DMA, pltpu.SemaphoreType.DMA, sems(2), sems(2),
        ],
        compiler_params=pltpu.CompilerParams(collective_id=3, has_side_effects=True, vmem_limit_bytes=40 << 20),
    )(q, k, v, w)


PART_COLS = (640, 640, 768)
PART_ORDERS = ((0, 1, 2), (1, 2, 0), (2, 0, 1))


def rms_scale(values):
    return lax.rsqrt(jnp.mean(values * values, axis=-1, keepdims=True) + 1e-06)


def cross(left, right, left_axis, right_axis):
    return lax.dot_general(
        left, right, (((left_axis,), (right_axis,)), ((), ())), preferred_element_type=jnp.float32
    )


SPAN = 96


def local_head(h, first, inside, qkv, gcore, gq, ab):
    rows = slice(first, first + SPAN)
    bf = jnp.bfloat16
    width = gcore.shape[1]
    at = [pl.ds(pl.multiple_of(n * width + h * LOCAL_HEAD_DIM, LOCAL_HEAD_DIM), LOCAL_HEAD_DIM) for n in range(3)]
    q, k, v = (qkv[rows, part] for part in at)
    q_scale, k_scale = rms_scale(q), rms_scale(k)
    qn, kn = q * q_scale, k * k_scale
    qb, kb, vb = qn.astype(bf), kn.astype(bf), v.astype(bf)
    scale = 1.0 / math.sqrt(LOCAL_HEAD_DIM)
    e = jnp.where(inside, jnp.exp(cross(qb, kb, 1, 1) * scale), 0.0)
    p = e / jnp.sum(e, axis=-1, keepdims=True)
    pb = p.astype(bf)
    ab[rows, at[0]] = cross(pb, vb, 1, 0).astype(bf)
    back = gcore[rows, at[0]].astype(bf)
    dp = cross(back, vb, 1, 1)
    ds = (p * (dp - jnp.sum(p * dp, axis=-1, keepdims=True)) * scale).astype(bf)

    def through_rms(grad, normed, factor):
        return (factor * (grad - normed * jnp.mean(grad * normed, axis=-1, keepdims=True))).astype(bf)

    gq[rows, at[0]] = through_rms(cross(ds, kb, 1, 0), qn, q_scale)
    gq[rows, at[1]] = through_rms(cross(ds, qb, 0, 0), kn, k_scale)
    gq[rows, at[2]] = cross(pb, back, 0, 0).astype(bf)


def grads_kernel(
    emb_ref, ctx_ref, wqkv_ref, wout_ref, gb_ref, hid_ref, out_q, out_o,
    state, qkv, gcore, gq, xt, abt, xn2, gq2, ab2, gb2,
    part0, part1, part2, relay0, relay1, relay2, near0, near1, near2,
    sum0, sum1, sum2, got0, got1, got2, low0, low1, low2, last0, last1, last2,
    fin, other, pair_send, pair_recv, send1, recv1, send2, recv2, send3, recv3,
    fin_send, fin_recv,
):
    place = coords()
    core = place[3]

    def peer_along(axis, step):
        at = list(place)
        at[axis] = lax.rem(at[axis] + step, 4)
        return device_at(*at)

    partner = device_at(place[0], place[1], place[2], 1 - core)
    greet([partner] + [peer_along(axis, step) for axis in range(3) for step in (1, 2, 3)])

    rows, width = emb_ref.shape
    qh, oh = gq2.shape[1], gb2.shape[1]
    mine_q, mine_o = pl.multiple_of(core * qh, qh), pl.multiple_of(core * oh, oh)
    its_q, its_o = pl.multiple_of((1 - core) * qh, qh), pl.multiple_of((1 - core) * oh, oh)
    top, bottom = pl.ds(0, rows), pl.ds(rows, rows)
    swaps = [
        remote(xn2.at[top], xn2.at[bottom], pair_send.at[0], pair_recv.at[0], partner),
        remote(gq.at[:, pl.ds(its_q, qh)], gq2.at[bottom], pair_send.at[1], pair_recv.at[1], partner),
        remote(ab2.at[top], ab2.at[bottom], pair_send.at[2], pair_recv.at[2], partner),
        remote(gb_ref.at[:, pl.ds(its_o, oh)], gb2.at[bottom], pair_send.at[3], pair_recv.at[3], partner),
    ]
    swaps[3].start()
    state[...] = emb_ref[...].astype(jnp.float32) + ctx_ref[...].astype(jnp.bfloat16).astype(jnp.float32)
    normed = (state[...] * rms_scale(state[...])).astype(jnp.bfloat16)
    xn2[top] = normed
    swaps[0].start()
    gb2[top] = gb_ref[:, pl.ds(mine_o, oh)]

    def project(n, carry):
        at = pl.ds(pl.multiple_of(n * 512, 512), 512)
        qkv[:, at] = jnp.dot(xn2[top], wqkv_ref[:, at], preferred_element_type=jnp.float32)
        return carry

    lax.fori_loop(0, 3 * width // 512, project, 0)
    for n in range(2):
        at = slice(n * width // 2, (n + 1) * width // 2)
        gcore[:, at] = cross(gb_ref[...], wout_ref[at], 1, 1)
    row = lax.broadcasted_iota(jnp.int32, (SPAN, SPAN), 0)
    column = lax.broadcasted_iota(jnp.int32, (SPAN, SPAN), 1)
    inside = (column <= row) & (column >= row - lax.rem(row, PATCH))

    def heads(n, carry):
        for i in range(8):
            h = 8 * n + i
            for first in range(0, rows, SPAN):
                local_head(h, first, inside, qkv, gcore, gq, ab2)
        return carry

    lax.fori_loop(0, LOCAL_HEADS // 8, heads, 0)
    swaps[1].start()
    swaps[2].start()
    gq2[top] = gq[:, pl.ds(mine_q, qh)]
    xt[0] = xn2[top].T
    swaps[0].wait_recv()
    xt[1] = xn2[bottom].T

    parts = (part0, part1, part2)
    relays, nears = (relay0, relay1, relay2), (near0, near1, near2)
    sums, gots = (sum0, sum1, sum2), (got0, got1, got2)
    lows, lasts = (low0, low1, low2), (last0, last1, last2)

    def fill(part, order, left, right, columns, into):
        span = slice(*columns)
        for z in range(4):
            at = slice(z * 256, (z + 1) * 256)
            block = (
                jnp.dot(left[0, at], right[top, span], preferred_element_type=jnp.float32)
                + jnp.dot(left[1, at], right[bottom, span], preferred_element_type=jnp.float32)
            ).astype(jnp.bfloat16)
            for y in range(4):
                for x in range(4):
                    at = (x, y, z)
                    row = (y * 4 + x) * 16
                    part[
                        at[order[0]], at[order[1]], at[order[2]], :, into : into + columns[1] - columns[0]
                    ] = block[row : row + 16]

    first = []

    def stage1(k):
        order = PART_ORDERS[k]
        axis = order[0]
        me = place[axis]
        right, left, far = lax.rem(me + 1, 4), lax.rem(me + 3, 4), lax.rem(me + 2, 4)
        to_right, to_left = peer_along(axis, 1), peer_along(axis, 3)
        part, relay, near = parts[k], relays[k], nears[k]
        lo, hi = pl.ds(0, 2), pl.ds(2, 2)

        def copy(n, source, target, peer):
            return remote(source, target, send1.at[k, n], recv1.at[k, n], peer)

        copies = [
            copy(0, part.at[far, lo], relay.at[0], to_right),
            copy(1, part.at[far, hi], relay.at[1], to_left),
            copy(2, part.at[right, hi], near.at[0, hi], to_right),
            copy(3, part.at[left, lo], near.at[1, lo], to_left),
            copy(4, part.at[right, lo], near.at[0, lo], to_right),
            copy(5, part.at[left, hi], near.at[1, hi], to_left),
        ]
        for n in range(4):
            copies[n].start()
        return copies, (right, left)

    def add_relay(k, copies, sides):
        part, relay = parts[k], relays[k]
        for n in range(2):
            copies[n].wait_recv()
            for j in range(2):
                at = 2 * n + j
                part[sides[n], at] = (
                    part[sides[n], at].astype(jnp.float32) + relay[n, j].astype(jnp.float32)
                ).astype(jnp.bfloat16)
            copies[4 + n].start()

    def stage2(k, copies):
        order = PART_ORDERS[k]
        for n in range(2, 6):
            copies[n].wait_recv()
        me = place[order[0]]
        for j in range(4):
            sums[k][j] = (
                parts[k][me, j].astype(jnp.float32)
                + nears[k][0, j].astype(jnp.float32)
                + nears[k][1, j].astype(jnp.float32)
            ).astype(jnp.bfloat16)
        axis = order[1]
        at = place[axis]
        sends = []
        for d in range(1, 4):
            send = remote(
                sums[k].at[lax.rem(at + d, 4)], gots[k].at[d - 1],
                send2.at[k, d - 1], recv2.at[k, d - 1], peer_along(axis, d),
            )
            send.start()
            sends.append(send)
        return sends

    def stage3(k, copies):
        order = PART_ORDERS[k]
        for copy in copies:
            copy.wait_recv()
        me = place[order[1]]
        total = sums[k][me].astype(jnp.float32)
        for d in range(3):
            total = total + gots[k][d].astype(jnp.float32)
        lows[k][...] = total.astype(jnp.bfloat16)
        axis = order[2]
        at = place[axis]
        sends = []
        for d in range(1, 4):
            send = remote(
                lows[k].at[lax.rem(at + d, 4)], lasts[k].at[d - 1],
                send3.at[k, d - 1], recv3.at[k, d - 1], peer_along(axis, d),
            )
            send.start()
            sends.append(send)
        return sends

    def finish(k, copies):
        for copy in copies:
            copy.wait_recv()
        me = place[PART_ORDERS[k][2]]
        total = lows[k][me].astype(jnp.float32)
        for d in range(3):
            total = total + lasts[k][d].astype(jnp.float32)
        start = sum(PART_COLS[:k])
        fin[:, start : start + PART_COLS[k]] = total

    swaps[1].wait_recv()
    split = PART_COLS[0] + PART_COLS[1]
    fill(part0, PART_ORDERS[0], xt, gq2, (0, PART_COLS[0]), 0)
    first.append(stage1(0))
    fill(part1, PART_ORDERS[1], xt, gq2, (PART_COLS[0], split), 0)
    first.append(stage1(1))
    fill(part2, PART_ORDERS[2], xt, gq2, (split, qh), 0)
    abt[0] = ab2[top].T
    swaps[2].wait_recv()
    abt[1] = ab2[bottom].T
    swaps[3].wait_recv()
    fill(part2, PART_ORDERS[2], abt, gb2, (0, oh), qh - split)
    first.append(stage1(2))
    add_relay(0, *first[0])
    add_relay(1, *first[1])
    hid_ref[...] = (
        state[...] + jnp.dot(ab2[top], wout_ref[...], preferred_element_type=jnp.float32)
    ).astype(jnp.bfloat16)
    add_relay(2, *first[2])
    second = [stage2(k, first[k][0]) for k in range(3)]
    third = [stage3(k, second[k]) for k in range(3)]
    for k in range(3):
        finish(k, third[k])

    keep, give = pl.multiple_of(core * 8, 8), pl.multiple_of((1 - core) * 8, 8)
    end = remote(fin.at[pl.ds(give, 8)], other, fin_send, fin_recv, partner)
    end.start()
    out_q[:, pl.ds(mine_q, qh)] = fin[pl.ds(keep, 8), 0:qh]
    out_o[:, pl.ds(mine_o, oh)] = fin[pl.ds(keep, 8), qh : qh + oh]
    end.wait_recv()
    out_q[:, pl.ds(its_q, qh)] = other[:, 0:qh]
    out_o[:, pl.ds(its_o, oh)] = other[:, qh : qh + oh]
    for copy in swaps + [c for f in first for c in f[0]] + [c for s in second + third for c in s] + [end]:
        copy.wait_send()


def local_window(emb, context, w_qkv, w_out, cotangent):
    rows, width = emb.shape
    qw, ow = w_qkv.shape[1], w_out.shape[1]
    bf, f32 = jnp.bfloat16, jnp.float32
    vmem = pl.BlockSpec(memory_space=pltpu.VMEM)

    def each(*lead):
        return [pltpu.VMEM((*lead, 16, c), bf) for c in PART_COLS]

    def sems(*shape):
        return pltpu.SemaphoreType.DMA(shape)

    return pl.pallas_call(
        grads_kernel,
        name="local_window",
        out_shape=(
            jax.ShapeDtypeStruct((rows, width), bf),
            jax.ShapeDtypeStruct((8, qw), f32),
            jax.ShapeDtypeStruct((8, ow), f32),
        ),
        in_specs=[vmem] * 5,
        out_specs=(vmem,) * 3,
        scratch_shapes=[
            pltpu.VMEM((rows, width), f32),
            pltpu.VMEM((rows, qw), f32),
            pltpu.VMEM((rows, width), f32),
            pltpu.VMEM((rows, qw), bf),
            pltpu.VMEM((2, width, rows), bf),
            pltpu.VMEM((2, width, rows), bf),
            pltpu.VMEM((2 * rows, width), bf),
            pltpu.VMEM((2 * rows, qw // 2), bf),
            pltpu.VMEM((2 * rows, width), bf),
            pltpu.VMEM((2 * rows, ow // 2), bf),
            *each(4, 4, 4), *each(2, 2, 4), *each(2, 4, 4),
            *each(4, 4), *each(3, 4), *each(4), *each(3),
            pltpu.VMEM((16, (qw + ow) // 2), f32),
            pltpu.VMEM((8, (qw + ow) // 2), f32),
            sems(4), sems(4), sems(3, 6), sems(3, 6), sems(3, 3), sems(3, 3), sems(3, 3), sems(3, 3),
            pltpu.SemaphoreType.DMA, pltpu.SemaphoreType.DMA,
        ],
        compiler_params=pltpu.CompilerParams(collective_id=5, has_side_effects=True, vmem_limit_bytes=44 << 20),
    )(emb, context, w_qkv, w_out, cotangent)


def per_device(byte_embeds, local_embeds, global_qkv, global_out, local_qkv, local_out, cotangent):
    flat = project_patches(byte_embeds, global_qkv)
    context = attend_and_project(*flat, global_out).reshape(local_embeds.shape)
    hidden, grad_qkv, grad_out = local_window(local_embeds, context, local_qkv[0], local_out[0], cotangent)
    return (hidden, grad_qkv[None], grad_out[None])


def solution(mesh):
    in_specs = (
        P(("ctx", "tp"), None),
        P(("ctx", "tp"), None),
        P(None, None, "tp"),
        P("tp", None),
        P(),
        P(),
        P(("ctx", "tp"), None),
    )
    out_specs = (P(("ctx", "tp"), None), P(None, ("ctx", "tp"), None), P(None, ("ctx", "tp"), None))
    return jax.shard_map(
        per_device, mesh=mesh, in_specs=in_specs, out_specs=out_specs, check_vma=False
    )
```

```python
import math

import jax
import jax.numpy as jnp
from jax import lax
from jax.experimental import pallas as pl
from jax.experimental.pallas import tpu as pltpu
from jax.sharding import PartitionSpec as P

PATCH = 8
HEAD_DIM = 128
LOCAL_HEADS = 8
LOCAL_HEAD_DIM = 128


MESH = pl.DeviceIdType.MESH


def coords():
    ctx, tp = lax.axis_index("ctx"), lax.axis_index("tp")
    x, core = lax.rem(lax.div(tp, 2), 4), lax.rem(tp, 2)
    y = lax.rem(ctx, 2) * 2 + lax.div(tp, 8)
    return x, y, lax.div(ctx, 2), core


def device_at(x, y, z, core):
    return {"ctx": z * 2 + lax.div(y, 2), "tp": lax.rem(y, 2) * 8 + x * 2 + core}


def greet(peers):
    barrier = pltpu.get_barrier_semaphore()
    for peer in peers:
        pl.semaphore_signal(barrier, inc=1, device_id=peer, device_id_type=MESH)
    pl.semaphore_wait(barrier, len(peers))


def remote(source, target, send_sem, recv_sem, peer):
    return pltpu.make_async_remote_copy(
        src_ref=source,
        dst_ref=target,
        send_sem=send_sem,
        recv_sem=recv_sem,
        device_id=peer,
        device_id_type=MESH,
    )


def rms_norm(values):
    return values * lax.rsqrt(jnp.mean(values * values, axis=-1, keepdims=True) + 1e-06)


CHUNK = 512
LANES = 4096


def project_kernel(
    bytes_ref, w_ref, q_ref, k_ref, v_ref, theirs, wide_rows, xs, ws, acc,
    swap_send, swap_recv, w_sem, p_send, p_recv, q_send, q_recv, f_send, f_recv,
):
    x, y, z, core = coords()
    pair = lax.rem(y, 2)
    partner = device_at(x, y, z, 1 - core)
    across = device_at(x, y + 1 - 2 * pair, z, core)

    def beside(step):
        return device_at(lax.rem(x + step, 4), y, z, core)

    greet([partner, across, beside(1), beside(2), beside(3)])
    copies = []

    def begin(copy):
        copy.start()
        copies.append(copy)
        return copy

    swap = begin(remote(bytes_ref, theirs, swap_send, swap_recv, partner))
    order = [c for n in range(4) for c in (4 + n, n)]
    mine, its = [core * 8 + c for c in range(8)], [(1 - core) * 8 + c for c in range(8)]
    loads = {}
    for c in order:
        for who, g in enumerate((mine[c], its[c])):
            load = pltpu.make_async_copy(
                w_ref.at[:, pl.ds(pl.multiple_of(g * CHUNK, CHUNK), CHUNK), :], ws.at[g], w_sem.at[who, c]
            )
            load.start()
            loads[who, c] = load
    rows = bytes_ref.shape[0]
    lane_tiles = bytes_ref.shape[1] // 128

    def spread(source, side):
        at = pl.ds(pl.multiple_of(side * rows, rows), rows)
        for n in range(lane_tiles):
            wide_rows[n, at] = source[:, n * 128 : (n + 1) * 128].astype(jnp.float32)

    spread(bytes_ref, core)
    acc[...] = jnp.zeros_like(acc)
    swap.wait_recv()
    spread(theirs, 1 - core)

    def entries(n, b):
        return wide_rows[n, pl.ds(b, 48, stride=PATCH), :]

    squares = jnp.zeros((48, 128), jnp.float32)
    for n in range(lane_tiles):
        for b in range(PATCH):
            squares = squares + entries(n, b) * entries(n, b)
    mean = jnp.sum(squares, axis=-1, keepdims=True) / (PATCH * lane_tiles * 128)
    scale = lax.rsqrt(mean + 1e-06)
    for side in (0, 1):

        @pl.when(core == side)
        def _():
            for c in range(8):
                for n in range(4):
                    normed = entries(c % 2 * 4 + n, side * 4 + c // 2) * scale
                    xs[side * 8 + c, pair, x, :, n * 128 : (n + 1) * 128] = normed.astype(jnp.bfloat16)

    right, left = lax.rem(x + 1, 4), lax.rem(x + 3, 4)
    pc, qc = {}, {}
    for n in range(4):
        g = mine[n]

        def copy(k, part, peer):
            return remote(part, part, p_send.at[n, k], p_recv.at[n, k], peer)

        pc[n] = [
            copy(0, xs.at[g, pair, x], across),
            copy(1, xs.at[g, :, x], beside(1)),
            copy(2, xs.at[g, :, x], beside(3)),
            copy(3, xs.at[g, 0, left], beside(1)),
            copy(4, xs.at[g, 1, right], beside(3)),
        ]
        g = mine[4 + n]

        def copy(k, part, peer):
            return remote(part, part, q_send.at[n, k], q_recv.at[n, k], peer)

        qc[n] = [copy(0, xs.at[g, pair], across)] + [copy(d, xs.at[g, pair, x], beside(d)) for d in (1, 2, 3)]
    for n in range(4):
        begin(pc[n][0])
        for d in (2, 1, 3):
            begin(qc[n][d])

    forwards = {
        c: remote(xs.at[mine[c]], xs.at[mine[c]], f_send.at[c], f_recv.at[c], partner) for c in range(8)
    }

    def multiply(who, c):
        loads[who, c].wait()
        g = (mine, its)[who][c]
        block = xs[g].reshape(acc.shape[1], CHUNK)

        def body(j, carry):
            acc[j] += jnp.dot(block, ws[g, j], preferred_element_type=jnp.float32)
            return carry

        lax.fori_loop(0, 3, body, 0)

    def p_turn(n):
        pc[n][0].wait_recv()
        begin(pc[n][1])
        begin(pc[n][2])

    def q_turn(n):
        for d in (1, 2, 3):
            qc[n][d].wait_recv()
        begin(qc[n][0])

    def p_relay(n):
        pc[n][1].wait_recv()
        begin(pc[n][3])
        pc[n][2].wait_recv()
        begin(pc[n][4])

    def p_done(n):
        pc[n][3].wait_recv()
        pc[n][4].wait_recv()
        begin(forwards[n])
        multiply(0, n)

    def q_done(n):
        qc[n][0].wait_recv()
        begin(forwards[4 + n])
        multiply(0, 4 + n)

    def other(c):
        forwards[c].wait_recv()
        multiply(1, c)

    p_turn(0)
    p_turn(1)
    q_turn(0)
    p_turn(2)
    p_turn(3)
    q_turn(1)
    q_turn(2)
    q_turn(3)
    q_done(0)
    p_relay(0)
    other(4)
    p_relay(1)
    p_done(0)
    q_done(1)
    p_relay(2)
    other(0)
    p_done(1)
    p_relay(3)
    other(5)
    other(1)
    q_done(2)
    p_done(2)
    other(6)
    other(2)
    p_done(3)
    q_done(3)
    other(3)
    other(7)

    for j, out in enumerate((q_ref, k_ref, v_ref)):
        for head in range(out.shape[1] // HEAD_DIM):
            at = slice(head * HEAD_DIM, (head + 1) * HEAD_DIM)
            value = acc[j, :, at]
            if j < 2:
                value = rms_norm(value)
            out[:, at] = value.astype(jnp.bfloat16)
    for copy in copies:
        copy.wait_send()


def project_patches(byte_rows, w):
    bf, f32 = jnp.bfloat16, jnp.float32
    vmem = pl.BlockSpec(memory_space=pltpu.VMEM)
    rows, width = byte_rows.shape
    total, cols = 2 * rows // PATCH * 8, w.shape[2]

    def sems(*shape):
        return pltpu.SemaphoreType.DMA(shape)

    return pl.pallas_call(
        project_kernel,
        name="project_patches",
        out_shape=[jax.ShapeDtypeStruct((total, cols), bf)] * 3,
        in_specs=[vmem, pl.BlockSpec(memory_space=pl.ANY)],
        out_specs=[vmem] * 3,
        scratch_shapes=[
            pltpu.VMEM((rows, width), bf),
            pltpu.VMEM((width // 128, 2 * rows, 128), f32),
            pltpu.VMEM((16, 2, 4, 48, CHUNK), bf),
            pltpu.VMEM((16, 3, CHUNK, cols), bf),
            pltpu.VMEM((3, total, cols), f32),
            pltpu.SemaphoreType.DMA, pltpu.SemaphoreType.DMA,
            sems(2, 8), sems(4, 5), sems(4, 5), sems(4, 4), sems(4, 4), sems(8), sems(8),
        ],
        compiler_params=pltpu.CompilerParams(collective_id=1, has_side_effects=True, vmem_limit_bytes=44 << 20),
    )(byte_rows, w)


def attend(
    x, y, z, core, begin, q_ref, k_ref, v_ref, att2, q2, ka, va, acc, tall, back,
    y_send, y_recv, z_send, z_recv, row_send, row_recv, back_send, back_recv, swap_send, swap_recv,
):
    half = lax.div(y, 2)
    partner = device_at(x, y, z, 1 - core)
    opposite = device_at(x, lax.rem(y + 2, 4), z, core)
    rows = q_ref.shape[0]
    mine = pl.ds(pl.multiple_of(half * HEAD_DIM, HEAD_DIM), HEAD_DIM)
    its = pl.ds(pl.multiple_of((1 - half) * HEAD_DIM, HEAD_DIM), HEAD_DIM)

    across = [
        begin(remote(source.at[:, its], target, y_send.at[n], y_recv.at[n], opposite))
        for n, (source, target) in enumerate(
            ((k_ref, ka.at[z, half]), (v_ref, va.at[z, half]), (q_ref, q2.at[half]))
        )
    ]

    above, below = device_at(x, y, lax.rem(z + 1, 4), core), device_at(x, y, lax.rem(z + 3, 4), core)
    stores = (ka, va)
    jobs = []

    def piece(owner, kind, which):
        return stores[kind].at[owner, half if which == 0 else 1 - half]

    def job(slot, kind, which, owner, peer, sends, fresh):
        target = piece(owner, kind, which)
        source = (k_ref, v_ref)[kind].at[:, mine] if fresh and which == 0 else target
        made = remote(source, target, z_send.at[slot, kind, which], z_recv.at[slot, kind, which], peer)
        jobs.append((sends, made))
        return made

    direct, wrap, transit, relay_k, relay_v = {}, {}, {}, {}, {}
    for which in (0, 1):
        for kind in (0, 1):
            direct[kind, which] = job(0, kind, which, z, above, z < 3, True)
            wrap[kind, which] = job(1, kind, which, z, below, z == 0, True)
        transit[which] = job(3, 1, which, z, below, z == 1, True)
        relay_k[which] = job(2, 0, which, lax.rem(z + 3, 4), above, (z == 1) | (z == 2), False)
        relay_v[which] = job(2, 1, which, 1 - lax.div(z, 3), below, (z == 0) | (z == 3), False)

    def send_fresh(kind, which):
        pl.when(z < 3)(direct[kind, which].start)
        pl.when(z == 0)(wrap[kind, which].start)
        if kind == 1:
            pl.when(z == 1)(transit[which].start)

    def send_on(which):
        @pl.when((z == 1) | (z == 2))
        def _():
            direct[0, which].wait_recv()
            relay_k[which].start()

        @pl.when(z == 3)
        def _():
            wrap[1, which].wait_recv()
            relay_v[which].start()

        @pl.when(z == 0)
        def _():
            transit[which].wait_recv()
            relay_v[which].start()

    send_fresh(0, 0)
    send_fresh(1, 0)
    ka[z, half] = k_ref[:, mine]
    va[z, half] = v_ref[:, mine]
    q2[half] = q_ref[:, mine]
    for kind in (0, 1):
        across[kind].wait_recv()
        send_fresh(kind, 1)
    across[2].wait_recv()
    send_on(0)

    tile = 128
    tiles = rows // tile
    scale = 1.0 / math.sqrt(HEAD_DIM)

    def attend_tile(block, n, keys, values, masked, first):
        s = lax.dot_general(
            q2[block, n * tile : (n + 1) * tile], keys, (((1,), (1,)), ((), ())), preferred_element_type=jnp.float32
        )
        e = jnp.exp(s * scale)
        if masked:
            row = n * tile + lax.broadcasted_iota(jnp.int32, e.shape, 0)
            e = jnp.where(lax.broadcasted_iota(jnp.int32, e.shape, 1) <= row, e, 0.0)
        sums = jnp.dot(e.astype(jnp.bfloat16), values, preferred_element_type=jnp.float32)
        at = slice(n * tile, (n + 1) * tile)
        acc[block, at] = sums if first else acc[block, at] + sums

    def with_ones(values):
        return jnp.concatenate([values, jnp.ones_like(values)], axis=1)

    for k in (0, 1):
        keys, values = ka[z, k], with_ones(va[z, k])
        for block in range(k, 2):
            for n in range(tiles):
                attend_tile(block, n, keys, values, block == k, k == 0)

    send_on(1)

    def attend_all(owner):
        def body(k, carry):
            keys, values = ka[owner, k], with_ones(va[owner, k])
            for block in (0, 1):
                for n in range(tiles):
                    attend_tile(block, n, keys, values, False, False)
            return carry

        lax.fori_loop(0, 2, body, 0)

    @pl.when(z == 3)
    def _():
        for which in (0, 1):
            wrap[0, which].wait_recv()
        attend_all(0)

    @pl.when(z >= 1)
    def _():
        for which in (0, 1):
            pl.when(z == 3)(direct[0, which].wait_recv)
            direct[1, which].wait_recv()
        attend_all(z - 1)

    @pl.when(z >= 2)
    def _():
        for which in (0, 1):
            relay_k[which].wait_recv()
            relay_v[which].wait_recv()
        attend_all(z - 2)

    for block in (0, 1):
        tall[8 + block * rows : 8 + (block + 1) * rows] = acc[block, :, 0:HEAD_DIM] / acc[block, :, HEAD_DIM:]
    row = remote(
        tall.at[pl.ds(2 * rows, 8)], tall.at[pl.ds(0, 8)], row_send, row_recv,
        device_at(x, y, lax.rem(z + 1, 4), core),
    )
    pl.when(z < 3)(row.start)
    pl.when(z > 0)(row.wait_recv)

    @pl.when(z == 0)
    def _():
        tall[0:8] = jnp.zeros((8, HEAD_DIM), jnp.float32)

    for part in (0, 1):

        @pl.when(half == part)
        def _():
            back[...] = tall[7 + (1 - part) * rows : 7 + (2 - part) * rows].astype(jnp.bfloat16)
            att2[:, part * HEAD_DIM : (part + 1) * HEAD_DIM] = tall[
                7 + part * rows : 7 + (part + 1) * rows
            ].astype(jnp.bfloat16)

    width = 2 * HEAD_DIM
    far_mine = pl.ds(pl.multiple_of(width + half * HEAD_DIM, HEAD_DIM), HEAD_DIM)
    far_its = pl.ds(pl.multiple_of(width + (1 - half) * HEAD_DIM, HEAD_DIM), HEAD_DIM)
    returned = begin(remote(back, att2.at[:, mine], back_send, back_recv, opposite))
    near = begin(remote(att2.at[:, mine], att2.at[:, far_mine], swap_send.at[0], swap_recv.at[0], partner))
    returned.wait_recv()
    last = begin(remote(att2.at[:, its], att2.at[:, far_its], swap_send.at[1], swap_recv.at[1], partner))
    near.wait_recv()
    last.wait_recv()
    pl.when(z < 3)(row.wait_send)
    for sends, copy in jobs:
        pl.when(sends)(copy.wait_send)


def out_kernel(
    q_ref, k_ref, v_ref, w_ref, out_ref, q2, ka, va, acc, tall, back, att2, w2, pbuf, relay, near, psum, pgot, qbuf, qgot, qsum, qlast, fin, other,
    w_sem, pair_send, pair_recv, p_send, p_recv, q_send, q_recv, fin_send, fin_recv,
    *att_sems,
):
    x, y, z, core = coords()
    pair = lax.rem(y, 2)
    partner = device_at(x, y, z, 1 - core)
    across = device_at(x, y + 1 - 2 * pair, z, core)

    def beside(step):
        return device_at(lax.rem(x + step, 4), y, z, core)

    greet(
        [partner, across, beside(1), beside(2), beside(3), device_at(x, lax.rem(y + 2, 4), z, core)]
        + [device_at(x, y, lax.rem(z + d, 4), core) for d in (1, 2, 3)]
    )
    depth = q_ref.shape[1]
    copies = []

    def begin(copy):
        copy.start()
        copies.append(copy)
        return copy

    order = [c for n in range(4) for c in (4 + n, n)]
    theirs, mine = {}, {}
    for c in order:
        into = pl.ds(c * CHUNK, CHUNK)
        give = pl.ds(pl.multiple_of((1 - core) * LANES + c * CHUNK, CHUNK), CHUNK)
        keep = pl.ds(pl.multiple_of(core * LANES + c * CHUNK, CHUNK), CHUNK)
        theirs[c] = begin(
            remote(w_ref.at[:, give], w2.at[pl.ds(depth, depth), into], pair_send.at[c], pair_recv.at[c], partner)
        )
        mine[c] = pltpu.make_async_copy(w_ref.at[:, keep], w2.at[pl.ds(0, depth), into], w_sem.at[c])
        mine[c].start()
    attend(
        x, y, z, core, begin, q_ref, k_ref, v_ref, att2, q2, ka, va, acc, tall, back, *att_sems
    )

    right, left, far = lax.rem(x + 1, 4), lax.rem(x + 3, 4), lax.rem(x + 2, 4)
    pcopies, qcopies = {}, {}
    for c in order:
        mine[c].wait()
        theirs[c].wait_recv()
        block = jnp.dot(
            att2[...], w2[:, c * CHUNK : (c + 1) * CHUNK], preferred_element_type=jnp.float32
        ).astype(jnp.bfloat16)
        for row in range(8):
            piece = block[row * 48 : row * 48 + 48]
            if c < 4:
                pbuf[c, row % 4, row // 4] = piece
            else:
                qbuf[c - 4, row // 4, row % 4] = piece
        if c < 4:

            def copy(k, source, target, peer):
                return remote(source, target, p_send.at[c, k], p_recv.at[c, k], peer)

            pcopies[c] = [
                copy(0, pbuf.at[c, far, 0], relay.at[c, 0], beside(1)),
                copy(1, pbuf.at[c, far, 1], relay.at[c, 1], beside(3)),
                copy(2, pbuf.at[c, right, 1], near.at[c, 0, 1], beside(1)),
                copy(3, pbuf.at[c, left, 0], near.at[c, 1, 0], beside(3)),
                copy(4, pbuf.at[c, right, 0], near.at[c, 0, 0], beside(1)),
                copy(5, pbuf.at[c, left, 1], near.at[c, 1, 1], beside(3)),
                copy(6, psum.at[c, 1 - pair], pgot.at[c], across),
            ]
            for k in range(4):
                begin(pcopies[c][k])
        else:
            n = c - 4
            qcopies[n] = [remote(qbuf.at[n, 1 - pair], qgot.at[n], q_send.at[n, 0], q_recv.at[n, 0], across)] + [
                remote(qsum.at[n, lax.rem(x + d, 4)], qlast.at[n, d - 1], q_send.at[n, d], q_recv.at[n, d], beside(d))
                for d in (1, 2, 3)
            ]
            begin(qcopies[n][0])

    def wide(value):
        return value.astype(jnp.float32)

    def p_relay(n):
        for k, side in ((0, right), (1, left)):
            pcopies[n][k].wait_recv()
            pbuf[n, side, k] = (wide(pbuf[n, side, k]) + wide(relay[n, k])).astype(jnp.bfloat16)
            begin(pcopies[n][4 + k])

    def p_across(n):
        for k in range(2, 6):
            pcopies[n][k].wait_recv()
        for k in range(2):
            psum[n, k] = (wide(pbuf[n, x, k]) + wide(near[n, 0, k]) + wide(near[n, 1, k])).astype(jnp.bfloat16)
        begin(pcopies[n][6])

    def p_end(n):
        pcopies[n][6].wait_recv()
        fin[:, n * CHUNK : (n + 1) * CHUNK] = wide(psum[n, pair]) + wide(pgot[n])

    def q_beside(n):
        qcopies[n][0].wait_recv()
        for k in range(4):
            qsum[n, k] = (wide(qbuf[n, pair, k]) + wide(qgot[n, k])).astype(jnp.bfloat16)
        for k in (2, 1, 3):
            begin(qcopies[n][k])

    def q_end(n):
        for k in (1, 2, 3):
            qcopies[n][k].wait_recv()
        total = wide(qsum[n, x])
        for k in range(3):
            total = total + wide(qlast[n, k])
        fin[:, (4 + n) * CHUNK : (5 + n) * CHUNK] = total

    p_relay(0)
    p_relay(1)
    q_beside(0)
    p_relay(2)
    p_relay(3)
    q_beside(1)
    p_across(0)
    p_across(1)
    q_beside(2)
    p_across(2)
    p_across(3)
    q_end(0)
    q_end(1)
    q_beside(3)
    for n in range(4):
        p_end(n)
    q_end(2)
    q_end(3)

    keep, give = pl.multiple_of(core * 24, 8), pl.multiple_of((1 - core) * 24, 8)
    end = begin(remote(fin.at[pl.ds(give, 24)], other, fin_send, fin_recv, partner))
    for b in range(4):
        out_ref[:, core * 4 + b, :] = fin[pl.ds(keep, 24), b * 1024 : b * 1024 + 1024]
    end.wait_recv()
    for b in range(4):
        out_ref[:, (1 - core) * 4 + b, :] = other[:, b * 1024 : b * 1024 + 1024]
    for copy in copies:
        copy.wait_send()


def attend_and_project(q, k, v, w):
    rows, depth = q.shape
    bf, f32 = jnp.bfloat16, jnp.float32
    vmem = pl.BlockSpec(memory_space=pltpu.VMEM)

    def units(*lead):
        return pltpu.VMEM((*lead, 48, CHUNK), bf)

    def sems(*shape):
        return pltpu.SemaphoreType.DMA(shape)

    return pl.pallas_call(
        out_kernel,
        name="attend_out",
        out_shape=jax.ShapeDtypeStruct((24, 8, 1024), f32),
        in_specs=[vmem] * 3 + [pl.BlockSpec(memory_space=pl.ANY)],
        out_specs=vmem,
        scratch_shapes=[
            pltpu.VMEM((2, rows, HEAD_DIM), bf),
            pltpu.VMEM((4, 2, rows, HEAD_DIM), bf),
            pltpu.VMEM((4, 2, rows, HEAD_DIM), bf),
            pltpu.VMEM((2, rows, 2 * HEAD_DIM), f32),
            pltpu.VMEM((8 + 2 * rows, HEAD_DIM), f32),
            pltpu.VMEM((rows, HEAD_DIM), bf),
            pltpu.VMEM((rows, 2 * depth), bf),
            pltpu.VMEM((2 * depth, LANES), bf),
            units(4, 4, 2), units(4, 2), units(4, 2, 2), units(4, 2), units(4),
            units(4, 2, 4), units(4, 4), units(4, 4), units(4, 3),
            pltpu.VMEM((48, LANES), f32),
            pltpu.VMEM((24, LANES), f32),
            sems(8), sems(8), sems(8), sems(4, 7), sems(4, 7), sems(4, 4), sems(4, 4),
            pltpu.SemaphoreType.DMA, pltpu.SemaphoreType.DMA,
            sems(3), sems(3), sems(4, 2, 2), sems(4, 2, 2),
            pltpu.SemaphoreType.DMA, pltpu.SemaphoreType.DMA,
            pltpu.SemaphoreType.DMA, pltpu.SemaphoreType.DMA, sems(2), sems(2),
        ],
        compiler_params=pltpu.CompilerParams(collective_id=3, has_side_effects=True, vmem_limit_bytes=40 << 20),
    )(q, k, v, w)


PART_COLS = (640, 640, 768)
PART_ORDERS = ((0, 1, 2), (1, 2, 0), (2, 0, 1))


def rms_scale(values):
    return lax.rsqrt(jnp.mean(values * values, axis=-1, keepdims=True) + 1e-06)


def cross(left, right, left_axis, right_axis):
    return lax.dot_general(
        left, right, (((left_axis,), (right_axis,)), ((), ())), preferred_element_type=jnp.float32
    )


SPAN = 192


def local_head(h, first, inside, qkv, gcore, gq, ab):
    rows = slice(first, first + SPAN)
    bf = jnp.bfloat16
    width = gcore.shape[1]
    at = [pl.ds(pl.multiple_of(n * width + h * LOCAL_HEAD_DIM, LOCAL_HEAD_DIM), LOCAL_HEAD_DIM) for n in range(3)]
    q, k, v = (qkv[rows, part] for part in at)
    q_scale, k_scale = rms_scale(q), rms_scale(k)
    qn, kn = q * q_scale, k * k_scale
    qb, kb, vb = qn.astype(bf), kn.astype(bf), v.astype(bf)
    scale = 1.0 / math.sqrt(LOCAL_HEAD_DIM)
    e = jnp.where(inside, jnp.exp(cross(qb, kb, 1, 1) * scale), 0.0)
    p = e / jnp.sum(e, axis=-1, keepdims=True)
    pb = p.astype(bf)
    ab[rows, at[0]] = cross(pb, vb, 1, 0).astype(bf)
    back = gcore[rows, at[0]].astype(bf)
    dp = cross(back, vb, 1, 1)
    ds = (p * (dp - jnp.sum(p * dp, axis=-1, keepdims=True)) * scale).astype(bf)

    def through_rms(grad, normed, factor):
        return (factor * (grad - normed * jnp.mean(grad * normed, axis=-1, keepdims=True))).astype(bf)

    gq[rows, at[0]] = through_rms(cross(ds, kb, 1, 0), qn, q_scale)
    gq[rows, at[1]] = through_rms(cross(ds, qb, 0, 0), kn, k_scale)
    gq[rows, at[2]] = cross(pb, back, 0, 0).astype(bf)


def grads_kernel(
    emb_ref, ctx_ref, wqkv_ref, wout_ref, gb_ref, hid_ref, out_q, out_o,
    state, qkv, gcore, gq, xt, abt, xn2, gq2, ab2, gb2,
    part0, part1, part2, relay0, relay1, relay2, near0, near1, near2,
    sum0, sum1, sum2, got0, got1, got2, low0, low1, low2, last0, last1, last2,
    fin, other, pair_send, pair_recv, send1, recv1, send2, recv2, send3, recv3,
    fin_send, fin_recv,
):
    place = coords()
    core = place[3]

    def peer_along(axis, step):
        at = list(place)
        at[axis] = lax.rem(at[axis] + step, 4)
        return device_at(*at)

    partner = device_at(place[0], place[1], place[2], 1 - core)
    greet([partner] + [peer_along(axis, step) for axis in range(3) for step in (1, 2, 3)])

    rows, width = emb_ref.shape
    qh, oh = gq2.shape[1], gb2.shape[1]
    mine_q, mine_o = pl.multiple_of(core * qh, qh), pl.multiple_of(core * oh, oh)
    its_q, its_o = pl.multiple_of((1 - core) * qh, qh), pl.multiple_of((1 - core) * oh, oh)
    top, bottom = pl.ds(0, rows), pl.ds(rows, rows)
    swaps = [
        remote(xn2.at[top], xn2.at[bottom], pair_send.at[0], pair_recv.at[0], partner),
        remote(gq.at[:, pl.ds(its_q, qh)], gq2.at[bottom], pair_send.at[1], pair_recv.at[1], partner),
        remote(ab2.at[top], ab2.at[bottom], pair_send.at[2], pair_recv.at[2], partner),
        remote(gb_ref.at[:, pl.ds(its_o, oh)], gb2.at[bottom], pair_send.at[3], pair_recv.at[3], partner),
    ]
    swaps[3].start()
    state[...] = emb_ref[...].astype(jnp.float32) + ctx_ref[...].astype(jnp.bfloat16).astype(jnp.float32)
    normed = (state[...] * rms_scale(state[...])).astype(jnp.bfloat16)
    xn2[top] = normed
    swaps[0].start()
    gb2[top] = gb_ref[:, pl.ds(mine_o, oh)]

    def project(n, carry):
        at = pl.ds(pl.multiple_of(n * 512, 512), 512)
        qkv[:, at] = jnp.dot(xn2[top], wqkv_ref[:, at], preferred_element_type=jnp.float32)
        return carry

    lax.fori_loop(0, 3 * width // 512, project, 0)
    for n in range(2):
        at = slice(n * width // 2, (n + 1) * width // 2)
        gcore[:, at] = cross(gb_ref[...], wout_ref[at], 1, 1)
    row = lax.broadcasted_iota(jnp.int32, (SPAN, SPAN), 0)
    column = lax.broadcasted_iota(jnp.int32, (SPAN, SPAN), 1)
    inside = (column <= row) & (column >= row - lax.rem(row, PATCH))

    def heads(n, carry):
        for i in range(8):
            h = 8 * n + i
            for first in range(0, rows, SPAN):
                local_head(h, first, inside, qkv, gcore, gq, ab2)
        return carry

    lax.fori_loop(0, LOCAL_HEADS // 8, heads, 0)
    swaps[1].start()
    swaps[2].start()
    gq2[top] = gq[:, pl.ds(mine_q, qh)]
    xt[0] = xn2[top].T
    swaps[0].wait_recv()
    xt[1] = xn2[bottom].T

    parts = (part0, part1, part2)
    relays, nears = (relay0, relay1, relay2), (near0, near1, near2)
    sums, gots = (sum0, sum1, sum2), (got0, got1, got2)
    lows, lasts = (low0, low1, low2), (last0, last1, last2)

    def fill(part, order, left, right, columns, into):
        span = slice(*columns)
        for z in range(4):
            at = slice(z * 256, (z + 1) * 256)
            block = (
                jnp.dot(left[0, at], right[top, span], preferred_element_type=jnp.float32)
                + jnp.dot(left[1, at], right[bottom, span], preferred_element_type=jnp.float32)
            ).astype(jnp.bfloat16)
            for y in range(4):
                for x in range(4):
                    at = (x, y, z)
                    row = (y * 4 + x) * 16
                    part[
                        at[order[0]], at[order[1]], at[order[2]], :, into : into + columns[1] - columns[0]
                    ] = block[row : row + 16]

    first = []

    def stage1(k):
        order = PART_ORDERS[k]
        axis = order[0]
        me = place[axis]
        right, left, far = lax.rem(me + 1, 4), lax.rem(me + 3, 4), lax.rem(me + 2, 4)
        to_right, to_left = peer_along(axis, 1), peer_along(axis, 3)
        part, relay, near = parts[k], relays[k], nears[k]
        lo, hi = pl.ds(0, 2), pl.ds(2, 2)

        def copy(n, source, target, peer):
            return remote(source, target, send1.at[k, n], recv1.at[k, n], peer)

        copies = [
            copy(0, part.at[far, lo], relay.at[0], to_right),
            copy(1, part.at[far, hi], relay.at[1], to_left),
            copy(2, part.at[right, hi], near.at[0, hi], to_right),
            copy(3, part.at[left, lo], near.at[1, lo], to_left),
            copy(4, part.at[right, lo], near.at[0, lo], to_right),
            copy(5, part.at[left, hi], near.at[1, hi], to_left),
        ]
        for n in range(4):
            copies[n].start()
        return copies, (right, left)

    def add_relay(k, copies, sides):
        part, relay = parts[k], relays[k]
        for n in range(2):
            copies[n].wait_recv()
            for j in range(2):
                at = 2 * n + j
                part[sides[n], at] = (
                    part[sides[n], at].astype(jnp.float32) + relay[n, j].astype(jnp.float32)
                ).astype(jnp.bfloat16)
            copies[4 + n].start()

    def stage2(k, copies):
        order = PART_ORDERS[k]
        for n in range(2, 6):
            copies[n].wait_recv()
        me = place[order[0]]
        for j in range(4):
            sums[k][j] = (
                parts[k][me, j].astype(jnp.float32)
                + nears[k][0, j].astype(jnp.float32)
                + nears[k][1, j].astype(jnp.float32)
            ).astype(jnp.bfloat16)
        axis = order[1]
        at = place[axis]
        sends = []
        for d in range(1, 4):
            send = remote(
                sums[k].at[lax.rem(at + d, 4)], gots[k].at[d - 1],
                send2.at[k, d - 1], recv2.at[k, d - 1], peer_along(axis, d),
            )
            send.start()
            sends.append(send)
        return sends

    def stage3(k, copies):
        order = PART_ORDERS[k]
        for copy in copies:
            copy.wait_recv()
        me = place[order[1]]
        total = sums[k][me].astype(jnp.float32)
        for d in range(3):
            total = total + gots[k][d].astype(jnp.float32)
        lows[k][...] = total.astype(jnp.bfloat16)
        axis = order[2]
        at = place[axis]
        sends = []
        for d in range(1, 4):
            send = remote(
                lows[k].at[lax.rem(at + d, 4)], lasts[k].at[d - 1],
                send3.at[k, d - 1], recv3.at[k, d - 1], peer_along(axis, d),
            )
            send.start()
            sends.append(send)
        return sends

    def finish(k, copies):
        for copy in copies:
            copy.wait_recv()
        me = place[PART_ORDERS[k][2]]
        total = lows[k][me].astype(jnp.float32)
        for d in range(3):
            total = total + lasts[k][d].astype(jnp.float32)
        start = sum(PART_COLS[:k])
        fin[:, start : start + PART_COLS[k]] = total

    swaps[1].wait_recv()
    split = PART_COLS[0] + PART_COLS[1]
    fill(part0, PART_ORDERS[0], xt, gq2, (0, PART_COLS[0]), 0)
    first.append(stage1(0))
    fill(part1, PART_ORDERS[1], xt, gq2, (PART_COLS[0], split), 0)
    first.append(stage1(1))
    fill(part2, PART_ORDERS[2], xt, gq2, (split, qh), 0)
    abt[0] = ab2[top].T
    swaps[2].wait_recv()
    abt[1] = ab2[bottom].T
    swaps[3].wait_recv()
    fill(part2, PART_ORDERS[2], abt, gb2, (0, oh), qh - split)
    first.append(stage1(2))
    add_relay(0, *first[0])
    add_relay(1, *first[1])
    hid_ref[...] = (
        state[...] + jnp.dot(ab2[top], wout_ref[...], preferred_element_type=jnp.float32)
    ).astype(jnp.bfloat16)
    add_relay(2, *first[2])
    second = [stage2(k, first[k][0]) for k in range(3)]
    third = [stage3(k, second[k]) for k in range(3)]
    for k in range(3):
        finish(k, third[k])

    keep, give = pl.multiple_of(core * 8, 8), pl.multiple_of((1 - core) * 8, 8)
    end = remote(fin.at[pl.ds(give, 8)], other, fin_send, fin_recv, partner)
    end.start()
    out_q[:, pl.ds(mine_q, qh)] = fin[pl.ds(keep, 8), 0:qh]
    out_o[:, pl.ds(mine_o, oh)] = fin[pl.ds(keep, 8), qh : qh + oh]
    end.wait_recv()
    out_q[:, pl.ds(its_q, qh)] = other[:, 0:qh]
    out_o[:, pl.ds(its_o, oh)] = other[:, qh : qh + oh]
    for copy in swaps + [c for f in first for c in f[0]] + [c for s in second + third for c in s] + [end]:
        copy.wait_send()


def local_window(emb, context, w_qkv, w_out, cotangent):
    rows, width = emb.shape
    qw, ow = w_qkv.shape[1], w_out.shape[1]
    bf, f32 = jnp.bfloat16, jnp.float32
    vmem = pl.BlockSpec(memory_space=pltpu.VMEM)

    def each(*lead):
        return [pltpu.VMEM((*lead, 16, c), bf) for c in PART_COLS]

    def sems(*shape):
        return pltpu.SemaphoreType.DMA(shape)

    return pl.pallas_call(
        grads_kernel,
        name="local_window",
        out_shape=(
            jax.ShapeDtypeStruct((rows, width), bf),
            jax.ShapeDtypeStruct((8, qw), f32),
            jax.ShapeDtypeStruct((8, ow), f32),
        ),
        in_specs=[vmem] * 5,
        out_specs=(vmem,) * 3,
        scratch_shapes=[
            pltpu.VMEM((rows, width), f32),
            pltpu.VMEM((rows, qw), f32),
            pltpu.VMEM((rows, width), f32),
            pltpu.VMEM((rows, qw), bf),
            pltpu.VMEM((2, width, rows), bf),
            pltpu.VMEM((2, width, rows), bf),
            pltpu.VMEM((2 * rows, width), bf),
            pltpu.VMEM((2 * rows, qw // 2), bf),
            pltpu.VMEM((2 * rows, width), bf),
            pltpu.VMEM((2 * rows, ow // 2), bf),
            *each(4, 4, 4), *each(2, 2, 4), *each(2, 4, 4),
            *each(4, 4), *each(3, 4), *each(4), *each(3),
            pltpu.VMEM((16, (qw + ow) // 2), f32),
            pltpu.VMEM((8, (qw + ow) // 2), f32),
            sems(4), sems(4), sems(3, 6), sems(3, 6), sems(3, 3), sems(3, 3), sems(3, 3), sems(3, 3),
            pltpu.SemaphoreType.DMA, pltpu.SemaphoreType.DMA,
        ],
        compiler_params=pltpu.CompilerParams(collective_id=5, has_side_effects=True, vmem_limit_bytes=44 << 20),
    )(emb, context, w_qkv, w_out, cotangent)


def per_device(byte_embeds, local_embeds, global_qkv, global_out, local_qkv, local_out, cotangent):
    flat = project_patches(byte_embeds, global_qkv)
    context = attend_and_project(*flat, global_out).reshape(local_embeds.shape)
    hidden, grad_qkv, grad_out = local_window(local_embeds, context, local_qkv[0], local_out[0], cotangent)
    return (hidden, grad_qkv[None], grad_out[None])


def solution(mesh):
    in_specs = (
        P(("ctx", "tp"), None),
        P(("ctx", "tp"), None),
        P(None, None, "tp"),
        P("tp", None),
        P(),
        P(),
        P(("ctx", "tp"), None),
    )
    out_specs = (P(("ctx", "tp"), None), P(None, ("ctx", "tp"), None), P(None, ("ctx", "tp"), None))
    return jax.shard_map(
        per_device, mesh=mesh, in_specs=in_specs, out_specs=out_specs, check_vma=False
    )
```

```python
import functools
import math

import jax
import jax.numpy as jnp
from jax import lax
from jax.experimental import pallas as pl
from jax.experimental.pallas import tpu as pltpu
from jax.sharding import PartitionSpec as P

PATCH = 8
HEAD_DIM = 128
LOCAL_HEADS = 8
LOCAL_HEAD_DIM = 128


MESH = pl.DeviceIdType.MESH


def coords():
    ctx, tp = lax.axis_index("ctx"), lax.axis_index("tp")
    x, core = lax.rem(lax.div(tp, 2), 4), lax.rem(tp, 2)
    y = lax.rem(ctx, 2) * 2 + lax.div(tp, 8)
    return x, y, lax.div(ctx, 2), core


def device_at(x, y, z, core):
    return {"ctx": z * 2 + lax.div(y, 2), "tp": lax.rem(y, 2) * 8 + x * 2 + core}


def greet(peers):
    barrier = pltpu.get_barrier_semaphore()
    for peer in peers:
        pl.semaphore_signal(barrier, inc=1, device_id=peer, device_id_type=MESH)
    pl.semaphore_wait(barrier, len(peers))


def remote(source, target, send_sem, recv_sem, peer):
    return pltpu.make_async_remote_copy(
        src_ref=source,
        dst_ref=target,
        send_sem=send_sem,
        recv_sem=recv_sem,
        device_id=peer,
        device_id_type=MESH,
    )


def rms_norm(values):
    return values * lax.rsqrt(jnp.mean(values * values, axis=-1, keepdims=True) + 1e-06)


CHUNK = 512
LANES = 4096


def project_stage(
    bytes_ref, w_ref, q_ref, k_ref, v_ref, ours, theirs, wide_rows, xs, ws, acc,
    own_sem, swap_send, swap_recv, w_sem, p_send, p_recv, q_send, q_recv, f_send, f_recv,
):
    x, y, z, core = coords()
    pair = lax.rem(y, 2)
    partner = device_at(x, y, z, 1 - core)
    across = device_at(x, y + 1 - 2 * pair, z, core)

    def beside(step):
        return device_at(lax.rem(x + step, 4), y, z, core)

    own = pltpu.make_async_copy(bytes_ref, ours, own_sem)
    own.start()
    greet(
        [partner] + [device_at(lax.rem(x + d, 4), y, z, core) for d in (1, 2, 3)]
        + [device_at(x, lax.rem(y + d, 4), z, core) for d in (1, 2, 3)]
        + [device_at(x, y, lax.rem(z + d, 4), core) for d in (1, 2, 3)]
    )
    copies = []

    def begin(copy):
        copy.start()
        copies.append(copy)
        return copy

    swap = begin(remote(bytes_ref, theirs, swap_send, swap_recv, partner))
    order = [c for n in range(4) for c in (4 + n, n)]
    mine, its = [core * 8 + c for c in range(8)], [(1 - core) * 8 + c for c in range(8)]
    loads = {}
    for c in order:
        for who, g in enumerate((mine[c], its[c])):
            load = pltpu.make_async_copy(
                w_ref.at[:, pl.ds(pl.multiple_of(g * CHUNK, CHUNK), CHUNK), :], ws.at[g], w_sem.at[who, c]
            )
            load.start()
            loads[who, c] = load
    rows = ours.shape[0]
    lane_tiles = ours.shape[1] // 128

    def spread(source, side):
        at = pl.ds(pl.multiple_of(side * rows, rows), rows)
        for n in range(lane_tiles):
            wide_rows[n, at] = source[:, n * 128 : (n + 1) * 128].astype(jnp.float32)

    own.wait()
    spread(ours, core)
    acc[...] = jnp.zeros_like(acc)
    swap.wait_recv()
    spread(theirs, 1 - core)

    def entries(n, b):
        return wide_rows[n, pl.ds(b, 48, stride=PATCH), :]

    squares = jnp.zeros((48, 128), jnp.float32)
    for n in range(lane_tiles):
        for b in range(PATCH):
            squares = squares + entries(n, b) * entries(n, b)
    mean = jnp.sum(squares, axis=-1, keepdims=True) / (PATCH * lane_tiles * 128)
    scale = lax.rsqrt(mean + 1e-06)
    for side in (0, 1):

        @pl.when(core == side)
        def _():
            for c in range(8):
                for n in range(4):
                    normed = entries(c % 2 * 4 + n, side * 4 + c // 2) * scale
                    xs[side * 8 + c, pair, x, :, n * 128 : (n + 1) * 128] = normed.astype(jnp.bfloat16)

    right, left = lax.rem(x + 1, 4), lax.rem(x + 3, 4)
    pc, qc = {}, {}
    for n in range(4):
        g = mine[n]

        def copy(k, part, peer):
            return remote(part, part, p_send.at[n, k], p_recv.at[n, k], peer)

        pc[n] = [
            copy(0, xs.at[g, pair, x], across),
            copy(1, xs.at[g, :, x], beside(1)),
            copy(2, xs.at[g, :, x], beside(3)),
            copy(3, xs.at[g, 0, left], beside(1)),
            copy(4, xs.at[g, 1, right], beside(3)),
        ]
        g = mine[4 + n]

        def copy(k, part, peer):
            return remote(part, part, q_send.at[n, k], q_recv.at[n, k], peer)

        qc[n] = [copy(0, xs.at[g, pair], across)] + [copy(d, xs.at[g, pair, x], beside(d)) for d in (1, 2, 3)]
    for n in range(4):
        begin(pc[n][0])
        for d in (2, 1, 3):
            begin(qc[n][d])

    forwards = {
        c: remote(xs.at[mine[c]], xs.at[mine[c]], f_send.at[c], f_recv.at[c], partner) for c in range(8)
    }

    def multiply(who, c):
        loads[who, c].wait()
        g = (mine, its)[who][c]
        block = xs[g].reshape(acc.shape[1], CHUNK)

        def body(j, carry):
            acc[j] += jnp.dot(block, ws[g, j], preferred_element_type=jnp.float32)
            return carry

        lax.fori_loop(0, 3, body, 0)

    def p_turn(n):
        pc[n][0].wait_recv()
        begin(pc[n][1])
        begin(pc[n][2])

    def q_turn(n):
        for d in (1, 2, 3):
            qc[n][d].wait_recv()
        begin(qc[n][0])

    def p_relay(n):
        pc[n][1].wait_recv()
        begin(pc[n][3])
        pc[n][2].wait_recv()
        begin(pc[n][4])

    def p_done(n):
        pc[n][3].wait_recv()
        pc[n][4].wait_recv()
        begin(forwards[n])
        if n < 3:
            multiply(0, n)

    def q_done(n):
        qc[n][0].wait_recv()
        begin(forwards[4 + n])
        multiply(0, 4 + n)

    def other(c):
        forwards[c].wait_recv()
        multiply(1, c)

    p_turn(0)
    p_turn(1)
    q_turn(0)
    p_turn(2)
    p_turn(3)
    q_turn(1)
    q_turn(2)
    q_turn(3)
    p_relay(0)
    q_done(0)
    p_relay(1)
    other(4)
    p_done(0)
    p_relay(2)
    q_done(1)
    other(0)
    p_relay(3)
    p_done(1)
    other(5)
    q_done(2)
    other(1)
    p_done(2)
    other(6)
    p_done(3)
    q_done(3)
    multiply(0, 3)
    other(2)
    other(3)
    other(7)

    for j, out in enumerate((q_ref, k_ref, v_ref)):
        for head in range(out.shape[1] // HEAD_DIM):
            at = slice(head * HEAD_DIM, (head + 1) * HEAD_DIM)
            value = acc[j, :, at]
            if j < 2:
                value = rms_norm(value)
            out[:, at] = value.astype(jnp.bfloat16)
    return copies


def attend(
    x, y, z, core, begin, meanwhile, q_ref, k_ref, v_ref, att2, q2, ka, va, acc, tall, back,
    y_send, y_recv, z_send, z_recv, row_send, row_recv, back_send, back_recv, swap_send, swap_recv,
):
    half = lax.div(y, 2)
    partner = device_at(x, y, z, 1 - core)
    opposite = device_at(x, lax.rem(y + 2, 4), z, core)
    rows = q_ref.shape[0]
    mine = pl.ds(pl.multiple_of(half * HEAD_DIM, HEAD_DIM), HEAD_DIM)
    its = pl.ds(pl.multiple_of((1 - half) * HEAD_DIM, HEAD_DIM), HEAD_DIM)

    across = [
        begin(remote(source.at[:, its], target, y_send.at[n], y_recv.at[n], opposite))
        for n, (source, target) in enumerate(
            ((k_ref, ka.at[z, half]), (v_ref, va.at[z, half]), (q_ref, q2.at[half]))
        )
    ]

    above, below = device_at(x, y, lax.rem(z + 1, 4), core), device_at(x, y, lax.rem(z + 3, 4), core)
    stores = (ka, va)
    jobs = []

    def piece(owner, kind, which):
        return stores[kind].at[owner, half if which == 0 else 1 - half]

    def job(slot, kind, which, owner, peer, sends, fresh):
        target = piece(owner, kind, which)
        source = (k_ref, v_ref)[kind].at[:, mine] if fresh and which == 0 else target
        made = remote(source, target, z_send.at[slot, kind, which], z_recv.at[slot, kind, which], peer)
        jobs.append((sends, made))
        return made

    direct, wrap, transit, relay_k, relay_v = {}, {}, {}, {}, {}
    for which in (0, 1):
        for kind in (0, 1):
            direct[kind, which] = job(0, kind, which, z, above, z < 3, True)
            wrap[kind, which] = job(1, kind, which, z, below, z == 0, True)
        transit[which] = job(3, 1, which, z, below, z == 1, True)
        relay_k[which] = job(2, 0, which, lax.rem(z + 3, 4), above, (z == 1) | (z == 2), False)
        relay_v[which] = job(2, 1, which, 1 - lax.div(z, 3), below, (z == 0) | (z == 3), False)

    def send_fresh(kind, which):
        pl.when(z < 3)(direct[kind, which].start)
        pl.when(z == 0)(wrap[kind, which].start)
        if kind == 1:
            pl.when(z == 1)(transit[which].start)

    def send_on(which):
        @pl.when((z == 1) | (z == 2))
        def _():
            direct[0, which].wait_recv()
            relay_k[which].start()

        @pl.when(z == 3)
        def _():
            wrap[1, which].wait_recv()
            relay_v[which].start()

        @pl.when(z == 0)
        def _():
            transit[which].wait_recv()
            relay_v[which].start()

    send_fresh(0, 0)
    send_fresh(1, 0)
    ka[z, half] = k_ref[:, mine]
    va[z, half] = v_ref[:, mine]
    q2[half] = q_ref[:, mine]
    for kind in (0, 1):
        across[kind].wait_recv()
        send_fresh(kind, 1)
    across[2].wait_recv()
    send_on(0)

    tile = 128
    tiles = rows // tile
    scale = 1.0 / math.sqrt(HEAD_DIM)

    def attend_tile(block, n, keys, values, masked, first):
        s = lax.dot_general(
            q2[block, n * tile : (n + 1) * tile], keys, (((1,), (1,)), ((), ())), preferred_element_type=jnp.float32
        )
        e = jnp.exp(s * scale)
        if masked:
            row = n * tile + lax.broadcasted_iota(jnp.int32, e.shape, 0)
            e = jnp.where(lax.broadcasted_iota(jnp.int32, e.shape, 1) <= row, e, 0.0)
        sums = jnp.dot(e.astype(jnp.bfloat16), values, preferred_element_type=jnp.float32)
        at = slice(n * tile, (n + 1) * tile)
        acc[block, at] = sums if first else acc[block, at] + sums

    def with_ones(values):
        return jnp.concatenate([values, jnp.ones_like(values)], axis=1)

    for k in (0, 1):
        keys, values = ka[z, k], with_ones(va[z, k])
        for block in range(k, 2):
            for n in range(tiles):
                attend_tile(block, n, keys, values, block == k, k == 0)

    send_on(1)

    def attend_all(owner):
        def body(k, carry):
            keys, values = ka[owner, k], with_ones(va[owner, k])
            for block in (0, 1):
                for n in range(tiles):
                    attend_tile(block, n, keys, values, False, False)
            return carry

        lax.fori_loop(0, 2, body, 0)

    @pl.when(z == 3)
    def _():
        for which in (0, 1):
            wrap[0, which].wait_recv()
        attend_all(0)

    @pl.when(z >= 1)
    def _():
        for which in (0, 1):
            pl.when(z == 3)(direct[0, which].wait_recv)
            direct[1, which].wait_recv()
        attend_all(z - 1)

    @pl.when(z >= 2)
    def _():
        for which in (0, 1):
            relay_k[which].wait_recv()
            relay_v[which].wait_recv()
        attend_all(z - 2)

    for block in (0, 1):
        tall[8 + block * rows : 8 + (block + 1) * rows] = acc[block, :, 0:HEAD_DIM] / acc[block, :, HEAD_DIM:]
    row = remote(
        tall.at[pl.ds(2 * rows, 8)], tall.at[pl.ds(0, 8)], row_send, row_recv,
        device_at(x, y, lax.rem(z + 1, 4), core),
    )
    pl.when(z < 3)(row.start)
    pl.when(z > 0)(row.wait_recv)

    @pl.when(z == 0)
    def _():
        tall[0:8] = jnp.zeros((8, HEAD_DIM), jnp.float32)

    for part in (0, 1):

        @pl.when(half == part)
        def _():
            back[...] = tall[7 + (1 - part) * rows : 7 + (2 - part) * rows].astype(jnp.bfloat16)
            att2[:, part * HEAD_DIM : (part + 1) * HEAD_DIM] = tall[
                7 + part * rows : 7 + (part + 1) * rows
            ].astype(jnp.bfloat16)

    width = 2 * HEAD_DIM
    far_mine = pl.ds(pl.multiple_of(width + half * HEAD_DIM, HEAD_DIM), HEAD_DIM)
    far_its = pl.ds(pl.multiple_of(width + (1 - half) * HEAD_DIM, HEAD_DIM), HEAD_DIM)
    returned = begin(remote(back, att2.at[:, mine], back_send, back_recv, opposite))
    near = begin(remote(att2.at[:, mine], att2.at[:, far_mine], swap_send.at[0], swap_recv.at[0], partner))
    meanwhile()
    returned.wait_recv()
    last = begin(remote(att2.at[:, its], att2.at[:, far_its], swap_send.at[1], swap_recv.at[1], partner))
    near.wait_recv()
    last.wait_recv()
    pl.when(z < 3)(row.wait_send)
    for sends, copy in jobs:
        pl.when(sends)(copy.wait_send)


def output_stage(
    meanwhile, q_ref, k_ref, v_ref, w_ref, out_ref, q2, ka, va, acc, tall, back, att2, w2, pbuf, relay, near, psum, pgot, qbuf, qgot, qsum, qlast, fin, other,
    w_sem, pair_send, pair_recv, p_send, p_recv, q_send, q_recv, fin_send, fin_recv,
    *att_sems,
):
    x, y, z, core = coords()
    pair = lax.rem(y, 2)
    partner = device_at(x, y, z, 1 - core)
    across = device_at(x, y + 1 - 2 * pair, z, core)

    def beside(step):
        return device_at(lax.rem(x + step, 4), y, z, core)

    depth = q_ref.shape[1]
    copies = []

    def begin(copy):
        copy.start()
        copies.append(copy)
        return copy

    order = [c for n in range(4) for c in (4 + n, n)]
    theirs, mine = {}, {}
    for c in order:
        into = pl.ds(c * CHUNK, CHUNK)
        give = pl.ds(pl.multiple_of((1 - core) * LANES + c * CHUNK, CHUNK), CHUNK)
        keep = pl.ds(pl.multiple_of(core * LANES + c * CHUNK, CHUNK), CHUNK)
        theirs[c] = begin(
            remote(w_ref.at[:, give], w2.at[pl.ds(depth, depth), into], pair_send.at[c], pair_recv.at[c], partner)
        )
        mine[c] = pltpu.make_async_copy(w_ref.at[:, keep], w2.at[pl.ds(0, depth), into], w_sem.at[c])
        mine[c].start()
    attend(
        x, y, z, core, begin, meanwhile, q_ref, k_ref, v_ref, att2, q2, ka, va, acc, tall, back, *att_sems
    )

    right, left, far = lax.rem(x + 1, 4), lax.rem(x + 3, 4), lax.rem(x + 2, 4)
    pcopies, qcopies = {}, {}
    for c in order:
        mine[c].wait()
        theirs[c].wait_recv()
        block = jnp.dot(
            att2[...], w2[:, c * CHUNK : (c + 1) * CHUNK], preferred_element_type=jnp.float32
        ).astype(jnp.bfloat16)
        for row in range(8):
            piece = block[row * 48 : row * 48 + 48]
            if c < 4:
                pbuf[c, row % 4, row // 4] = piece
            else:
                qbuf[c - 4, row // 4, row % 4] = piece
        if c < 4:

            def copy(k, source, target, peer):
                return remote(source, target, p_send.at[c, k], p_recv.at[c, k], peer)

            pcopies[c] = [
                copy(0, pbuf.at[c, far, 0], relay.at[c, 0], beside(1)),
                copy(1, pbuf.at[c, far, 1], relay.at[c, 1], beside(3)),
                copy(2, pbuf.at[c, right, 1], near.at[c, 0, 1], beside(1)),
                copy(3, pbuf.at[c, left, 0], near.at[c, 1, 0], beside(3)),
                copy(4, pbuf.at[c, right, 0], near.at[c, 0, 0], beside(1)),
                copy(5, pbuf.at[c, left, 1], near.at[c, 1, 1], beside(3)),
                copy(6, psum.at[c, 1 - pair], pgot.at[c], across),
            ]
            for k in range(4):
                begin(pcopies[c][k])
        else:
            n = c - 4
            qcopies[n] = [remote(qbuf.at[n, 1 - pair], qgot.at[n], q_send.at[n, 0], q_recv.at[n, 0], across)] + [
                remote(qsum.at[n, lax.rem(x + d, 4)], qlast.at[n, d - 1], q_send.at[n, d], q_recv.at[n, d], beside(d))
                for d in (1, 2, 3)
            ]
            begin(qcopies[n][0])

    def wide(value):
        return value.astype(jnp.float32)

    def p_relay(n):
        for k, side in ((0, right), (1, left)):
            pcopies[n][k].wait_recv()
            pbuf[n, side, k] = (wide(pbuf[n, side, k]) + wide(relay[n, k])).astype(jnp.bfloat16)
            begin(pcopies[n][4 + k])

    def p_across(n):
        for k in range(2, 6):
            pcopies[n][k].wait_recv()
        for k in range(2):
            psum[n, k] = (wide(pbuf[n, x, k]) + wide(near[n, 0, k]) + wide(near[n, 1, k])).astype(jnp.bfloat16)
        begin(pcopies[n][6])

    def p_end(n):
        pcopies[n][6].wait_recv()
        fin[:, n * CHUNK : (n + 1) * CHUNK] = wide(psum[n, pair]) + wide(pgot[n])

    def q_beside(n):
        qcopies[n][0].wait_recv()
        for k in range(4):
            qsum[n, k] = (wide(qbuf[n, pair, k]) + wide(qgot[n, k])).astype(jnp.bfloat16)
        for k in (2, 1, 3):
            begin(qcopies[n][k])

    def q_end(n):
        for k in (1, 2, 3):
            qcopies[n][k].wait_recv()
        total = wide(qsum[n, x])
        for k in range(3):
            total = total + wide(qlast[n, k])
        fin[:, (4 + n) * CHUNK : (5 + n) * CHUNK] = total

    p_relay(0)
    p_relay(1)
    q_beside(0)
    p_relay(2)
    p_relay(3)
    q_beside(1)
    p_across(0)
    p_across(1)
    q_beside(2)
    p_across(2)
    p_across(3)
    q_end(0)
    q_end(1)
    q_beside(3)
    for n in range(4):
        p_end(n)
    q_end(2)
    q_end(3)

    keep, give = pl.multiple_of(core * 24, 8), pl.multiple_of((1 - core) * 24, 8)
    end = begin(remote(fin.at[pl.ds(give, 24)], other, fin_send, fin_recv, partner))
    for b in range(4):
        out_ref[:, core * 4 + b, :] = fin[pl.ds(keep, 24), b * 1024 : b * 1024 + 1024]
    end.wait_recv()
    for b in range(4):
        out_ref[:, (1 - core) * 4 + b, :] = other[:, b * 1024 : b * 1024 + 1024]
    return copies


PART_COLS = (640, 640, 768)
PART_ORDERS = ((0, 1, 2), (1, 2, 0), (2, 0, 1))


def rms_scale(values):
    return lax.rsqrt(jnp.mean(values * values, axis=-1, keepdims=True) + 1e-06)


def cross(left, right, left_axis, right_axis):
    return lax.dot_general(
        left, right, (((left_axis,), (right_axis,)), ((), ())), preferred_element_type=jnp.float32
    )


SPAN = 192


def local_head(group, i, first, inside, qkv, gcore, gq, ab):
    rows = slice(first, first + SPAN)
    bf = jnp.bfloat16
    width = gcore.shape[1]
    h = group * (LOCAL_HEADS // 2) + i
    at = [pl.ds(pl.multiple_of(n * width + h * LOCAL_HEAD_DIM, LOCAL_HEAD_DIM), LOCAL_HEAD_DIM) for n in range(3)]
    into = [slice(n * width // 2 + i * LOCAL_HEAD_DIM, n * width // 2 + (i + 1) * LOCAL_HEAD_DIM) for n in range(3)]
    q, k, v = (qkv[rows, part] for part in at)
    q_scale, k_scale = rms_scale(q), rms_scale(k)
    qn, kn = q * q_scale, k * k_scale
    qb, kb, vb = qn.astype(bf), kn.astype(bf), v.astype(bf)
    scale = 1.0 / math.sqrt(LOCAL_HEAD_DIM)
    e = jnp.where(inside, jnp.exp(cross(qb, kb, 1, 1) * scale), 0.0)
    p = e / jnp.sum(e, axis=-1, keepdims=True)
    pb = p.astype(bf)
    ab[rows, at[0]] = cross(pb, vb, 1, 0).astype(bf)
    back = gcore[rows, at[0]].astype(bf)
    dp = cross(back, vb, 1, 1)
    ds = (p * (dp - jnp.sum(p * dp, axis=-1, keepdims=True)) * scale).astype(bf)

    def through_rms(grad, normed, factor):
        return (factor * (grad - normed * jnp.mean(grad * normed, axis=-1, keepdims=True))).astype(bf)

    gq[group, rows, into[0]] = through_rms(cross(ds, kb, 1, 0), qn, q_scale)
    gq[group, rows, into[1]] = through_rms(cross(ds, qb, 0, 0), kn, k_scale)
    gq[group, rows, into[2]] = cross(pb, back, 0, 0).astype(bf)


def local_stage(
    emb_ref, ctx_ref, weights, gb_ref, hid_ref, out_q, out_o,
    state, qkv, gcore, gq, xt, abt, xn2, gq2, ab2, gb2,
    part0, part1, part2, relay0, relay1, relay2, near0, near1, near2,
    sum0, sum1, sum2, got0, got1, got2, low0, low1, low2, last0, last1, last2,
    fin, other, pair_send, pair_recv, send1, recv1, send2, recv2, send3, recv3,
    fin_send, fin_recv,
):
    place = coords()
    core = place[3]

    def peer_along(axis, step):
        at = list(place)
        at[axis] = lax.rem(at[axis] + step, 4)
        return device_at(*at)

    partner = device_at(place[0], place[1], place[2], 1 - core)
    rows, width = emb_ref.shape
    qh, oh = gq2.shape[1], gb2.shape[1]
    mine_o, its_o = pl.multiple_of(core * oh, oh), pl.multiple_of((1 - core) * oh, oh)
    top, bottom = pl.ds(0, rows), pl.ds(rows, rows)
    swaps = [
        remote(xn2.at[top], xn2.at[bottom], pair_send.at[0], pair_recv.at[0], partner),
        remote(gq.at[1 - core], gq2.at[bottom], pair_send.at[1], pair_recv.at[1], partner),
        remote(ab2.at[top], ab2.at[bottom], pair_send.at[2], pair_recv.at[2], partner),
        remote(gb_ref.at[:, pl.ds(its_o, oh)], gb2.at[bottom], pair_send.at[3], pair_recv.at[3], partner),
    ]
    swaps[3].start()
    state[...] = emb_ref[...].astype(jnp.float32) + ctx_ref[...].reshape(rows, width).astype(jnp.bfloat16).astype(jnp.float32)
    normed = (state[...] * rms_scale(state[...])).astype(jnp.bfloat16)
    xn2[top] = normed
    swaps[0].start()
    gb2[top] = gb_ref[:, pl.ds(mine_o, oh)]

    def product(left, n, first):
        blocks = [n, first + n]
        return sum(
            jnp.dot(
                left[top, r * 512 : (r + 1) * 512], weights[lax.div(at, 3), lax.rem(at, 3)],
                preferred_element_type=jnp.float32,
            )
            for r, at in enumerate(blocks)
        )

    def project(n, carry):
        qkv[:, pl.ds(pl.multiple_of(n * 256, 256), 256)] = product(xn2, n, 12)
        return carry

    lax.fori_loop(0, 3 * width // 256, project, 0)
    row = lax.broadcasted_iota(jnp.int32, (SPAN, SPAN), 0)
    column = lax.broadcasted_iota(jnp.int32, (SPAN, SPAN), 1)
    inside = (column <= row) & (column >= row - lax.rem(row, PATCH))

    for group in (1 - core, core):
        for i in range(LOCAL_HEADS // 2):
            for first in range(0, rows, SPAN):
                local_head(group, i, first, inside, qkv, gcore, gq, ab2)
        if group is not core:
            swaps[1].start()
    swaps[2].start()
    gq2[top] = gq[core]
    xt[0] = xn2[top].T
    swaps[0].wait_recv()
    xt[1] = xn2[bottom].T
    abt[0] = ab2[top].T

    parts = (part0, part1, part2)
    relays, nears = (relay0, relay1, relay2), (near0, near1, near2)
    sums, gots = (sum0, sum1, sum2), (got0, got1, got2)
    lows, lasts = (low0, low1, low2), (last0, last1, last2)

    def fill(part, order, left, right, columns, into):
        span = slice(*columns)
        for z in range(4):
            at = slice(z * 256, (z + 1) * 256)
            block = (
                jnp.dot(left[0, at], right[top, span], preferred_element_type=jnp.float32)
                + jnp.dot(left[1, at], right[bottom, span], preferred_element_type=jnp.float32)
            ).astype(jnp.bfloat16)
            for y in range(4):
                for x in range(4):
                    at = (x, y, z)
                    row = (y * 4 + x) * 16
                    part[
                        at[order[0]], at[order[1]], at[order[2]], :, into : into + columns[1] - columns[0]
                    ] = block[row : row + 16]

    first = []

    def stage1(k):
        order = PART_ORDERS[k]
        axis = order[0]
        me = place[axis]
        right, left, far = lax.rem(me + 1, 4), lax.rem(me + 3, 4), lax.rem(me + 2, 4)
        to_right, to_left = peer_along(axis, 1), peer_along(axis, 3)
        part, relay, near = parts[k], relays[k], nears[k]
        lo, hi = pl.ds(0, 2), pl.ds(2, 2)

        def copy(n, source, target, peer):
            return remote(source, target, send1.at[k, n], recv1.at[k, n], peer)

        copies = [
            copy(0, part.at[far, lo], relay.at[0], to_right),
            copy(1, part.at[far, hi], relay.at[1], to_left),
            copy(2, part.at[right, hi], near.at[0, hi], to_right),
            copy(3, part.at[left, lo], near.at[1, lo], to_left),
            copy(4, part.at[right, lo], near.at[0, lo], to_right),
            copy(5, part.at[left, hi], near.at[1, hi], to_left),
        ]
        for n in range(4):
            copies[n].start()
        return copies, (right, left)

    def add_relay(k, copies, sides):
        part, relay = parts[k], relays[k]
        for n in range(2):
            copies[n].wait_recv()
            for j in range(2):
                at = 2 * n + j
                part[sides[n], at] = (
                    part[sides[n], at].astype(jnp.float32) + relay[n, j].astype(jnp.float32)
                ).astype(jnp.bfloat16)
            copies[4 + n].start()

    def stage2(k, copies):
        order = PART_ORDERS[k]
        for n in range(2, 6):
            copies[n].wait_recv()
        me = place[order[0]]
        for j in range(4):
            sums[k][j] = (
                parts[k][me, j].astype(jnp.float32)
                + nears[k][0, j].astype(jnp.float32)
                + nears[k][1, j].astype(jnp.float32)
            ).astype(jnp.bfloat16)
        axis = order[1]
        at = place[axis]
        sends = []
        for d in range(1, 4):
            send = remote(
                sums[k].at[lax.rem(at + d, 4)], gots[k].at[d - 1],
                send2.at[k, d - 1], recv2.at[k, d - 1], peer_along(axis, d),
            )
            send.start()
            sends.append(send)
        return sends

    def stage3(k, copies):
        order = PART_ORDERS[k]
        for copy in copies:
            copy.wait_recv()
        me = place[order[1]]
        total = sums[k][me].astype(jnp.float32)
        for d in range(3):
            total = total + gots[k][d].astype(jnp.float32)
        lows[k][...] = total.astype(jnp.bfloat16)
        axis = order[2]
        at = place[axis]
        sends = []
        for d in range(1, 4):
            send = remote(
                lows[k].at[lax.rem(at + d, 4)], lasts[k].at[d - 1],
                send3.at[k, d - 1], recv3.at[k, d - 1], peer_along(axis, d),
            )
            send.start()
            sends.append(send)
        return sends

    def finish(k, copies):
        for copy in copies:
            copy.wait_recv()
        me = place[PART_ORDERS[k][2]]
        total = lows[k][me].astype(jnp.float32)
        for d in range(3):
            total = total + lasts[k][d].astype(jnp.float32)
        start = sum(PART_COLS[:k])
        fin[:, start : start + PART_COLS[k]] = total

    swaps[1].wait_recv()
    split = PART_COLS[0] + PART_COLS[1]
    fill(part0, PART_ORDERS[0], xt, gq2, (0, PART_COLS[0]), 0)
    first.append(stage1(0))
    fill(part1, PART_ORDERS[1], xt, gq2, (PART_COLS[0], split), 0)
    first.append(stage1(1))
    fill(part2, PART_ORDERS[2], xt, gq2, (split, qh), 0)
    swaps[2].wait_recv()
    abt[1] = ab2[bottom].T
    swaps[3].wait_recv()
    fill(part2, PART_ORDERS[2], abt, gb2, (0, oh), qh - split)
    first.append(stage1(2))
    add_relay(0, *first[0])
    add_relay(1, *first[1])
    for c in range(4):
        at = slice(c * 256, (c + 1) * 256)
        moved = sum(
            jnp.dot(
                ab2[top, r * 512 : (r + 1) * 512], weights[(24 + r * 4 + c) // 3, (24 + r * 4 + c) % 3],
                preferred_element_type=jnp.float32,
            )
            for r in range(2)
        )
        hid_ref[:, at] = (state[:, at] + moved).astype(jnp.bfloat16)
    add_relay(2, *first[2])
    second = [stage2(k, first[k][0]) for k in range(3)]
    third = [stage3(k, second[k]) for k in range(3)]
    for k in range(3):
        finish(k, third[k])

    keep, give = pl.multiple_of(core * 8, 8), pl.multiple_of((1 - core) * 8, 8)
    end = remote(fin.at[pl.ds(give, 8)], other, fin_send, fin_recv, partner)
    end.start()
    third_of = qh // 3
    for n in range(3):
        at = pl.ds(pl.multiple_of(n * width + core * third_of, third_of), third_of)
        out_q[:, at] = fin[pl.ds(keep, 8), n * third_of : (n + 1) * third_of]
    out_o[:, pl.ds(mine_o, oh)] = fin[pl.ds(keep, 8), qh : qh + oh]
    end.wait_recv()
    for n in range(3):
        at = pl.ds(pl.multiple_of(n * width + (1 - core) * third_of, third_of), third_of)
        out_q[:, at] = other[:, n * third_of : (n + 1) * third_of]
    out_o[:, pl.ds(its_o, oh)] = other[:, qh : qh + oh]
    for copy in swaps + [c for f in first for c in f[0]] + [c for s in second + third for c in s] + [end]:
        copy.wait_send()


def window_kernel(counts, *refs):
    byte_embeds, local_embeds, global_qkv, global_out, local_qkv, local_out, cotangent = refs[:7]
    hidden, grad_qkv, grad_out = refs[7:10]
    q, k, v, context, emb, cot, in_sems = refs[10:17]
    stages, at = [], 17
    for count in counts:
        stages.append(refs[at : at + count])
        at += count
    for_project, for_output, for_local = stages
    sent = project_stage(byte_embeds, global_qkv, q, k, v, *for_project)
    weights = for_project[4]
    loads = [
        pltpu.make_async_copy(local_embeds, emb, in_sems.at[32]),
        pltpu.make_async_copy(cotangent, cot, in_sems.at[33]),
    ]
    for source, blocks, first in ((local_qkv, 12, 0), (local_out, 4, 24)):
        for r in range(2):
            for c in range(blocks):
                n = first + r * blocks + c
                part = source.at[r * 512 : (r + 1) * 512, c * 256 : (c + 1) * 256]
                loads.append(pltpu.make_async_copy(part, weights.at[n // 3, n % 3], in_sems.at[n]))
    for load in loads:
        load.start()
    gcore = for_local[2]

    def meanwhile():
        for load in loads:
            load.wait()
        for r in range(2):
            gcore[:, r * 512 : (r + 1) * 512] = sum(
                cross(cot[:, c * 256 : (c + 1) * 256], weights[(24 + r * 4 + c) // 3, (24 + r * 4 + c) % 3], 1, 1)
                for c in range(4)
            )

    sent += output_stage(meanwhile, q, k, v, global_out, context, *for_output)
    local_stage(emb, context, weights, cot, hidden, grad_qkv, grad_out, *for_local)
    for copy in sent:
        copy.wait_send()


def window(byte_rows, emb, w, w_global_out, w_qkv, w_out, cotangent):
    bf, f32 = jnp.bfloat16, jnp.float32
    rows, width = byte_rows.shape
    total, cols = 2 * rows // PATCH * 8, w.shape[2]
    qw, ow = w_qkv.shape[1], w_out.shape[1]

    def sems(*shape):
        return pltpu.SemaphoreType.DMA(shape)

    def units(*lead):
        return pltpu.VMEM((*lead, 48, CHUNK), bf)

    def each(*lead):
        return [pltpu.VMEM((*lead, 16, c), bf) for c in PART_COLS]

    parts = [
        [

            pltpu.VMEM((rows, width), bf),
            pltpu.VMEM((rows, width), bf),
            pltpu.VMEM((width // 128, 2 * rows, 128), f32),
            pltpu.VMEM((16, 2, 4, 48, CHUNK), bf),
            pltpu.VMEM((16, 3, CHUNK, cols), bf),
            pltpu.VMEM((3, total, cols), f32),
            pltpu.SemaphoreType.DMA, pltpu.SemaphoreType.DMA, pltpu.SemaphoreType.DMA,
            sems(2, 8), sems(4, 5), sems(4, 5), sems(4, 4), sems(4, 4), sems(8), sems(8),
        ],
        [

            pltpu.VMEM((2, total, HEAD_DIM), bf),
            pltpu.VMEM((4, 2, total, HEAD_DIM), bf),
            pltpu.VMEM((4, 2, total, HEAD_DIM), bf),
            pltpu.VMEM((2, total, 2 * HEAD_DIM), f32),
            pltpu.VMEM((8 + 2 * total, HEAD_DIM), f32),
            pltpu.VMEM((total, HEAD_DIM), bf),
            pltpu.VMEM((total, 2 * cols), bf),
            pltpu.VMEM((2 * cols, LANES), bf),
            units(4, 4, 2), units(4, 2), units(4, 2, 2), units(4, 2), units(4),
            units(4, 2, 4), units(4, 4), units(4, 4), units(4, 3),
            pltpu.VMEM((48, LANES), f32),
            pltpu.VMEM((24, LANES), f32),
            sems(8), sems(8), sems(8), sems(4, 7), sems(4, 7), sems(4, 4), sems(4, 4),
            pltpu.SemaphoreType.DMA, pltpu.SemaphoreType.DMA,
            sems(3), sems(3), sems(4, 2, 2), sems(4, 2, 2),
            pltpu.SemaphoreType.DMA, pltpu.SemaphoreType.DMA,
            pltpu.SemaphoreType.DMA, pltpu.SemaphoreType.DMA, sems(2), sems(2),
        ],
        [

            pltpu.VMEM((rows, width), f32),
            pltpu.VMEM((rows, qw), f32),
            pltpu.VMEM((rows, width), f32),
            pltpu.VMEM((2, rows, qw // 2), bf),
            pltpu.VMEM((2, width, rows), bf),
            pltpu.VMEM((2, width, rows), bf),
            pltpu.VMEM((2 * rows, width), bf),
            pltpu.VMEM((2 * rows, qw // 2), bf),
            pltpu.VMEM((2 * rows, width), bf),
            pltpu.VMEM((2 * rows, ow // 2), bf),
            *each(4, 4, 4), *each(2, 2, 4), *each(2, 4, 4),
            *each(4, 4), *each(3, 4), *each(4), *each(3),
            pltpu.VMEM((16, (qw + ow) // 2), f32),
            pltpu.VMEM((8, (qw + ow) // 2), f32),
            sems(4), sems(4), sems(3, 6), sems(3, 6), sems(3, 3), sems(3, 3), sems(3, 3), sems(3, 3),
            pltpu.SemaphoreType.DMA, pltpu.SemaphoreType.DMA,
        ],
    ]
    inner = [pltpu.VMEM((total, cols), bf)] * 3 + [
        pltpu.VMEM((rows // PATCH, PATCH, width), f32),
        pltpu.VMEM((rows, width), bf),
        pltpu.VMEM((rows, width), bf),
        sems(34),
    ]
    vmem = pl.BlockSpec(memory_space=pltpu.VMEM)
    return pl.pallas_call(
        functools.partial(window_kernel, [len(part) for part in parts]),
        name="window",
        out_shape=(
            jax.ShapeDtypeStruct((rows, width), bf),
            jax.ShapeDtypeStruct((8, qw), f32),
            jax.ShapeDtypeStruct((8, ow), f32),
        ),
        in_specs=[pl.BlockSpec(memory_space=pl.ANY)] * 7,
        out_specs=(vmem,) * 3,
        scratch_shapes=inner + [shape for part in parts for shape in part],
        compiler_params=pltpu.CompilerParams(collective_id=1, has_side_effects=True, vmem_limit_bytes=67043328),
    )(byte_rows, emb, w, w_global_out, w_qkv, w_out, cotangent)


def per_device(byte_embeds, local_embeds, global_qkv, global_out, local_qkv, local_out, cotangent):
    hidden, grad_qkv, grad_out = window(
        byte_embeds, local_embeds, global_qkv, global_out, local_qkv[0], local_out[0], cotangent
    )
    return (hidden, grad_qkv[None], grad_out[None])


def solution(mesh):
    in_specs = (
        P(("ctx", "tp"), None),
        P(("ctx", "tp"), None),
        P(None, None, "tp"),
        P("tp", None),
        P(),
        P(),
        P(("ctx", "tp"), None),
    )
    out_specs = (P(("ctx", "tp"), None), P(None, ("ctx", "tp"), None), P(None, ("ctx", "tp"), None))
    return jax.shard_map(
        per_device, mesh=mesh, in_specs=in_specs, out_specs=out_specs, check_vma=False
    )
```

```python
import functools
import math

import jax
import jax.numpy as jnp
from jax import lax
from jax.experimental import pallas as pl
from jax.experimental.pallas import tpu as pltpu
from jax.sharding import PartitionSpec as P

PATCH = 8
HEAD_DIM = 128
LOCAL_HEADS = 8
LOCAL_HEAD_DIM = 128


MESH = pl.DeviceIdType.MESH


def coords():
    ctx, tp = lax.axis_index("ctx"), lax.axis_index("tp")
    x, core = lax.rem(lax.div(tp, 2), 4), lax.rem(tp, 2)
    y = lax.rem(ctx, 2) * 2 + lax.div(tp, 8)
    return x, y, lax.div(ctx, 2), core


def device_at(x, y, z, core):
    return {"ctx": z * 2 + lax.div(y, 2), "tp": lax.rem(y, 2) * 8 + x * 2 + core}


def greet(peers):
    barrier = pltpu.get_barrier_semaphore()
    for peer in peers:
        pl.semaphore_signal(barrier, inc=1, device_id=peer, device_id_type=MESH)
    pl.semaphore_wait(barrier, len(peers))


def remote(source, target, send_sem, recv_sem, peer):
    return pltpu.make_async_remote_copy(
        src_ref=source,
        dst_ref=target,
        send_sem=send_sem,
        recv_sem=recv_sem,
        device_id=peer,
        device_id_type=MESH,
    )


def rms_norm(values):
    return values * lax.rsqrt(jnp.mean(values * values, axis=-1, keepdims=True) + 1e-06)


CHUNK = 512
LANES = 4096


def project_stage(
    bytes_ref, w_ref, q_ref, k_ref, v_ref, ours, theirs, wide_rows, xs, ws, acc,
    own_sem, swap_send, swap_recv, w_sem, p_send, p_recv, q_send, q_recv, f_send, f_recv,
):
    x, y, z, core = coords()
    pair = lax.rem(y, 2)
    partner = device_at(x, y, z, 1 - core)
    across = device_at(x, y + 1 - 2 * pair, z, core)

    def beside(step):
        return device_at(lax.rem(x + step, 4), y, z, core)

    own = pltpu.make_async_copy(bytes_ref, ours, own_sem)
    own.start()
    greet(
        [partner] + [device_at(lax.rem(x + d, 4), y, z, core) for d in (1, 2, 3)]
        + [device_at(x, lax.rem(y + d, 4), z, core) for d in (1, 2, 3)]
        + [device_at(x, y, lax.rem(z + d, 4), core) for d in (1, 2, 3)]
    )
    copies = []

    def begin(copy):
        copy.start()
        copies.append(copy)
        return copy

    swap = begin(remote(bytes_ref, theirs, swap_send, swap_recv, partner))
    order = [c for n in range(4) for c in (4 + n, n)]
    mine, its = [core * 8 + c for c in range(8)], [(1 - core) * 8 + c for c in range(8)]
    loads = {}
    for c in order:
        for who, g in enumerate((mine[c], its[c])):
            load = pltpu.make_async_copy(
                w_ref.at[:, pl.ds(pl.multiple_of(g * CHUNK, CHUNK), CHUNK), :], ws.at[g], w_sem.at[who, c]
            )
            load.start()
            loads[who, c] = load
    rows = ours.shape[0]
    lane_tiles = ours.shape[1] // 128

    def spread(source, side):
        at = pl.ds(pl.multiple_of(side * rows, rows), rows)
        for n in range(lane_tiles):
            wide_rows[n, at] = source[:, n * 128 : (n + 1) * 128].astype(jnp.float32)

    own.wait()
    spread(ours, core)
    acc[...] = jnp.zeros_like(acc)
    swap.wait_recv()
    spread(theirs, 1 - core)

    def entries(n, b):
        return wide_rows[n, pl.ds(b, 48, stride=PATCH), :]

    squares = jnp.zeros((48, 128), jnp.float32)
    for n in range(lane_tiles):
        for b in range(PATCH):
            squares = squares + entries(n, b) * entries(n, b)
    mean = jnp.sum(squares, axis=-1, keepdims=True) / (PATCH * lane_tiles * 128)
    scale = lax.rsqrt(mean + 1e-06)
    for side in (0, 1):

        @pl.when(core == side)
        def _():
            for c in range(8):
                for n in range(4):
                    normed = entries(c % 2 * 4 + n, side * 4 + c // 2) * scale
                    xs[side * 8 + c, pair, x, :, n * 128 : (n + 1) * 128] = normed.astype(jnp.bfloat16)

    right, left = lax.rem(x + 1, 4), lax.rem(x + 3, 4)
    pc, qc = {}, {}
    for n in range(4):
        g = mine[n]

        def copy(k, part, peer):
            return remote(part, part, p_send.at[n, k], p_recv.at[n, k], peer)

        pc[n] = [
            copy(0, xs.at[g, pair, x], across),
            copy(1, xs.at[g, :, x], beside(1)),
            copy(2, xs.at[g, :, x], beside(3)),
            copy(3, xs.at[g, 0, left], beside(1)),
            copy(4, xs.at[g, 1, right], beside(3)),
        ]
        g = mine[4 + n]

        def copy(k, part, peer):
            return remote(part, part, q_send.at[n, k], q_recv.at[n, k], peer)

        qc[n] = [copy(0, xs.at[g, pair], across)] + [copy(d, xs.at[g, pair, x], beside(d)) for d in (1, 2, 3)]
    for n in range(4):
        begin(pc[n][0])
        for d in (2, 1, 3):
            begin(qc[n][d])

    forwards = {
        c: remote(xs.at[mine[c]], xs.at[mine[c]], f_send.at[c], f_recv.at[c], partner) for c in range(8)
    }

    def multiply(who, c):
        loads[who, c].wait()
        g = (mine, its)[who][c]
        block = xs[g].reshape(acc.shape[1], CHUNK)

        def body(j, carry):
            acc[j] += jnp.dot(block, ws[g, j], preferred_element_type=jnp.float32)
            return carry

        lax.fori_loop(0, 3, body, 0)

    def p_turn(n):
        pc[n][0].wait_recv()
        begin(pc[n][1])
        begin(pc[n][2])

    def q_turn(n):
        for d in (1, 2, 3):
            qc[n][d].wait_recv()
        begin(qc[n][0])

    def p_relay(n):
        pc[n][1].wait_recv()
        begin(pc[n][3])
        pc[n][2].wait_recv()
        begin(pc[n][4])

    def p_done(n):
        pc[n][3].wait_recv()
        pc[n][4].wait_recv()
        begin(forwards[n])
        if n < 3:
            multiply(0, n)

    def q_done(n):
        qc[n][0].wait_recv()
        begin(forwards[4 + n])
        multiply(0, 4 + n)

    def other(c):
        forwards[c].wait_recv()
        multiply(1, c)

    p_turn(0)
    p_turn(1)
    q_turn(0)
    p_turn(2)
    p_turn(3)
    q_turn(1)
    q_turn(2)
    q_turn(3)
    p_relay(0)
    q_done(0)
    p_relay(1)
    other(4)
    p_done(0)
    p_relay(2)
    q_done(1)
    other(0)
    p_relay(3)
    p_done(1)
    other(5)
    q_done(2)
    other(1)
    p_done(2)
    other(6)
    p_done(3)
    q_done(3)
    multiply(0, 3)
    other(2)
    other(3)
    other(7)

    for j, out in enumerate((q_ref, k_ref, v_ref)):
        for head in range(out.shape[1] // HEAD_DIM):
            at = slice(head * HEAD_DIM, (head + 1) * HEAD_DIM)
            value = acc[j, :, at]
            if j < 2:
                value = rms_norm(value)
            out[:, at] = value.astype(jnp.bfloat16)
    return copies


def attend(
    x, y, z, core, begin, meanwhile, q_ref, k_ref, v_ref, att2, q2, ka, va, acc, tall, back,
    y_send, y_recv, z_send, z_recv, row_send, row_recv, back_send, back_recv, swap_send, swap_recv,
):
    half = lax.div(y, 2)
    partner = device_at(x, y, z, 1 - core)
    opposite = device_at(x, lax.rem(y + 2, 4), z, core)
    rows = q_ref.shape[0]
    mine = pl.ds(pl.multiple_of(half * HEAD_DIM, HEAD_DIM), HEAD_DIM)
    its = pl.ds(pl.multiple_of((1 - half) * HEAD_DIM, HEAD_DIM), HEAD_DIM)

    across = [
        begin(remote(source.at[:, its], target, y_send.at[n], y_recv.at[n], opposite))
        for n, (source, target) in enumerate(
            ((k_ref, ka.at[z, half]), (v_ref, va.at[z, half]), (q_ref, q2.at[half]))
        )
    ]

    above, below = device_at(x, y, lax.rem(z + 1, 4), core), device_at(x, y, lax.rem(z + 3, 4), core)
    stores = (ka, va)
    jobs = []

    def piece(owner, kind, which):
        return stores[kind].at[owner, half if which == 0 else 1 - half]

    def job(slot, kind, which, owner, peer, sends, fresh):
        target = piece(owner, kind, which)
        source = (k_ref, v_ref)[kind].at[:, mine] if fresh and which == 0 else target
        made = remote(source, target, z_send.at[slot, kind, which], z_recv.at[slot, kind, which], peer)
        jobs.append((sends, made))
        return made

    direct, wrap, transit, relay_k, relay_v = {}, {}, {}, {}, {}
    for which in (0, 1):
        for kind in (0, 1):
            direct[kind, which] = job(0, kind, which, z, above, z < 3, True)
            wrap[kind, which] = job(1, kind, which, z, below, z == 0, True)
        transit[which] = job(3, 1, which, z, below, z == 1, True)
        relay_k[which] = job(2, 0, which, lax.rem(z + 3, 4), above, (z == 1) | (z == 2), False)
        relay_v[which] = job(2, 1, which, 1 - lax.div(z, 3), below, (z == 0) | (z == 3), False)

    def send_fresh(kind, which):
        pl.when(z < 3)(direct[kind, which].start)
        pl.when(z == 0)(wrap[kind, which].start)
        if kind == 1:
            pl.when(z == 1)(transit[which].start)

    def send_on(which):
        @pl.when((z == 1) | (z == 2))
        def _():
            direct[0, which].wait_recv()
            relay_k[which].start()

        @pl.when(z == 3)
        def _():
            wrap[1, which].wait_recv()
            relay_v[which].start()

        @pl.when(z == 0)
        def _():
            transit[which].wait_recv()
            relay_v[which].start()

    send_fresh(0, 0)
    send_fresh(1, 0)
    ka[z, half] = k_ref[:, mine]
    va[z, half] = v_ref[:, mine]
    q2[half] = q_ref[:, mine]
    for kind in (0, 1):
        across[kind].wait_recv()
        send_fresh(kind, 1)
    across[2].wait_recv()
    send_on(0)

    tile = 128
    tiles = rows // tile
    scale = 1.0 / math.sqrt(HEAD_DIM)

    def attend_tile(block, n, keys, values, masked, first):
        s = lax.dot_general(
            q2[block, n * tile : (n + 1) * tile], keys, (((1,), (1,)), ((), ())), preferred_element_type=jnp.float32
        )
        e = jnp.exp(s * scale)
        if masked:
            row = n * tile + lax.broadcasted_iota(jnp.int32, e.shape, 0)
            e = jnp.where(lax.broadcasted_iota(jnp.int32, e.shape, 1) <= row, e, 0.0)
        sums = jnp.dot(e.astype(jnp.bfloat16), values, preferred_element_type=jnp.float32)
        at = slice(n * tile, (n + 1) * tile)
        acc[block, at] = sums if first else acc[block, at] + sums

    def with_ones(values):
        return jnp.concatenate([values, jnp.ones_like(values)], axis=1)

    for k in (0, 1):
        keys, values = ka[z, k], with_ones(va[z, k])
        for block in range(k, 2):
            for n in range(tiles):
                attend_tile(block, n, keys, values, block == k, k == 0)

    send_on(1)

    def attend_all(owner):
        def body(k, carry):
            keys, values = ka[owner, k], with_ones(va[owner, k])
            for block in (0, 1):
                for n in range(tiles):
                    attend_tile(block, n, keys, values, False, False)
            return carry

        lax.fori_loop(0, 2, body, 0)

    @pl.when(z == 3)
    def _():
        for which in (0, 1):
            wrap[0, which].wait_recv()
        attend_all(0)

    @pl.when(z >= 1)
    def _():
        for which in (0, 1):
            pl.when(z == 3)(direct[0, which].wait_recv)
            direct[1, which].wait_recv()
        attend_all(z - 1)

    @pl.when(z >= 2)
    def _():
        for which in (0, 1):
            relay_k[which].wait_recv()
            relay_v[which].wait_recv()
        attend_all(z - 2)

    for block in (0, 1):
        tall[8 + block * rows : 8 + (block + 1) * rows] = acc[block, :, 0:HEAD_DIM] / acc[block, :, HEAD_DIM:]
    row = remote(
        tall.at[pl.ds(2 * rows, 8)], tall.at[pl.ds(0, 8)], row_send, row_recv,
        device_at(x, y, lax.rem(z + 1, 4), core),
    )
    pl.when(z < 3)(row.start)
    pl.when(z > 0)(row.wait_recv)

    @pl.when(z == 0)
    def _():
        tall[0:8] = jnp.zeros((8, HEAD_DIM), jnp.float32)

    for part in (0, 1):

        @pl.when(half == part)
        def _():
            back[...] = tall[7 + (1 - part) * rows : 7 + (2 - part) * rows].astype(jnp.bfloat16)
            att2[:, part * HEAD_DIM : (part + 1) * HEAD_DIM] = tall[
                7 + part * rows : 7 + (part + 1) * rows
            ].astype(jnp.bfloat16)

    width = 2 * HEAD_DIM
    far_mine = pl.ds(pl.multiple_of(width + half * HEAD_DIM, HEAD_DIM), HEAD_DIM)
    far_its = pl.ds(pl.multiple_of(width + (1 - half) * HEAD_DIM, HEAD_DIM), HEAD_DIM)
    returned = begin(remote(back, att2.at[:, mine], back_send, back_recv, opposite))
    near = begin(remote(att2.at[:, mine], att2.at[:, far_mine], swap_send.at[0], swap_recv.at[0], partner))
    meanwhile()
    returned.wait_recv()
    last = begin(remote(att2.at[:, its], att2.at[:, far_its], swap_send.at[1], swap_recv.at[1], partner))
    near.wait_recv()
    last.wait_recv()
    pl.when(z < 3)(row.wait_send)
    for sends, copy in jobs:
        pl.when(sends)(copy.wait_send)


def output_stage(
    meanwhile, q_ref, k_ref, v_ref, w_ref, out_ref, q2, ka, va, acc, tall, back, att2, w2, pbuf, relay, near, psum, pgot, qbuf, qgot, qsum, qlast, fin, other,
    w_sem, pair_send, pair_recv, p_send, p_recv, q_send, q_recv, fin_send, fin_recv,
    *att_sems,
):
    x, y, z, core = coords()
    pair = lax.rem(y, 2)
    partner = device_at(x, y, z, 1 - core)
    across = device_at(x, y + 1 - 2 * pair, z, core)

    def beside(step):
        return device_at(lax.rem(x + step, 4), y, z, core)

    depth = q_ref.shape[1]
    copies = []

    def begin(copy):
        copy.start()
        copies.append(copy)
        return copy

    order = [c for n in range(4) for c in (4 + n, n)]
    theirs, mine = {}, {}
    for c in order:
        into = pl.ds(c * CHUNK, CHUNK)
        give = pl.ds(pl.multiple_of((1 - core) * LANES + c * CHUNK, CHUNK), CHUNK)
        keep = pl.ds(pl.multiple_of(core * LANES + c * CHUNK, CHUNK), CHUNK)
        theirs[c] = begin(
            remote(w_ref.at[:, give], w2.at[pl.ds(depth, depth), into], pair_send.at[c], pair_recv.at[c], partner)
        )
        mine[c] = pltpu.make_async_copy(w_ref.at[:, keep], w2.at[pl.ds(0, depth), into], w_sem.at[c])
        mine[c].start()
    attend(
        x, y, z, core, begin, meanwhile, q_ref, k_ref, v_ref, att2, q2, ka, va, acc, tall, back, *att_sems
    )

    right, left, far = lax.rem(x + 1, 4), lax.rem(x + 3, 4), lax.rem(x + 2, 4)
    pcopies, qcopies = {}, {}
    for c in order:
        mine[c].wait()
        theirs[c].wait_recv()
        block = jnp.dot(
            att2[...], w2[:, c * CHUNK : (c + 1) * CHUNK], preferred_element_type=jnp.float32
        ).astype(jnp.bfloat16)
        for row in range(8):
            piece = block[row * 48 : row * 48 + 48]
            if c < 4:
                pbuf[c, row % 4, row // 4] = piece
            else:
                qbuf[c - 4, row // 4, row % 4] = piece
        if c < 4:

            def copy(k, source, target, peer):
                return remote(source, target, p_send.at[c, k], p_recv.at[c, k], peer)

            pcopies[c] = [
                copy(0, pbuf.at[c, far, 0], relay.at[c, 0], beside(1)),
                copy(1, pbuf.at[c, far, 1], relay.at[c, 1], beside(3)),
                copy(2, pbuf.at[c, right, 1], near.at[c, 0, 1], beside(1)),
                copy(3, pbuf.at[c, left, 0], near.at[c, 1, 0], beside(3)),
                copy(4, pbuf.at[c, right, 0], near.at[c, 0, 0], beside(1)),
                copy(5, pbuf.at[c, left, 1], near.at[c, 1, 1], beside(3)),
                copy(6, psum.at[c, 1 - pair], pgot.at[c], across),
            ]
            for k in range(4):
                begin(pcopies[c][k])
        else:
            n = c - 4
            qcopies[n] = [remote(qbuf.at[n, 1 - pair], qgot.at[n], q_send.at[n, 0], q_recv.at[n, 0], across)] + [
                remote(qsum.at[n, lax.rem(x + d, 4)], qlast.at[n, d - 1], q_send.at[n, d], q_recv.at[n, d], beside(d))
                for d in (1, 2, 3)
            ]
            begin(qcopies[n][0])

    def wide(value):
        return value.astype(jnp.float32)

    def p_relay(n):
        for k, side in ((0, right), (1, left)):
            pcopies[n][k].wait_recv()
            pbuf[n, side, k] = (wide(pbuf[n, side, k]) + wide(relay[n, k])).astype(jnp.bfloat16)
            begin(pcopies[n][4 + k])

    def p_across(n):
        for k in range(2, 6):
            pcopies[n][k].wait_recv()
        for k in range(2):
            psum[n, k] = (wide(pbuf[n, x, k]) + wide(near[n, 0, k]) + wide(near[n, 1, k])).astype(jnp.bfloat16)
        begin(pcopies[n][6])

    def p_end(n):
        pcopies[n][6].wait_recv()
        fin[:, n * CHUNK : (n + 1) * CHUNK] = wide(psum[n, pair]) + wide(pgot[n])

    def q_beside(n):
        qcopies[n][0].wait_recv()
        for k in range(4):
            qsum[n, k] = (wide(qbuf[n, pair, k]) + wide(qgot[n, k])).astype(jnp.bfloat16)
        for k in (2, 1, 3):
            begin(qcopies[n][k])

    def q_end(n):
        for k in (1, 2, 3):
            qcopies[n][k].wait_recv()
        total = wide(qsum[n, x])
        for k in range(3):
            total = total + wide(qlast[n, k])
        fin[:, (4 + n) * CHUNK : (5 + n) * CHUNK] = total

    p_relay(0)
    p_relay(1)
    q_beside(0)
    p_relay(2)
    p_relay(3)
    q_beside(1)
    p_across(0)
    p_across(1)
    q_beside(2)
    p_across(2)
    p_across(3)
    q_end(0)
    q_end(1)
    q_beside(3)
    for n in range(4):
        p_end(n)
    q_end(2)
    q_end(3)

    keep, give = pl.multiple_of(core * 24, 8), pl.multiple_of((1 - core) * 24, 8)
    end = begin(remote(fin.at[pl.ds(give, 24)], other, fin_send, fin_recv, partner))
    for b in range(4):
        out_ref[:, core * 4 + b, :] = fin[pl.ds(keep, 24), b * 1024 : b * 1024 + 1024]
    end.wait_recv()
    for b in range(4):
        out_ref[:, (1 - core) * 4 + b, :] = other[:, b * 1024 : b * 1024 + 1024]
    return copies


PART_COLS = (768, 640, 640)
PART_ORDERS = ((0, 1, 2), (1, 2, 0), (2, 0, 1))


def rms_scale(values):
    return lax.rsqrt(jnp.mean(values * values, axis=-1, keepdims=True) + 1e-06)


def cross(left, right, left_axis, right_axis):
    return lax.dot_general(
        left, right, (((left_axis,), (right_axis,)), ((), ())), preferred_element_type=jnp.float32
    )


SPAN = 192


def local_head(group, i, first, inside, qkv, gcore, gq, ab):
    rows = slice(first, first + SPAN)
    bf = jnp.bfloat16
    width = gcore.shape[1]
    h = group * (LOCAL_HEADS // 2) + i
    at = [pl.ds(pl.multiple_of(n * width + h * LOCAL_HEAD_DIM, LOCAL_HEAD_DIM), LOCAL_HEAD_DIM) for n in range(3)]
    into = [slice(n * width // 2 + i * LOCAL_HEAD_DIM, n * width // 2 + (i + 1) * LOCAL_HEAD_DIM) for n in range(3)]
    q, k, v = (qkv[rows, part] for part in at)
    q_scale, k_scale = rms_scale(q), rms_scale(k)
    qn, kn = q * q_scale, k * k_scale
    qb, kb, vb = qn.astype(bf), kn.astype(bf), v.astype(bf)
    scale = 1.0 / math.sqrt(LOCAL_HEAD_DIM)
    e = jnp.where(inside, jnp.exp(cross(qb, kb, 1, 1) * scale), 0.0)
    p = e / jnp.sum(e, axis=-1, keepdims=True)
    pb = p.astype(bf)
    ab[rows, at[0]] = cross(pb, vb, 1, 0).astype(bf)
    back = gcore[rows, at[0]].astype(bf)
    dp = cross(back, vb, 1, 1)
    ds = (p * (dp - jnp.sum(p * dp, axis=-1, keepdims=True)) * scale).astype(bf)

    def through_rms(grad, normed, factor):
        return (factor * (grad - normed * jnp.mean(grad * normed, axis=-1, keepdims=True))).astype(bf)

    gq[group, rows, into[0]] = through_rms(cross(ds, kb, 1, 0), qn, q_scale)
    gq[group, rows, into[1]] = through_rms(cross(ds, qb, 0, 0), kn, k_scale)
    gq[group, rows, into[2]] = cross(pb, back, 0, 0).astype(bf)


def local_stage(
    emb_ref, ctx_ref, weights, gb_ref, hid_ref, out_q, out_o,
    state, qkv, gcore, gq, xt, abt, xn2, gq2, ab2, gb2,
    part0, part1, part2, relay0, relay1, relay2, near0, near1, near2,
    sum0, sum1, sum2, got0, got1, got2, low0, low1, low2, last0, last1, last2,
    fin, other, pair_send, pair_recv, send1, recv1, send2, recv2, send3, recv3,
    fin_send, fin_recv,
):
    place = coords()
    core = place[3]

    def peer_along(axis, step):
        at = list(place)
        at[axis] = lax.rem(at[axis] + step, 4)
        return device_at(*at)

    partner = device_at(place[0], place[1], place[2], 1 - core)
    rows, width = emb_ref.shape
    qh, oh = gq2.shape[1], gb2.shape[1]
    mine_o, its_o = pl.multiple_of(core * oh, oh), pl.multiple_of((1 - core) * oh, oh)
    top, bottom = pl.ds(0, rows), pl.ds(rows, rows)
    swaps = [
        remote(xn2.at[top], xn2.at[bottom], pair_send.at[0], pair_recv.at[0], partner),
        remote(gq.at[1 - core], gq2.at[bottom], pair_send.at[1], pair_recv.at[1], partner),
        remote(ab2.at[top], ab2.at[bottom], pair_send.at[2], pair_recv.at[2], partner),
        remote(gb_ref.at[:, pl.ds(its_o, oh)], gb2.at[bottom], pair_send.at[3], pair_recv.at[3], partner),
    ]
    swaps[3].start()
    state[...] = emb_ref[...].astype(jnp.float32) + ctx_ref[...].reshape(rows, width).astype(jnp.bfloat16).astype(jnp.float32)
    normed = (state[...] * rms_scale(state[...])).astype(jnp.bfloat16)
    xn2[top] = normed
    swaps[0].start()
    gb2[top] = gb_ref[:, pl.ds(mine_o, oh)]

    def product(left, n, first):
        blocks = [n, first + n]
        return sum(
            jnp.dot(
                left[top, r * 512 : (r + 1) * 512], weights[lax.div(at, 3), lax.rem(at, 3)],
                preferred_element_type=jnp.float32,
            )
            for r, at in enumerate(blocks)
        )

    def project(n, carry):
        qkv[:, pl.ds(pl.multiple_of(n * 256, 256), 256)] = product(xn2, n, 12)
        return carry

    lax.fori_loop(0, 3 * width // 256, project, 0)
    row = lax.broadcasted_iota(jnp.int32, (SPAN, SPAN), 0)
    column = lax.broadcasted_iota(jnp.int32, (SPAN, SPAN), 1)
    inside = (column <= row) & (column >= row - lax.rem(row, PATCH))

    for group in (1 - core, core):
        for i in range(LOCAL_HEADS // 2):
            for first in range(0, rows, SPAN):
                local_head(group, i, first, inside, qkv, gcore, gq, ab2)
        if group is not core:
            swaps[1].start()
    swaps[2].start()
    gq2[top] = gq[core]
    xt[0] = xn2[top].T
    swaps[0].wait_recv()
    xt[1] = xn2[bottom].T
    abt[0] = ab2[top].T

    parts = (part0, part1, part2)
    relays, nears = (relay0, relay1, relay2), (near0, near1, near2)
    sums, gots = (sum0, sum1, sum2), (got0, got1, got2)
    lows, lasts = (low0, low1, low2), (last0, last1, last2)

    def fill(part, order, left, right, columns, into):
        span = slice(*columns)
        for z in range(4):
            at = slice(z * 256, (z + 1) * 256)
            block = (
                jnp.dot(left[0, at], right[top, span], preferred_element_type=jnp.float32)
                + jnp.dot(left[1, at], right[bottom, span], preferred_element_type=jnp.float32)
            ).astype(jnp.bfloat16)
            for y in range(4):
                for x in range(4):
                    at = (x, y, z)
                    row = (y * 4 + x) * 16
                    part[
                        at[order[0]], at[order[1]], at[order[2]], :, into : into + columns[1] - columns[0]
                    ] = block[row : row + 16]

    first = []

    def stage1(k):
        order = PART_ORDERS[k]
        axis = order[0]
        me = place[axis]
        right, left, far = lax.rem(me + 1, 4), lax.rem(me + 3, 4), lax.rem(me + 2, 4)
        to_right, to_left = peer_along(axis, 1), peer_along(axis, 3)
        part, relay, near = parts[k], relays[k], nears[k]
        lo, hi = pl.ds(0, 2), pl.ds(2, 2)

        def copy(n, source, target, peer):
            return remote(source, target, send1.at[k, n], recv1.at[k, n], peer)

        copies = [
            copy(0, part.at[far, lo], relay.at[0], to_right),
            copy(1, part.at[far, hi], relay.at[1], to_left),
            copy(2, part.at[right, hi], near.at[0, hi], to_right),
            copy(3, part.at[left, lo], near.at[1, lo], to_left),
            copy(4, part.at[right, lo], near.at[0, lo], to_right),
            copy(5, part.at[left, hi], near.at[1, hi], to_left),
        ]
        for n in range(4):
            copies[n].start()
        return copies, (right, left)

    def add_relay(k, copies, sides):
        part, relay = parts[k], relays[k]
        for n in range(2):
            copies[n].wait_recv()
            for j in range(2):
                at = 2 * n + j
                part[sides[n], at] = (
                    part[sides[n], at].astype(jnp.float32) + relay[n, j].astype(jnp.float32)
                ).astype(jnp.bfloat16)
            copies[4 + n].start()

    def stage2(k, copies):
        order = PART_ORDERS[k]
        for n in range(2, 6):
            copies[n].wait_recv()
        me = place[order[0]]
        for j in range(4):
            sums[k][j] = (
                parts[k][me, j].astype(jnp.float32)
                + nears[k][0, j].astype(jnp.float32)
                + nears[k][1, j].astype(jnp.float32)
            ).astype(jnp.bfloat16)
        axis = order[1]
        at = place[axis]
        sends = []
        for d in range(1, 4):
            send = remote(
                sums[k].at[lax.rem(at + d, 4)], gots[k].at[d - 1],
                send2.at[k, d - 1], recv2.at[k, d - 1], peer_along(axis, d),
            )
            send.start()
            sends.append(send)
        return sends

    def stage3(k, copies):
        order = PART_ORDERS[k]
        for copy in copies:
            copy.wait_recv()
        me = place[order[1]]
        total = sums[k][me].astype(jnp.float32)
        for d in range(3):
            total = total + gots[k][d].astype(jnp.float32)
        lows[k][...] = total.astype(jnp.bfloat16)
        axis = order[2]
        at = place[axis]
        sends = []
        for d in range(1, 4):
            send = remote(
                lows[k].at[lax.rem(at + d, 4)], lasts[k].at[d - 1],
                send3.at[k, d - 1], recv3.at[k, d - 1], peer_along(axis, d),
            )
            send.start()
            sends.append(send)
        return sends

    def finish(k, copies):
        for copy in copies:
            copy.wait_recv()
        me = place[PART_ORDERS[k][2]]
        total = lows[k][me].astype(jnp.float32)
        for d in range(3):
            total = total + lasts[k][d].astype(jnp.float32)
        start = sum(PART_COLS[:k])
        fin[:, start : start + PART_COLS[k]] = total

    swaps[1].wait_recv()
    split = PART_COLS[0] + PART_COLS[1]
    fill(part0, PART_ORDERS[0], xt, gq2, (0, PART_COLS[0]), 0)
    first.append(stage1(0))
    fill(part1, PART_ORDERS[1], xt, gq2, (PART_COLS[0], split), 0)
    first.append(stage1(1))
    fill(part2, PART_ORDERS[2], xt, gq2, (split, qh), 0)
    swaps[2].wait_recv()
    abt[1] = ab2[bottom].T
    swaps[3].wait_recv()
    fill(part2, PART_ORDERS[2], abt, gb2, (0, oh), qh - split)
    first.append(stage1(2))
    add_relay(0, *first[0])
    add_relay(1, *first[1])
    add_relay(2, *first[2])
    for c in range(4):
        at = slice(c * 256, (c + 1) * 256)
        moved = sum(
            jnp.dot(
                ab2[top, r * 512 : (r + 1) * 512], weights[(24 + r * 4 + c) // 3, (24 + r * 4 + c) % 3],
                preferred_element_type=jnp.float32,
            )
            for r in range(2)
        )
        hid_ref[:, at] = (state[:, at] + moved).astype(jnp.bfloat16)
    second = [stage2(k, first[k][0]) for k in range(3)]
    third = [stage3(k, second[k]) for k in range(3)]
    for k in range(3):
        finish(k, third[k])

    keep, give = pl.multiple_of(core * 8, 8), pl.multiple_of((1 - core) * 8, 8)
    end = remote(fin.at[pl.ds(give, 8)], other, fin_send, fin_recv, partner)
    end.start()
    third_of = qh // 3
    for n in range(3):
        at = pl.ds(pl.multiple_of(n * width + core * third_of, third_of), third_of)
        out_q[:, at] = fin[pl.ds(keep, 8), n * third_of : (n + 1) * third_of]
    out_o[:, pl.ds(mine_o, oh)] = fin[pl.ds(keep, 8), qh : qh + oh]
    end.wait_recv()
    for n in range(3):
        at = pl.ds(pl.multiple_of(n * width + (1 - core) * third_of, third_of), third_of)
        out_q[:, at] = other[:, n * third_of : (n + 1) * third_of]
    out_o[:, pl.ds(its_o, oh)] = other[:, qh : qh + oh]
    for copy in swaps + [c for f in first for c in f[0]] + [c for s in second + third for c in s] + [end]:
        copy.wait_send()


def window_kernel(counts, *refs):
    byte_embeds, local_embeds, global_qkv, global_out, local_qkv, local_out, cotangent = refs[:7]
    hidden, grad_qkv, grad_out = refs[7:10]
    q, k, v, context, emb, cot, in_sems = refs[10:17]
    stages, at = [], 17
    for count in counts:
        stages.append(refs[at : at + count])
        at += count
    for_project, for_output, for_local = stages
    sent = project_stage(byte_embeds, global_qkv, q, k, v, *for_project)
    weights = for_project[4]
    loads = [
        pltpu.make_async_copy(local_embeds, emb, in_sems.at[32]),
        pltpu.make_async_copy(cotangent, cot, in_sems.at[33]),
    ]
    for source, blocks, first in ((local_qkv, 12, 0), (local_out, 4, 24)):
        for r in range(2):
            for c in range(blocks):
                n = first + r * blocks + c
                part = source.at[r * 512 : (r + 1) * 512, c * 256 : (c + 1) * 256]
                loads.append(pltpu.make_async_copy(part, weights.at[n // 3, n % 3], in_sems.at[n]))
    for load in loads:
        load.start()
    gcore = for_local[2]

    def meanwhile():
        for load in loads:
            load.wait()
        for r in range(2):
            gcore[:, r * 512 : (r + 1) * 512] = sum(
                cross(cot[:, c * 256 : (c + 1) * 256], weights[(24 + r * 4 + c) // 3, (24 + r * 4 + c) % 3], 1, 1)
                for c in range(4)
            )

    sent += output_stage(meanwhile, q, k, v, global_out, context, *for_output)
    local_stage(emb, context, weights, cot, hidden, grad_qkv, grad_out, *for_local)
    for copy in sent:
        copy.wait_send()


def window(byte_rows, emb, w, w_global_out, w_qkv, w_out, cotangent):
    bf, f32 = jnp.bfloat16, jnp.float32
    rows, width = byte_rows.shape
    total, cols = 2 * rows // PATCH * 8, w.shape[2]
    qw, ow = w_qkv.shape[1], w_out.shape[1]

    def sems(*shape):
        return pltpu.SemaphoreType.DMA(shape)

    def units(*lead):
        return pltpu.VMEM((*lead, 48, CHUNK), bf)

    def each(*lead):
        return [pltpu.VMEM((*lead, 16, c), bf) for c in PART_COLS]

    parts = [
        [

            pltpu.VMEM((rows, width), bf),
            pltpu.VMEM((rows, width), bf),
            pltpu.VMEM((width // 128, 2 * rows, 128), f32),
            pltpu.VMEM((16, 2, 4, 48, CHUNK), bf),
            pltpu.VMEM((16, 3, CHUNK, cols), bf),
            pltpu.VMEM((3, total, cols), f32),
            pltpu.SemaphoreType.DMA, pltpu.SemaphoreType.DMA, pltpu.SemaphoreType.DMA,
            sems(2, 8), sems(4, 5), sems(4, 5), sems(4, 4), sems(4, 4), sems(8), sems(8),
        ],
        [

            pltpu.VMEM((2, total, HEAD_DIM), bf),
            pltpu.VMEM((4, 2, total, HEAD_DIM), bf),
            pltpu.VMEM((4, 2, total, HEAD_DIM), bf),
            pltpu.VMEM((2, total, 2 * HEAD_DIM), f32),
            pltpu.VMEM((8 + 2 * total, HEAD_DIM), f32),
            pltpu.VMEM((total, HEAD_DIM), bf),
            pltpu.VMEM((total, 2 * cols), bf),
            pltpu.VMEM((2 * cols, LANES), bf),
            units(4, 4, 2), units(4, 2), units(4, 2, 2), units(4, 2), units(4),
            units(4, 2, 4), units(4, 4), units(4, 4), units(4, 3),
            pltpu.VMEM((48, LANES), f32),
            pltpu.VMEM((24, LANES), f32),
            sems(8), sems(8), sems(8), sems(4, 7), sems(4, 7), sems(4, 4), sems(4, 4),
            pltpu.SemaphoreType.DMA, pltpu.SemaphoreType.DMA,
            sems(3), sems(3), sems(4, 2, 2), sems(4, 2, 2),
            pltpu.SemaphoreType.DMA, pltpu.SemaphoreType.DMA,
            pltpu.SemaphoreType.DMA, pltpu.SemaphoreType.DMA, sems(2), sems(2),
        ],
        [

            pltpu.VMEM((rows, width), f32),
            pltpu.VMEM((rows, qw), f32),
            pltpu.VMEM((rows, width), f32),
            pltpu.VMEM((2, rows, qw // 2), bf),
            pltpu.VMEM((2, width, rows), bf),
            pltpu.VMEM((2, width, rows), bf),
            pltpu.VMEM((2 * rows, width), bf),
            pltpu.VMEM((2 * rows, qw // 2), bf),
            pltpu.VMEM((2 * rows, width), bf),
            pltpu.VMEM((2 * rows, ow // 2), bf),
            *each(4, 4, 4), *each(2, 2, 4), *each(2, 4, 4),
            *each(4, 4), *each(3, 4), *each(4), *each(3),
            pltpu.VMEM((16, (qw + ow) // 2), f32),
            pltpu.VMEM((8, (qw + ow) // 2), f32),
            sems(4), sems(4), sems(3, 6), sems(3, 6), sems(3, 3), sems(3, 3), sems(3, 3), sems(3, 3),
            pltpu.SemaphoreType.DMA, pltpu.SemaphoreType.DMA,
        ],
    ]
    inner = [pltpu.VMEM((total, cols), bf)] * 3 + [
        pltpu.VMEM((rows // PATCH, PATCH, width), f32),
        pltpu.VMEM((rows, width), bf),
        pltpu.VMEM((rows, width), bf),
        sems(34),
    ]
    vmem = pl.BlockSpec(memory_space=pltpu.VMEM)
    return pl.pallas_call(
        functools.partial(window_kernel, [len(part) for part in parts]),
        name="window",
        out_shape=(
            jax.ShapeDtypeStruct((rows, width), bf),
            jax.ShapeDtypeStruct((8, qw), f32),
            jax.ShapeDtypeStruct((8, ow), f32),
        ),
        in_specs=[pl.BlockSpec(memory_space=pl.ANY)] * 7,
        out_specs=(vmem,) * 3,
        scratch_shapes=inner + [shape for part in parts for shape in part],
        compiler_params=pltpu.CompilerParams(collective_id=1, has_side_effects=True, vmem_limit_bytes=67043328),
    )(byte_rows, emb, w, w_global_out, w_qkv, w_out, cotangent)


def per_device(byte_embeds, local_embeds, global_qkv, global_out, local_qkv, local_out, cotangent):
    hidden, grad_qkv, grad_out = window(
        byte_embeds, local_embeds, global_qkv, global_out, local_qkv[0], local_out[0], cotangent
    )
    return (hidden, grad_qkv[None], grad_out[None])


def solution(mesh):
    in_specs = (
        P(("ctx", "tp"), None),
        P(("ctx", "tp"), None),
        P(None, None, "tp"),
        P("tp", None),
        P(),
        P(),
        P(("ctx", "tp"), None),
    )
    out_specs = (P(("ctx", "tp"), None), P(None, ("ctx", "tp"), None), P(None, ("ctx", "tp"), None))
    return jax.shard_map(
        per_device, mesh=mesh, in_specs=in_specs, out_specs=out_specs, check_vma=False
    )
```
